32 devices in a mesh: patch: 8 (over y, x, core), group: 4 (over z).
Axes of the slice: x: 2, y: 2, z: 4, core: 2. Of those that a mesh axis runs over, the one named last changes fastest.
Arguments:
- grid_latent: bfloat16 [16384, 512], P(('patch', 'group')), may hold values from -6 to 6
- mesh_latent: bfloat16 [8192, 512], P(('patch', 'group')), may hold values from -6 to 6
- cotangent: bfloat16 [8192, 512], P(('patch', 'group')), may hold values from -6 to 6
- halo_rows: int32 [8192], P(('patch', 'group')), may hold values from 0 to 511
- encoder_sender: int32 [24576], P(('patch', 'group')), may hold values from 0 to 767
- encoder_target: int32 [24576], P(('patch', 'group')), may hold values from 0 to 255
- encoder_count: int32 [32], P(('patch', 'group')), may hold values from 96 to 768, as said below
- process_sender: int32 [24576], P(('patch', 'group')), may hold values from 0 to 319
- process_target: int32 [24576], P(('patch', 'group')), may hold values from 0 to 255
- process_count: int32 [32], P(('patch', 'group')), may hold values from 96 to 768, as said below
- encoder_source: bfloat16 [512, 512], replicated, may hold values from -0.25 to 0.25
- encoder_dest: bfloat16 [512, 512], replicated, may hold values from -0.25 to 0.25
- encoder_output: bfloat16 [512, 512], replicated, may hold values from -0.25 to 0.25
- encoder_gain: float32 [512], replicated, may hold values from 0.5 to 1.5
- process_source: bfloat16 [512, 512], replicated, may hold values from -0.25 to 0.25
- process_dest: bfloat16 [512, 512], replicated, may hold values from -0.25 to 0.25
- process_output: bfloat16 [512, 512], replicated, may hold values from -0.25 to 0.25
- process_gain: float32 [512], replicated, may hold values from 0.5 to 1.5
Outputs:
- grid_grad: bfloat16 [16384, 512], P(('patch', 'group'))
- mesh_grad: bfloat16 [8192, 512], P(('patch', 'group'))
The draws below stay inside these ranges and needn't reach their ends.
Inputs may be any that keep to these rules, and one draw needn't show every extreme that they name: `halo_rows`: a block's entries are rows of its own grid nodes. `encoder_sender`: rows of the block's extended grid table. `encoder_target`: rows of the block's own mesh nodes. The first encoder_count slots of a block are edges, the rest padding; some block is full in every draw. `process_sender`: rows of the block's sender table: its own mesh nodes, then the coarse nodes of its group. `process_target`: rows of the block's own mesh nodes. The first process_count slots of a block are edges, the rest padding; some block is full in every draw.
All inputs are finite; a program needn't handle non-finite values.
Results may differ from the reference program's by a relative error of at most 0.01.
Values may be sent and summed in bfloat16 or wider, within the bound.
No kernel may reach another device: no remote copies, remote signals or barrier semaphores. Data moves between devices by JAX's collectives and lax.ppermute only.
A program may use at most 64 MiB of HBM per device.

```python
import jax
import jax.numpy as jnp
from jax import lax

D = 512
HIDDEN_SIZE = 512
GRID_DEV = 512
MESH_DEV = 256
HALO = 128
COARSE_DEV = 16
E_CAP = 768
P_CAP = 768
GRID = 16384
MESH = 8192
N_PATCH = 8
N_GROUP = 4
DEVICES = 32


def draw_counts(key, capacity, salt_value):
    folded = jax.random.fold_in(key, salt_value)
    key_spread, key_full = jax.random.split(folded)
    spread = jax.random.randint(key_spread, (DEVICES,), 0, 64)
    floor_count = capacity // 8
    counts = floor_count + (capacity - floor_count) * spread * spread // 4096
    chosen = jax.random.randint(key_full, (), 0, DEVICES)
    return jnp.where(jnp.arange(DEVICES) == chosen, capacity, counts).astype(jnp.int32)


def draw_encoder_count(key, part):
    return draw_counts(key, E_CAP, 11)


def draw_process_count(key, part):
    return draw_counts(key, P_CAP, 23)


def place_ends(array, rng, smallest, high):
    longest = array.shape.index(max(array.shape))
    spots = []
    for shift in (0, 1):
        where = [jax.random.randint(jax.random.fold_in(rng, axis), (), 0, length) for axis, length in enumerate(array.shape)]
        where[longest] = (where[longest] + shift) % array.shape[longest]
        spots.append(tuple(where))
    return array.at[spots[0]].set(smallest).at[spots[1]].set(high)


def levels(key, dims, cuts, smallest, largest):
    def one(dim, parts):
        heights = jax.random.uniform(jax.random.fold_in(jax.random.fold_in(key, 6), dim), (parts,), jnp.float32, smallest / len(cuts), largest / len(cuts))
        return jnp.repeat(jnp.exp(heights), dims[dim] // parts).reshape((-1,) + (1,) * (len(dims) - dim - 1))

    level = one(*cuts[0])
    for cut in cuts[1:]:
        level = level * one(*cut)
    return level


def normal_values(rng, shape, scale, limit, cuts=(), kind=jnp.bfloat16):
    entries = scale * jax.random.normal(rng, shape, jnp.float32)
    if cuts:
        entries = entries * levels(rng, shape, cuts, -0.22, 0.18)
    return jnp.clip(entries, -limit, limit).astype(kind)


def setup_inputs(seed: int = 0) -> dict:
    keys = jax.random.split(jax.random.key(seed), 19)
    grid_latent = normal_values(keys[0], (GRID, D), 1.0, 6.0, ((0, 32),))
    mesh_latent = normal_values(keys[1], (MESH, D), 1.0, 6.0, ((0, 32),))
    cotangent = normal_values(keys[2], (MESH, D), 1.0, 6.0, ((0, 32),))
    halo_rows = place_ends(jax.random.randint(keys[3], (2 * HALO * DEVICES,), 0, GRID_DEV), jax.random.fold_in(keys[3], 1), 0, GRID_DEV - 1).astype(jnp.int32)
    encoder_sender = place_ends(jax.random.randint(keys[4], (E_CAP * DEVICES,), 0, GRID_DEV + 2 * HALO), jax.random.fold_in(keys[4], 1), 0, (GRID_DEV + 2 * HALO) - 1).astype(jnp.int32)
    encoder_target = place_ends(jax.random.randint(keys[5], (E_CAP * DEVICES,), 0, MESH_DEV), jax.random.fold_in(keys[5], 1), 0, MESH_DEV - 1).astype(jnp.int32)
    encoder_count = draw_encoder_count(jax.random.fold_in(keys[18], 71), 0)
    process_sender = place_ends(jax.random.randint(keys[7], (P_CAP * DEVICES,), 0, MESH_DEV + N_GROUP * COARSE_DEV), jax.random.fold_in(keys[7], 1), 0, (MESH_DEV + N_GROUP * COARSE_DEV) - 1).astype(jnp.int32)
    process_target = place_ends(jax.random.randint(keys[8], (P_CAP * DEVICES,), 0, MESH_DEV), jax.random.fold_in(keys[8], 1), 0, MESH_DEV - 1).astype(jnp.int32)
    process_count = draw_process_count(jax.random.fold_in(keys[18], 71), 0)
    encoder_source = normal_values(keys[10], (D, HIDDEN_SIZE), D ** -0.5, 0.25)
    encoder_dest = normal_values(keys[11], (D, HIDDEN_SIZE), D ** -0.5, 0.25)
    encoder_output = normal_values(keys[12], (HIDDEN_SIZE, D), HIDDEN_SIZE ** -0.5, 0.25)
    encoder_gain = jnp.clip(1.0 + 0.1 * jax.random.normal(keys[13], (D,), jnp.float32), 0.5, 1.5)
    process_source = normal_values(keys[14], (D, HIDDEN_SIZE), D ** -0.5, 0.25)
    process_dest = normal_values(keys[15], (D, HIDDEN_SIZE), D ** -0.5, 0.25)
    process_output = normal_values(keys[16], (HIDDEN_SIZE, D), HIDDEN_SIZE ** -0.5, 0.25)
    process_gain = jnp.clip(1.0 + 0.1 * jax.random.normal(keys[17], (D,), jnp.float32), 0.5, 1.5)
    return dict(grid_latent=grid_latent, mesh_latent=mesh_latent, cotangent=cotangent, halo_rows=halo_rows, encoder_sender=encoder_sender, encoder_target=encoder_target, encoder_count=encoder_count, process_sender=process_sender, process_target=process_target, process_count=process_count, encoder_source=encoder_source, encoder_dest=encoder_dest, encoder_output=encoder_output, encoder_gain=encoder_gain, process_source=process_source, process_dest=process_dest, process_output=process_output, process_gain=process_gain)


EPSILON = 1e-05

def silu_slope(values):
    logistic = jax.nn.sigmoid(values)
    return logistic * (1.0 + values * (1.0 - logistic))

def norm_forward(values, norm_gain):
    center = values - lax.optimization_barrier(jnp.mean(values, axis=-1, keepdims=True))
    inverse = lax.rsqrt(lax.optimization_barrier(jnp.mean(center * center, axis=-1, keepdims=True)) + EPSILON)
    normed = center * inverse
    return (normed * norm_gain, normed, inverse)

def norm_backward(grad_out, normed, inverse, norm_gain):
    scaled = grad_out * norm_gain
    return inverse * (scaled - lax.optimization_barrier(jnp.mean(scaled, axis=-1, keepdims=True)) - normed * lax.optimization_barrier(jnp.mean(scaled * normed, axis=-1, keepdims=True)))

def edge_forward(source, dest_proj, sender, target, live_count, out_weight, mesh_count):
    preact = source[sender] + dest_proj[target]
    hidden = jax.nn.silu(preact).astype(jnp.bfloat16)
    message = jnp.dot(hidden, out_weight, preferred_element_type=jnp.float32).astype(jnp.bfloat16)
    live_slots = jnp.arange(sender.shape[0], dtype=jnp.int32) < live_count
    onehot = ((target[None, :] == jnp.arange(mesh_count, dtype=jnp.int32)[:, None]) & live_slots[None, :]).astype(jnp.bfloat16)
    gathered = jnp.dot(onehot, message, preferred_element_type=jnp.float32)
    return (gathered, preact, onehot, live_slots)

def edge_backward(grad_gathered, preact, onehot, live_slots, sender, target, out_weight, table_rows):
    grad_message = jnp.where(live_slots[:, None], grad_gathered[target], 0.0).astype(jnp.bfloat16)
    grad_hidden = jnp.dot(grad_message, out_weight.T, preferred_element_type=jnp.float32)
    grad_preact = (grad_hidden * silu_slope(preact)).astype(jnp.bfloat16)
    chooser = (sender[None, :] == jnp.arange(table_rows, dtype=jnp.int32)[:, None]).astype(jnp.bfloat16)
    grad_source = jnp.dot(chooser, grad_preact, preferred_element_type=jnp.float32)
    grad_dest = jnp.dot(onehot, grad_preact, preferred_element_type=jnp.float32)
    return (grad_source, grad_dest)

def encoder_pass(extended, mesh_rows, sender, target, live_count, source_weight, dest_weight, out_weight, norm_gain):
    source = jnp.dot(extended, source_weight, preferred_element_type=jnp.float32)
    dest_proj = jnp.dot(mesh_rows, dest_weight, preferred_element_type=jnp.float32)
    gathered, preact, onehot, live_slots = edge_forward(source, dest_proj, sender, target, live_count, out_weight, mesh_rows.shape[0])
    shifted, normed, inverse = norm_forward(gathered, norm_gain)
    updated = (mesh_rows.astype(jnp.float32) + shifted).astype(jnp.bfloat16)
    return (updated, (preact, onehot, live_slots, normed, inverse))

def encoder_backward(grad_updated, stored, table_rows, sender, target, source_weight, dest_weight, out_weight, norm_gain):
    preact, onehot, live_slots, normed, inverse = stored
    grad_gathered = norm_backward(grad_updated, normed, inverse, norm_gain)
    grad_source, grad_dest = edge_backward(grad_gathered, preact, onehot, live_slots, sender, target, out_weight, table_rows)
    mesh_grad = grad_updated + jnp.dot(grad_dest.astype(jnp.bfloat16), dest_weight.T, preferred_element_type=jnp.float32)
    grad_extended = jnp.dot(grad_source.astype(jnp.bfloat16), source_weight.T, preferred_element_type=jnp.float32)
    return (mesh_grad, grad_extended)

def process_grads(updated, coarse_proj, sender, target, live_count, cotangent, source_weight, dest_weight, out_weight, norm_gain):
    local_proj = jnp.dot(updated, source_weight, preferred_element_type=jnp.float32)
    source = jnp.concatenate([local_proj, coarse_proj], axis=0)
    dest_proj = jnp.dot(updated, dest_weight, preferred_element_type=jnp.float32)
    gathered, preact, onehot, live_slots = edge_forward(source, dest_proj, sender, target, live_count, out_weight, updated.shape[0])
    unused, normed, inverse = norm_forward(gathered, norm_gain)
    grad_out = cotangent.astype(jnp.float32)
    grad_gathered = norm_backward(grad_out, normed, inverse, norm_gain)
    grad_source, grad_dest = edge_backward(grad_gathered, preact, onehot, live_slots, sender, target, out_weight, source.shape[0])
    mesh_count = updated.shape[0]
    grad_local = grad_out + jnp.dot(grad_source[:mesh_count].astype(jnp.bfloat16), source_weight.T, preferred_element_type=jnp.float32)
    grad_local = grad_local + jnp.dot(grad_dest.astype(jnp.bfloat16), dest_weight.T, preferred_element_type=jnp.float32)
    return (grad_local, grad_source[mesh_count:])

def add_rim(base_rows, rim_index, returned):
    return base_rows.at[rim_index].add(returned)

def reference(grid_latent, mesh_latent, cotangent, halo_rows, encoder_sender, encoder_target, encoder_count, process_sender, process_target, process_count, encoder_source, encoder_dest, encoder_output, encoder_gain, process_source, process_dest, process_output, process_gain):
    blocks = N_PATCH * N_GROUP
    grid_blocks = grid_latent.reshape(blocks, GRID_DEV, D)
    mesh_blocks = mesh_latent.reshape(blocks, MESH_DEV, D)
    cotangents = cotangent.reshape(blocks, MESH_DEV, D)
    rim_index = halo_rows.reshape(blocks, 2 * HALO)
    outgoing = jnp.take_along_axis(grid_blocks, rim_index[:, :, None], axis=1)
    by_patch = outgoing.reshape(N_PATCH, N_GROUP, 2 * HALO, D)
    from_before = jnp.roll(by_patch, 1, axis=0)[:, :, HALO:].reshape(blocks, HALO, D)
    from_after = jnp.roll(by_patch, -1, axis=0)[:, :, :HALO].reshape(blocks, HALO, D)
    extended = jnp.concatenate([grid_blocks, from_before, from_after], axis=1)
    enc_senders = encoder_sender.reshape(blocks, E_CAP)
    enc_targets = encoder_target.reshape(blocks, E_CAP)
    proc_senders = process_sender.reshape(blocks, P_CAP)
    proc_targets = process_target.reshape(blocks, P_CAP)

    def encode_block(pieces):
        table, mesh_rows, sender, target, live_count = pieces
        return encoder_pass(table, mesh_rows, sender, target, live_count, encoder_source, encoder_dest, encoder_output, encoder_gain)[0]
    updated = lax.map(encode_block, (extended, mesh_blocks, enc_senders, enc_targets, encoder_count))
    coarse = updated.reshape(N_PATCH, N_GROUP, MESH_DEV, D)[:, :, :COARSE_DEV].reshape(N_PATCH * N_GROUP * COARSE_DEV, D)
    coarse_proj = jnp.dot(coarse, process_source, preferred_element_type=jnp.float32).reshape(N_PATCH, N_GROUP * COARSE_DEV, HIDDEN_SIZE)

    def process_block(pieces):
        number, mesh_rows, sender, target, live_count, cot_rows = pieces
        return process_grads(mesh_rows, coarse_proj[number // N_GROUP], sender, target, live_count, cot_rows, process_source, process_dest, process_output, process_gain)
    numbers = jnp.arange(blocks, dtype=jnp.int32)
    grad_local, grad_coarse = lax.map(process_block, (numbers, updated, proc_senders, proc_targets, process_count, cotangents))
    summed = lax.optimization_barrier(jnp.sum(grad_coarse.reshape(N_PATCH, N_GROUP, N_GROUP * COARSE_DEV, HIDDEN_SIZE), axis=1))
    summed = summed.reshape(blocks * COARSE_DEV, HIDDEN_SIZE)
    back_weight = process_source.astype(jnp.float32).T
    coarse_grad = jnp.dot(summed, back_weight, precision=lax.Precision.HIGHEST, preferred_element_type=jnp.float32)
    grad_updated = grad_local.at[:, :COARSE_DEV].add(coarse_grad.reshape(blocks, COARSE_DEV, D))

    def encode_back(pieces):
        grad_rows, table, mesh_rows, sender, target, live_count = pieces
        unused, stored = encoder_pass(table, mesh_rows, sender, target, live_count, encoder_source, encoder_dest, encoder_output, encoder_gain)
        return encoder_backward(grad_rows, stored, table.shape[0], sender, target, encoder_source, encoder_dest, encoder_output, encoder_gain)
    mesh_grad, grad_extended = lax.map(encode_back, (grad_updated, extended, mesh_blocks, enc_senders, enc_targets, encoder_count))
    grad_before = grad_extended[:, GRID_DEV:GRID_DEV + HALO].reshape(N_PATCH, N_GROUP, HALO, D)
    grad_after = grad_extended[:, GRID_DEV + HALO:].reshape(N_PATCH, N_GROUP, HALO, D)
    returned = jnp.concatenate([jnp.roll(grad_after, 1, axis=0), jnp.roll(grad_before, -1, axis=0)], axis=2)
    returned = returned.reshape(blocks, 2 * HALO, D)
    grid_grad = jax.vmap(add_rim)(grad_extended[:, :GRID_DEV], rim_index, returned)
    return (grid_grad.reshape(GRID, D).astype(jnp.bfloat16), mesh_grad.reshape(MESH, D).astype(jnp.bfloat16))
```

```python
import functools

import jax
import jax.numpy as jnp
from jax import lax
from jax.experimental import pallas as pl
from jax.experimental.pallas import tpu as pltpu
from jax.sharding import PartitionSpec as P

EPSILON = 1e-05
LANES = 128
F32 = jnp.float32
BF16 = jnp.bfloat16
I32 = jnp.int32


def mm(a, b):
    return jnp.dot(a, b, preferred_element_type=F32)


def mm_t(a, b):
    return lax.dot_general(a, b, (((1,), (1,)), ((), ())), preferred_element_type=F32)


def sigmoid(v):
    return 0.5 + 0.5 * jnp.tanh(0.5 * v)


def ceil_to(n, k):
    return (n + k - 1) // k * k


def to_columns(row):
    n = row.shape[1]
    parts = []
    for i in range(0, n, LANES):
        parts.append(jnp.broadcast_to(row[:, i : i + LANES], (LANES, LANES)).T)
    return jnp.concatenate(parts, axis=0)


def pick(columns, first, width):
    lane = lax.broadcasted_iota(I32, columns.shape, 1)
    parts = []
    for i in range(0, width, LANES):
        parts.append(jnp.where(columns == lane + (first + i), 1.0, 0.0).astype(BF16))
    return parts[0] if len(parts) == 1 else jnp.concatenate(parts, axis=1)


def spread(row, first, height):
    shape = (height, row.shape[1])
    return jnp.where(row == lax.broadcasted_iota(I32, shape, 0) + first, 1.0, 0.0).astype(BF16)


def live_targets(target, count):
    slot = lax.broadcasted_iota(I32, target.shape, 1)
    return jnp.where(slot < count, target, -1)


def normalise(values):
    center = values - jnp.mean(values, axis=-1, keepdims=True)
    inverse = lax.rsqrt(jnp.mean(center * center, axis=-1, keepdims=True) + EPSILON)
    return center * inverse, inverse


def normalise_back(scaled, normed, inverse):
    return inverse * (
        scaled
        - jnp.mean(scaled, axis=-1, keepdims=True)
        - normed * jnp.mean(scaled * normed, axis=-1, keepdims=True)
    )


def halves(rows, even):
    half = rows.shape[1] // 2
    first, second = rows[:, :half], rows[:, half:]
    return jnp.where(even, second, first), jnp.where(even, first, second)


def coarse_slots(sender, mesh_rows, coarse, me, groups):
    offset = sender - mesh_rows
    owner = offset // coarse
    row = offset - owner * coarse
    step = me - owner
    step = jnp.where(step < 0, step + groups, step)
    moved = jnp.where(step == 0, row, mesh_rows + (step - 1) * coarse + row)
    return jnp.where(offset < 0, sender, moved)


def select_kernel(place, halo, grid, near, far):
    even = place[0] == 0
    rows_near, rows_far = halves(halo[...], even)
    table = grid[...]
    near[...] = mm(pick(to_columns(rows_near), 0, table.shape[0]), table).astype(BF16)
    far[...] = mm(pick(to_columns(rows_far), 0, table.shape[0]), table).astype(BF16)


def encode_local_kernel(
    sender, target, count, grid, mesh, w_source, w_dest, preact, send_col, target_col
):
    send_col[...] = to_columns(sender[...])
    target_col[...] = to_columns(live_targets(target[...], count[0]))
    rows = grid.shape[0]
    source = mm(grid[...], w_source[...]).astype(BF16)
    dest = mm(mesh[...], w_dest[...]).astype(BF16)
    preact[...] = mm(pick(send_col[...], 0, rows), source) + mm(
        pick(target_col[...], 0, mesh.shape[0]), dest
    )


def encode_halo_kernel(
    grid_rows,
    place,
    count,
    near,
    far,
    part,
    send_col,
    target,
    mesh16,
    w_source,
    w_out,
    gain,
    hidden,
    slope,
    updated16,
):
    even = place[0] == 0
    rim = near.shape[0]
    source = mm(jnp.concatenate([near[...], far[...]], axis=0), w_source[...]).astype(BF16)
    near_first = jnp.where(even, grid_rows + rim, grid_rows)
    far_first = jnp.where(even, grid_rows, grid_rows + rim)
    chooser = jnp.concatenate(
        [pick(send_col[...], near_first, rim), pick(send_col[...], far_first, rim)], axis=1
    )
    preact = part[...] + mm(chooser, source)
    logistic = sigmoid(preact)
    hid = (preact * logistic).astype(BF16)
    hidden[...] = hid
    slope[...] = (logistic * (1.0 + preact * (1.0 - logistic))).astype(BF16)
    coarse = mesh16.shape[0]
    live = live_targets(target[...], count[0])
    summed = mm(spread(live, 0, coarse), hid).astype(BF16)
    normed, _ = normalise(mm(summed, w_out[...]))
    updated16[...] = (mesh16[...].astype(F32) + normed * gain[...]).astype(BF16)


def process_local_kernel(
    groups,
    coarse,
    place,
    count,
    process_count,
    hidden,
    target,
    mesh,
    sender2,
    target2,
    w_out,
    gain,
    w_source,
    w_dest,
    normed_ref,
    inverse_ref,
    part,
    send_col,
    target_col,
):
    rows = mesh.shape[0]
    moved = coarse_slots(sender2[...], rows, coarse, place[1], groups)
    send_col[...] = to_columns(moved)
    target_col[...] = to_columns(live_targets(target2[...], process_count[0]))
    live = live_targets(target[...], count[0])
    summed = mm(spread(live, 0, rows), hidden[...]).astype(BF16)
    normed, inverse = normalise(mm(summed, w_out[...]))
    normed_ref[...] = normed
    inverse_ref[...] = jnp.broadcast_to(inverse, inverse_ref.shape)
    updated = (mesh[...].astype(F32) + normed * gain[...]).astype(BF16)
    source = mm(updated, w_source[...]).astype(BF16)
    dest = mm(updated, w_dest[...]).astype(BF16)
    part[...] = mm(pick(send_col[...], 0, rows), source) + mm(
        pick(target_col[...], 0, rows), dest
    )


def process_kernel(
    groups,
    coarse,
    place,
    process_count,
    part,
    send_col,
    target_col,
    sender2,
    target2,
    cotangent,
    w_source,
    w_out,
    gain,
    *refs,
):
    peers = groups - 1
    received, grad_ref, returned = refs[:peers], refs[peers], refs[peers + 1 :]
    rows = cotangent.shape[0]
    width = ceil_to(peers * coarse, LANES)
    blocks = [r[...] for r in received]
    if width > peers * coarse:
        blocks.append(jnp.zeros((width - peers * coarse, w_source.shape[0]), BF16))
    source = mm(jnp.concatenate(blocks, axis=0), w_source[...]).astype(BF16)
    preact = part[...] + mm(pick(send_col[...], rows, width), source)
    logistic = sigmoid(preact)
    hid = (preact * logistic).astype(BF16)
    slope = logistic * (1.0 + preact * (1.0 - logistic))
    live = live_targets(target2[...], process_count[0])
    summed = mm(spread(live, 0, rows), hid).astype(BF16)
    normed, inverse = normalise(mm(summed, w_out[...]))
    scaled = cotangent[...].astype(F32) * gain[...]
    back = normalise_back(scaled, normed, inverse).astype(BF16)
    back = mm_t(back, w_out[...]).astype(BF16)
    grad = (mm(pick(target_col[...], 0, rows), back) * slope).astype(BF16)
    grad_ref[...] = grad
    moved = coarse_slots(sender2[...], rows, coarse, place[1], groups)
    sums = mm(spread(moved, rows, peers * coarse), grad)
    for i, out in enumerate(returned):
        out[...] = sums[i * coarse : (i + 1) * coarse].astype(BF16)


def process_back_kernel(
    groups,
    coarse,
    place,
    process_count,
    grad,
    sender2,
    target2,
    cotangent,
    w_source,
    w_dest,
    w_out,
    gain,
    normed,
    inverse,
    target_col,
    grad_local,
    raw,
):
    rows = cotangent.shape[0]
    moved = coarse_slots(sender2[...], rows, coarse, place[1], groups)
    live = live_targets(target2[...], process_count[0])
    table = mm(spread(moved, 0, rows), grad[...]).astype(BF16)
    dest = mm(spread(live, 0, rows), grad[...]).astype(BF16)
    local = cotangent[...].astype(F32) + mm_t(table, w_source[...]) + mm_t(dest, w_dest[...])
    grad_local[...] = local
    back = normalise_back(local * gain[...], normed[...], inverse[:, :1])
    fine = lax.broadcasted_iota(I32, back.shape, 0) >= coarse
    back = jnp.where(fine, back, 0.0).astype(BF16)
    back = mm_t(back, w_out[...]).astype(BF16)
    raw[...] = mm(pick(target_col[...], 0, rows), back)


def encode_back_kernel(
    groups,
    coarse,
    grid_rows,
    place,
    grad_local16,
    normed16,
    inverse16,
    raw,
    slope,
    target_col,
    sender,
    gain,
    w_source2,
    w_out,
    *refs,
):
    peers = groups - 1
    received = refs[:peers]
    grad_ref, near, far, updated16 = refs[peers:]
    total = received[0][...].astype(F32)
    for r in received[1:]:
        total = total + r[...].astype(F32)
    updated = grad_local16[...] + mm_t(total.astype(BF16), w_source2[...])
    updated16[...] = updated
    back = normalise_back(updated * gain[...], normed16[...], inverse16[:, :1]).astype(BF16)
    back = mm_t(back, w_out[...]).astype(BF16)
    back = jnp.concatenate([back, jnp.zeros((LANES - coarse, back.shape[1]), BF16)], axis=0)
    grad = ((raw[...] + mm(pick(target_col[...], 0, LANES), back)) * slope[...].astype(F32)).astype(
        BF16
    )
    grad_ref[...] = grad
    even = place[0] == 0
    rim = near.shape[0]
    near_first = jnp.where(even, grid_rows + rim, grid_rows)
    far_first = jnp.where(even, grid_rows, grid_rows + rim)
    near[...] = mm(spread(sender[...], near_first, rim), grad).astype(BF16)
    far[...] = mm(spread(sender[...], far_first, rim), grad).astype(BF16)


def own_back_kernel(
    count, grad, sender, target, grad_local, updated16, w_source, w_dest, mesh_grad, own
):
    coarse = updated16.shape[0]
    rows = grad_local.shape[0]
    live = live_targets(target[...], count[0])
    dest = mm(spread(live, 0, rows), grad[...]).astype(BF16)
    updated = jnp.concatenate([updated16[...], grad_local[coarse:, :]], axis=0)
    mesh_grad[...] = (updated + mm_t(dest, w_dest[...])).astype(BF16)
    source = mm(spread(sender[...], 0, own.shape[0]), grad[...]).astype(BF16)
    own[...] = mm_t(source, w_source[...])


def finish_kernel(place, halo, own, near, far, w_source, grid_grad):
    even = place[0] == 0
    rows_near, rows_far = halves(halo[...], even)
    peers = jnp.concatenate([near[...], far[...]], axis=0)
    projected = mm_t(peers, w_source[...]).astype(BF16)
    where = jnp.concatenate([rows_near, rows_far], axis=1)
    grid_grad[...] = (own[...] + mm(spread(where, 0, own.shape[0]), projected)).astype(BF16)


SMEM = pl.BlockSpec(memory_space=pltpu.SMEM)
VMEM = pl.BlockSpec(memory_space=pltpu.VMEM)


def call(kernel, name, scalars, arrays, outs, flops=0):
    args = list(scalars) + list(arrays)
    return pl.pallas_call(
        kernel,
        out_shape=[jax.ShapeDtypeStruct(s, d) for s, d in outs],
        in_specs=[SMEM] * len(scalars) + [VMEM] * len(arrays),
        out_specs=[VMEM] * len(outs),
        compiler_params=pltpu.CompilerParams(vmem_limit_bytes=24 << 20),
        cost_estimate=pl.CostEstimate(flops=flops, bytes_accessed=1 << 20, transcendentals=0),
        name=name,
    )(*args)


def pair_swaps(n):
    near = [(i, i ^ 1) for i in range(n)]
    far = [(i, (i + 1) % n if i % 2 else (i - 1) % n) for i in range(n)]
    return near, far


def on_device(
    grid_latent,
    mesh_latent,
    cotangent,
    halo_rows,
    encoder_sender,
    encoder_target,
    encoder_count,
    process_sender,
    process_target,
    process_count,
    encoder_source,
    encoder_dest,
    encoder_output,
    encoder_gain,
    process_source,
    process_dest,
    process_output,
    process_gain,
):
    patches, groups = lax.axis_size("patch"), lax.axis_size("group")
    near_swap, far_swap = pair_swaps(patches)
    grid_rows, width = grid_latent.shape
    mesh_rows = mesh_latent.shape[0]
    hidden_size = encoder_source.shape[1]
    coarse = mesh_rows // 16
    rim = halo_rows.shape[0] // 2
    slots, slots2 = encoder_sender.shape[0], process_sender.shape[0]
    halo = halo_rows[None]
    sender, target = encoder_sender[None], encoder_target[None]
    sender2, target2 = process_sender[None], process_target[None]
    gain, gain2 = encoder_gain[None], process_gain[None]
    place = jnp.stack([lax.axis_index("patch") % 2, lax.axis_index("group")]).astype(I32)
    big = 1 << 30

    near, far = call(
        select_kernel, "select", [place], [halo, grid_latent], [((rim, width), BF16)] * 2
    )
    far = lax.ppermute(far, "patch", far_swap)
    near = lax.ppermute(near, "patch", near_swap)
    part, send_col, target_col = call(
        lambda c, s, t, *r: encode_local_kernel(s, t, c, *r),
        "encode_local",
        [encoder_count],
        [sender, target, grid_latent, mesh_latent, encoder_source, encoder_dest],
        [((slots, hidden_size), F32), ((slots, LANES), I32), ((slots, LANES), I32)],
        big,
    )
    mesh16 = mesh_latent[:coarse]
    hidden, slope, updated16 = call(
        functools.partial(encode_halo_kernel, grid_rows),
        "encode_halo",
        [place, encoder_count],
        [near, far, part, send_col, target, mesh16, encoder_source, encoder_output, gain],
        [((slots, hidden_size), BF16), ((slots, hidden_size), BF16), ((coarse, width), BF16)],
    )
    shifts = [
        lax.ppermute(updated16, "group", [(i, (i + k) % groups) for i in range(groups)])
        for k in range(1, groups)
    ]
    normed, inverse, part2, send_col2, target_col2 = call(
        functools.partial(process_local_kernel, groups, coarse),
        "process_local",
        [place, encoder_count, process_count],
        [
            hidden,
            target,
            mesh_latent,
            sender2,
            target2,
            encoder_output,
            gain,
            process_source,
            process_dest,
        ],
        [
            ((mesh_rows, width), F32),
            ((mesh_rows, LANES), F32),
            ((slots2, hidden_size), F32),
            ((slots2, LANES), I32),
            ((slots2, LANES), I32),
        ],
        big,
    )
    grad2, *pieces = call(
        functools.partial(process_kernel, groups, coarse),
        "process",
        [place, process_count],
        [
            part2,
            send_col2,
            target_col2,
            sender2,
            target2,
            cotangent,
            process_source,
            process_output,
            gain2,
            *shifts,
        ],
        [((slots2, hidden_size), BF16)] + [((coarse, hidden_size), BF16)] * (groups - 1),
    )
    pieces = [
        lax.ppermute(piece, "group", [(i, (i - k) % groups) for i in range(groups)])
        for k, piece in enumerate(pieces, 1)
    ]
    grad_local, raw = call(
        functools.partial(process_back_kernel, groups, coarse),
        "process_back",
        [place, process_count],
        [
            grad2,
            sender2,
            target2,
            cotangent,
            process_source,
            process_dest,
            encoder_output,
            gain,
            normed,
            inverse,
            target_col,
        ],
        [((mesh_rows, width), F32), ((slots, hidden_size), F32)],
        big,
    )
    grad, near, far, grad16 = call(
        functools.partial(encode_back_kernel, groups, coarse, grid_rows),
        "encode_back",
        [place],
        [
            grad_local[:coarse],
            normed[:coarse],
            inverse[:coarse],
            raw,
            slope,
            target_col,
            sender,
            gain,
            process_source,
            encoder_output,
            *pieces,
        ],
        [((slots, hidden_size), BF16)] + [((rim, hidden_size), BF16)] * 2 + [((coarse, width), F32)],
    )
    far = lax.ppermute(far, "patch", far_swap)
    near = lax.ppermute(near, "patch", near_swap)
    mesh_grad, own = call(
        own_back_kernel,
        "own_back",
        [encoder_count],
        [grad, sender, target, grad_local, grad16, encoder_source, encoder_dest],
        [((mesh_rows, width), BF16), ((grid_rows, width), F32)],
        big,
    )
    (grid_grad,) = call(
        finish_kernel,
        "finish",
        [place],
        [halo, own, near, far, encoder_source],
        [((grid_rows, width), BF16)],
    )
    return grid_grad, mesh_grad


def solution(mesh):
    rows, flat, whole = P(("patch", "group"), None), P(("patch", "group")), P()
    return jax.shard_map(
        on_device,
        mesh=mesh,
        in_specs=(rows,) * 3 + (flat,) * 7 + (whole,) * 8,
        out_specs=(rows, rows),
        check_vma=False,
    )
```

```python
import functools

import jax
import jax.numpy as jnp
from jax import lax
from jax.experimental import pallas as pl
from jax.experimental.pallas import tpu as pltpu
from jax.sharding import PartitionSpec as P

EPSILON = 1e-05
LANES = 128
F32 = jnp.float32
BF16 = jnp.bfloat16
I32 = jnp.int32


def mm(a, b):
    return jnp.dot(a, b, preferred_element_type=F32)


def mm_t(a, b):
    return lax.dot_general(a, b, (((1,), (1,)), ((), ())), preferred_element_type=F32)


def sigmoid(v):
    return 0.5 + 0.5 * jnp.tanh(0.5 * v)


def ceil_to(n, k):
    return (n + k - 1) // k * k


def to_columns(row):
    n = row.shape[1]
    parts = []
    for i in range(0, n, LANES):
        parts.append(jnp.broadcast_to(row[:, i : i + LANES], (LANES, LANES)).T)
    return jnp.concatenate(parts, axis=0)


def pick(columns, first, width):
    lane = lax.broadcasted_iota(I32, columns.shape, 1)
    parts = []
    for i in range(0, width, LANES):
        parts.append(jnp.where(columns == lane + (first + i), 1.0, 0.0).astype(BF16))
    return parts[0] if len(parts) == 1 else jnp.concatenate(parts, axis=1)


def spread(row, first, height):
    shape = (height, row.shape[1])
    return jnp.where(row == lax.broadcasted_iota(I32, shape, 0) + first, 1.0, 0.0).astype(BF16)


def live_targets(target, count):
    slot = lax.broadcasted_iota(I32, target.shape, 1)
    return jnp.where(slot < count, target, -1)


def normalise(values):
    center = values - jnp.mean(values, axis=-1, keepdims=True)
    inverse = lax.rsqrt(jnp.mean(center * center, axis=-1, keepdims=True) + EPSILON)
    return center * inverse, inverse


def normalise_back(scaled, normed, inverse):
    return inverse * (
        scaled
        - jnp.mean(scaled, axis=-1, keepdims=True)
        - normed * jnp.mean(scaled * normed, axis=-1, keepdims=True)
    )


def halves(rows, even):
    half = rows.shape[1] // 2
    first, second = rows[:, :half], rows[:, half:]
    return jnp.where(even, second, first), jnp.where(even, first, second)


def coarse_slots(sender, mesh_rows, coarse, me, groups):
    offset = sender - mesh_rows
    owner = offset // coarse
    row = offset - owner * coarse
    step = me - owner
    step = jnp.where(step < 0, step + groups, step)
    moved = jnp.where(step == 0, row, mesh_rows + (step - 1) * coarse + row)
    return jnp.where(offset < 0, sender, moved)


def even_patch():
    return lax.rem(lax.axis_index("patch"), 2) == 0


def as_row(ref):
    return ref[...].reshape(1, ref.shape[0])


def select_kernel(halo_hbm, grid_hbm, near, far, table, halo, sems):
    copies = [
        pltpu.make_async_copy(halo_hbm, halo, sems.at[0]),
        pltpu.make_async_copy(grid_hbm, table, sems.at[1]),
    ]
    for copy in copies:
        copy.start()
    copies[0].wait()
    rows_near, rows_far = halves(as_row(halo), even_patch())
    pick_near = pick(to_columns(rows_near), 0, table.shape[0])
    pick_far = pick(to_columns(rows_far), 0, table.shape[0])
    copies[1].wait()
    near[...] = mm(pick_near, table[...]).astype(BF16)
    far[...] = mm(pick_far, table[...]).astype(BF16)


def encode_local_kernel(
    groups,
    coarse,
    counts,
    sender,
    target,
    sender2,
    target2,
    grid,
    mesh,
    w_source,
    w_dest,
    part,
    send_row,
    send_col,
    live_row,
    live_col,
    send_row2,
    send_col2,
    live_row2,
    live_col2,
):
    rows = mesh.shape[0]
    send_row[...] = as_row(sender)
    send_col[...] = to_columns(as_row(sender))
    send_row2[...] = coarse_slots(as_row(sender2), rows, coarse, lax.axis_index("group"), groups)
    send_col2[...] = to_columns(send_row2[...])
    source = mm(grid[...], w_source[...]).astype(BF16)
    dest = mm(mesh[...], w_dest[...]).astype(BF16)
    live_row[...] = live_targets(as_row(target), counts[0])
    live_col[...] = to_columns(live_row[...])
    live_row2[...] = live_targets(as_row(target2), counts[1])
    live_col2[...] = to_columns(live_row2[...])
    part[...] = mm(pick(send_col[...], 0, grid.shape[0]), source) + mm(
        pick(live_col[...], 0, rows), dest
    )


def rim_starts(grid_rows, rim):
    even = even_patch()
    return (
        jnp.where(even, grid_rows + rim, grid_rows),
        jnp.where(even, grid_rows, grid_rows + rim),
    )


def encode_halo_kernel(
    grid_rows,
    coarse,
    near,
    far,
    part,
    send_col,
    live_row,
    mesh,
    w_source,
    w_out,
    gain,
    hidden,
    slope,
    updated16,
):
    rim = near.shape[0]
    source = mm(jnp.concatenate([near[...], far[...]], axis=0), w_source[...]).astype(BF16)
    near_first, far_first = rim_starts(grid_rows, rim)
    chooser = jnp.concatenate(
        [pick(send_col[...], near_first, rim), pick(send_col[...], far_first, rim)], axis=1
    )
    preact = part[...] + mm(chooser, source)
    logistic = sigmoid(preact)
    hid = (preact * logistic).astype(BF16)
    hidden[...] = hid
    slope[...] = (logistic * (1.0 + preact * (1.0 - logistic))).astype(BF16)
    summed = mm(spread(live_row[...], 0, coarse), hid).astype(BF16)
    normed, _ = normalise(mm(summed, w_out[...]))
    updated16[...] = (mesh[:coarse, :].astype(F32) + normed * as_row(gain)).astype(BF16)


def process_local_kernel(
    hidden,
    live_row,
    mesh,
    send_col2,
    live_col2,
    w_out,
    gain,
    w_source,
    w_dest,
    normed_ref,
    inverse_ref,
    part,
):
    rows = mesh.shape[0]
    summed = mm(spread(live_row[...], 0, rows), hidden[...]).astype(BF16)
    normed, inverse = normalise(mm(summed, w_out[...]))
    normed_ref[...] = normed
    inverse_ref[...] = jnp.broadcast_to(inverse, inverse_ref.shape)
    updated = (mesh[...].astype(F32) + normed * as_row(gain)).astype(BF16)
    source = mm(updated, w_source[...]).astype(BF16)
    dest = mm(updated, w_dest[...]).astype(BF16)
    part[...] = mm(pick(send_col2[...], 0, rows), source) + mm(pick(live_col2[...], 0, rows), dest)


def process_kernel(
    groups,
    coarse,
    part,
    send_row2,
    send_col2,
    live_row2,
    live_col2,
    cotangent,
    w_source,
    w_out,
    gain,
    *refs,
):
    peers = groups - 1
    received, grad_ref, returned = refs[:peers], refs[peers], refs[peers + 1 :]
    rows = cotangent.shape[0]
    width = ceil_to(peers * coarse, LANES)
    blocks = [r[...] for r in received]
    if width > peers * coarse:
        blocks.append(jnp.zeros((width - peers * coarse, w_source.shape[0]), BF16))
    source = mm(jnp.concatenate(blocks, axis=0), w_source[...]).astype(BF16)
    preact = part[...] + mm(pick(send_col2[...], rows, width), source)
    logistic = sigmoid(preact)
    hid = (preact * logistic).astype(BF16)
    slope = logistic * (1.0 + preact * (1.0 - logistic))
    summed = mm(spread(live_row2[...], 0, rows), hid).astype(BF16)
    normed, inverse = normalise(mm(summed, w_out[...]))
    scaled = cotangent[...].astype(F32) * as_row(gain)
    back = normalise_back(scaled, normed, inverse).astype(BF16)
    back = mm_t(back, w_out[...]).astype(BF16)
    grad = (mm(pick(live_col2[...], 0, rows), back) * slope).astype(BF16)
    grad_ref[...] = grad
    sums = mm(spread(send_row2[...], rows, peers * coarse), grad)
    for i, out in enumerate(returned):
        out[...] = sums[i * coarse : (i + 1) * coarse].astype(BF16)


def process_back_kernel(
    coarse,
    grad,
    send_row2,
    live_row2,
    cotangent,
    w_source,
    w_dest,
    w_out,
    gain,
    normed,
    inverse,
    live_col,
    grad_local,
    raw,
):
    rows = cotangent.shape[0]
    table = mm(spread(send_row2[...], 0, rows), grad[...]).astype(BF16)
    dest = mm(spread(live_row2[...], 0, rows), grad[...]).astype(BF16)
    local = cotangent[...].astype(F32) + mm_t(table, w_source[...]) + mm_t(dest, w_dest[...])
    grad_local[...] = local
    back = normalise_back(local * as_row(gain), normed[...], inverse[:, :1])
    fine = lax.broadcasted_iota(I32, back.shape, 0) >= coarse
    back = jnp.where(fine, back, 0.0).astype(BF16)
    back = mm_t(back, w_out[...]).astype(BF16)
    raw[...] = mm(pick(live_col[...], 0, rows), back)


def encode_back_kernel(
    groups,
    coarse,
    grid_rows,
    grad_local,
    normed,
    inverse,
    raw,
    slope,
    live_col,
    send_row,
    gain,
    w_source2,
    w_out,
    *refs,
):
    peers = groups - 1
    received = refs[:peers]
    grad_ref, near, far, updated16 = refs[peers:]
    total = received[0][...].astype(F32)
    for r in received[1:]:
        total = total + r[...].astype(F32)
    updated = grad_local[:coarse, :] + mm_t(total.astype(BF16), w_source2[...])
    updated16[...] = updated
    back = normalise_back(updated * as_row(gain), normed[:coarse, :], inverse[:coarse, :1])
    back = mm_t(back.astype(BF16), w_out[...]).astype(BF16)
    back = jnp.concatenate([back, jnp.zeros((LANES - coarse, back.shape[1]), BF16)], axis=0)
    more = mm(pick(live_col[...], 0, LANES), back)
    grad = ((raw[...] + more) * slope[...].astype(F32)).astype(BF16)
    grad_ref[...] = grad
    rim = near.shape[0]
    near_first, far_first = rim_starts(grid_rows, rim)
    near[...] = mm(spread(send_row[...], near_first, rim), grad).astype(BF16)
    far[...] = mm(spread(send_row[...], far_first, rim), grad).astype(BF16)


def own_back_kernel(
    grad, send_row, live_row, grad_local, updated16, w_source, w_dest, mesh_grad, own
):
    coarse = updated16.shape[0]
    rows = grad_local.shape[0]
    dest = mm(spread(live_row[...], 0, rows), grad[...]).astype(BF16)
    updated = jnp.concatenate([updated16[...], grad_local[coarse:, :]], axis=0)
    mesh_grad[...] = (updated + mm_t(dest, w_dest[...])).astype(BF16)
    source = mm(spread(send_row[...], 0, own.shape[0]), grad[...]).astype(BF16)
    own[...] = mm_t(source, w_source[...])


def finish_kernel(halo, own, near, far, w_source, grid_grad):
    rows_near, rows_far = halves(as_row(halo), even_patch())
    peers = jnp.concatenate([near[...], far[...]], axis=0)
    projected = mm_t(peers, w_source[...]).astype(BF16)
    where = jnp.concatenate([rows_near, rows_far], axis=1)
    grid_grad[...] = (own[...] + mm(spread(where, 0, own.shape[0]), projected)).astype(BF16)


SMEM = pl.BlockSpec(memory_space=pltpu.SMEM)
HBM = pl.BlockSpec(memory_space=pltpu.HBM)
VMEM = pl.BlockSpec(memory_space=pltpu.VMEM)
MICROSECOND = 1 << 30


def call(kernel, name, arrays, outs, cost, raw=0, scalars=0, scratch=()):
    return pl.pallas_call(
        kernel,
        out_shape=[jax.ShapeDtypeStruct(s, d) for s, d in outs],
        in_specs=[HBM] * raw + [SMEM] * scalars + [VMEM] * (len(arrays) - raw - scalars),
        out_specs=[VMEM] * len(outs),
        scratch_shapes=list(scratch),
        compiler_params=pltpu.CompilerParams(vmem_limit_bytes=24 << 20),
        cost_estimate=pl.CostEstimate(
            flops=int(cost * MICROSECOND), bytes_accessed=1 << 20, transcendentals=0
        ),
        name=name,
    )(*(pltpu.with_memory_space_constraint(x, pltpu.HBM) for x in arrays[:raw]), *arrays[raw:])


def pair_swaps(n):
    near = [(i, i ^ 1) for i in range(n)]
    far = [(i, (i + 1) % n if i % 2 else (i - 1) % n) for i in range(n)]
    return near, far


def on_device(
    grid_latent,
    mesh_latent,
    cotangent,
    halo_rows,
    encoder_sender,
    encoder_target,
    encoder_count,
    process_sender,
    process_target,
    process_count,
    encoder_source,
    encoder_dest,
    encoder_output,
    encoder_gain,
    process_source,
    process_dest,
    process_output,
    process_gain,
):
    patches, groups = lax.axis_size("patch"), lax.axis_size("group")
    near_swap, far_swap = pair_swaps(patches)
    grid_rows, width = grid_latent.shape
    mesh_rows = mesh_latent.shape[0]
    hidden_size = encoder_source.shape[1]
    coarse = mesh_rows // 16
    rim = halo_rows.shape[0] // 2
    slots, slots2 = encoder_sender.shape[0], process_sender.shape[0]

    near, far, grid = call(
        select_kernel,
        "select",
        [halo_rows, grid_latent],
        [((rim, width), BF16)] * 2 + [((grid_rows, width), BF16)],
        4,
        raw=2,
        scratch=[pltpu.VMEM(halo_rows.shape, I32), pltpu.SemaphoreType.DMA((2,))],
    )
    far = lax.ppermute(far, "patch", far_swap)
    near = lax.ppermute(near, "patch", near_swap)
    part, send_row, send_col, live_row, live_col, send_row2, send_col2, live_row2, live_col2 = call(
        functools.partial(encode_local_kernel, groups, coarse),
        "encode_local",
        [
            jnp.concatenate([encoder_count, process_count]),
            encoder_sender,
            encoder_target,
            process_sender,
            process_target,
            grid,
            mesh_latent,
            encoder_source,
            encoder_dest,
        ],
        [((slots, hidden_size), F32)]
        + [((1, slots), I32), ((slots, LANES), I32)] * 2
        + [((1, slots2), I32), ((slots2, LANES), I32)] * 2,
        2,
        scalars=1,
    )
    hidden, slope, updated16 = call(
        functools.partial(encode_halo_kernel, grid_rows, coarse),
        "encode_halo",
        [
            near,
            far,
            part,
            send_col,
            live_row,
            mesh_latent,
            encoder_source,
            encoder_output,
            encoder_gain,
        ],
        [((slots, hidden_size), BF16), ((slots, hidden_size), BF16), ((coarse, width), BF16)],
        2,
    )
    shifts = [
        lax.ppermute(updated16, "group", [(i, (i + k) % groups) for i in range(groups)])
        for k in range(1, groups)
    ]
    normed, inverse, part2 = call(
        process_local_kernel,
        "process_local",
        [
            hidden,
            live_row,
            mesh_latent,
            send_col2,
            live_col2,
            encoder_output,
            encoder_gain,
            process_source,
            process_dest,
        ],
        [
            ((mesh_rows, width), F32),
            ((mesh_rows, LANES), F32),
            ((slots2, hidden_size), F32),
        ],
        2,
    )
    grad2, *pieces = call(
        functools.partial(process_kernel, groups, coarse),
        "process",
        [
            part2,
            send_row2,
            send_col2,
            live_row2,
            live_col2,
            cotangent,
            process_source,
            process_output,
            process_gain,
            *shifts,
        ],
        [((slots2, hidden_size), BF16)] + [((coarse, hidden_size), BF16)] * (groups - 1),
        2,
    )
    pieces = [
        lax.ppermute(piece, "group", [(i, (i - k) % groups) for i in range(groups)])
        for k, piece in enumerate(pieces, 1)
    ]
    grad_local, raw = call(
        functools.partial(process_back_kernel, coarse),
        "process_back",
        [
            grad2,
            send_row2,
            live_row2,
            cotangent,
            process_source,
            process_dest,
            encoder_output,
            encoder_gain,
            normed,
            inverse,
            live_col,
        ],
        [((mesh_rows, width), F32), ((slots, hidden_size), F32)],
        2,
    )
    grad, near, far, grad16 = call(
        functools.partial(encode_back_kernel, groups, coarse, grid_rows),
        "encode_back",
        [
            grad_local,
            normed,
            inverse,
            raw,
            slope,
            live_col,
            send_row,
            encoder_gain,
            process_source,
            encoder_output,
            *pieces,
        ],
        [((slots, hidden_size), BF16)]
        + [((rim, hidden_size), BF16)] * 2
        + [((coarse, width), F32)],
        2,
    )
    far = lax.ppermute(far, "patch", far_swap)
    near = lax.ppermute(near, "patch", near_swap)
    mesh_grad, own = call(
        own_back_kernel,
        "own_back",
        [grad, send_row, live_row, grad_local, grad16, encoder_source, encoder_dest],
        [((mesh_rows, width), BF16), ((grid_rows, width), F32)],
        2,
    )
    (grid_grad,) = call(
        finish_kernel,
        "finish",
        [halo_rows, own, near, far, encoder_source],
        [((grid_rows, width), BF16)],
        2,
    )
    return grid_grad, mesh_grad


def solution(mesh):
    rows, flat, whole = P(("patch", "group"), None), P(("patch", "group")), P()
    return jax.shard_map(
        on_device,
        mesh=mesh,
        in_specs=(rows,) * 3 + (flat,) * 7 + (whole,) * 8,
        out_specs=(rows, rows),
        check_vma=False,
    )
```

```python
import functools

import jax
import jax.numpy as jnp
from jax import lax
from jax.experimental import pallas as pl
from jax.experimental.pallas import tpu as pltpu
from jax.sharding import PartitionSpec as P


EPSILON = 1e-05
LANES = 128
F32 = jnp.float32
BF16 = jnp.bfloat16
I32 = jnp.int32


def mm(a, b):
    return jnp.dot(a, b, preferred_element_type=F32)


def mm_t(a, b):
    return lax.dot_general(a, b, (((1,), (1,)), ((), ())), preferred_element_type=F32)


def half_silu(u):
    t = jnp.tanh(u)
    a = 1.0 + t
    value = u * a
    return value, a + value * (1.0 - t)


def ceil_to(n, k):
    return (n + k - 1) // k * k


def to_columns(row):
    n = row.shape[1]
    parts = []
    for i in range(0, n, LANES):
        parts.append(jnp.broadcast_to(row[:, i : i + LANES], (LANES, LANES)).T)
    return jnp.concatenate(parts, axis=0)


def pick(columns, first, width):
    lane = lax.broadcasted_iota(I32, columns.shape, 1)
    parts = []
    for i in range(0, width, LANES):
        parts.append(jnp.where(columns == lane + (first + i), 1.0, 0.0).astype(BF16))
    return parts[0] if len(parts) == 1 else jnp.concatenate(parts, axis=1)


def spread(row, first, height):
    shape = (height, row.shape[1])
    return jnp.where(row == lax.broadcasted_iota(I32, shape, 0) + first, 1.0, 0.0).astype(BF16)


def only_live(rows, count):
    slot = lax.broadcasted_iota(I32, rows.shape, 1)
    return jnp.where(slot < count, rows, -1)


def normalise(values):
    center = values - jnp.mean(values, axis=-1, keepdims=True)
    inverse = lax.rsqrt(jnp.mean(center * center, axis=-1, keepdims=True) + EPSILON)
    return center * inverse, inverse


def centred(values):
    return values - jnp.mean(values, axis=-1, keepdims=True)


def normalise_back(centre, normed, inverse):
    return inverse * (centre - normed * jnp.mean(centre * normed, axis=-1, keepdims=True))


def halves(rows, even):
    half = rows.shape[1] // 2
    first, second = rows[:, :half], rows[:, half:]
    return jnp.where(even, second, first), jnp.where(even, first, second)


def coarse_slots(sender, mesh_rows, coarse, me):
    offset = sender - mesh_rows
    owner = offset // coarse
    row = offset - owner * coarse
    mask = owner ^ me
    moved = jnp.where(mask == 0, row, mesh_rows + (mask - 1) * coarse + row)
    return jnp.where(offset < 0, sender, moved)


def even_patch():
    return lax.rem(lax.axis_index("patch"), 2) == 0


def as_row(ref):
    return ref[...].reshape(1, ref.shape[0])


def select_kernel(halo_hbm, grid_hbm, near, far, table, halo, sems):
    copies = [
        pltpu.make_async_copy(halo_hbm, halo, sems.at[0]),
        pltpu.make_async_copy(grid_hbm, table, sems.at[1]),
    ]
    for copy in copies:
        copy.start()
    copies[0].wait()
    rows_near, rows_far = halves(as_row(halo), even_patch())
    pick_near = pick(to_columns(rows_near), 0, table.shape[0])
    pick_far = pick(to_columns(rows_far), 0, table.shape[0])
    copies[1].wait()
    near[...] = mm(pick_near, table[...]).astype(BF16)
    far[...] = mm(pick_far, table[...]).astype(BF16)


def rim_starts(grid_rows, rim):
    even = even_patch()
    return (
        jnp.where(even, grid_rows + rim, grid_rows),
        jnp.where(even, grid_rows, grid_rows + rim),
    )


def encode_local_kernel(
    coarse,
    counts,
    sender,
    target,
    sender2,
    target2,
    grid,
    mesh,
    w_source,
    w_dest,
    part,
    live_send,
    live_goal,
    live_send2,
    live_goal2,
    send_col2,
    goal_col2,
    pick_rim,
    pick_goal,
):
    rows, grid_rows = mesh.shape[0], grid.shape[0]
    rim = pick_rim.shape[1] // 2
    source = (0.5 * mm(grid[...], w_source[...])).astype(BF16)
    dest = (0.5 * mm(mesh[...], w_dest[...])).astype(BF16)
    send_col = to_columns(as_row(sender))
    near_first, far_first = rim_starts(grid_rows, rim)
    pick_rim[:, :rim] = pick(send_col, near_first, rim)
    pick_rim[:, rim:] = pick(send_col, far_first, rim)
    pick_goal[...] = pick(to_columns(as_row(target)), 0, rows)
    moved = coarse_slots(as_row(sender2), rows, coarse, lax.axis_index("group"))
    send_col2[...] = to_columns(moved)
    goal_col2[...] = to_columns(as_row(target2))
    part[...] = mm(pick(send_col, 0, grid_rows), source) + mm(pick_goal[...], dest)
    live_send[...] = only_live(as_row(sender), counts[0])
    live_goal[...] = only_live(as_row(target), counts[0])
    live_send2[...] = only_live(moved, counts[1])
    live_goal2[...] = only_live(as_row(target2), counts[1])


def pieces_of(n, size):
    return [slice(i, min(i + size, n)) for i in range(0, n, size)]


def encode_halo_kernel(
    coarse,
    near,
    far,
    part,
    pick_rim,
    live_goal,
    mesh,
    w_source,
    w_out,
    gain,
    hidden,
    half,
    updated16,
):
    halo = jnp.concatenate([near[...], far[...]], axis=0)
    source = (0.5 * mm(halo, w_source[...])).astype(BF16)
    for c in pieces_of(part.shape[0], 256):
        u = part[c, :] + mm(pick_rim[c, :], source)
        half[c, :] = u
        hidden[c, :] = (u + u * jnp.tanh(u)).astype(BF16)
    summed = mm(spread(live_goal[...], 0, coarse), hidden[...]).astype(BF16)
    normed, _ = normalise(mm(summed, w_out[...]))
    updated16[...] = (mesh[:coarse, :].astype(F32) + normed * as_row(gain)).astype(BF16)


def process_local_kernel(
    hidden,
    live_goal,
    mesh,
    send_col2,
    goal_col2,
    live_send2,
    live_goal2,
    cotangent,
    w_out,
    gain,
    gain2,
    w_source,
    w_dest,
    normed_ref,
    inverse_ref,
    part,
    pick_goal2,
    pick_coarse,
    sum_goal2,
    sum_coarse,
    centre2,
):
    rows = mesh.shape[0]
    summed = mm(spread(live_goal[...], 0, rows), hidden[...]).astype(BF16)
    normed, inverse = normalise(mm(summed, w_out[...]))
    normed_ref[...] = normed
    inverse_ref[...] = jnp.broadcast_to(inverse, inverse_ref.shape)
    updated = (mesh[...].astype(F32) + normed * as_row(gain)).astype(BF16)
    source = (0.5 * mm(updated, w_source[...])).astype(BF16)
    dest = (0.5 * mm(updated, w_dest[...])).astype(BF16)
    pick_goal2[...] = pick(goal_col2[...], 0, rows)
    pick_coarse[...] = pick(send_col2[...], rows, pick_coarse.shape[1])
    sum_goal2[...] = spread(live_goal2[...], 0, rows)
    sum_coarse[...] = spread(live_send2[...], rows, sum_coarse.shape[0])
    centre2[...] = centred(cotangent[...].astype(F32) * as_row(gain2))
    part[...] = mm(pick(send_col2[...], 0, rows), source) + mm(pick_goal2[...], dest)


def process_kernel(
    coarse,
    part,
    pick_goal2,
    pick_coarse,
    sum_goal2,
    sum_coarse,
    centre2,
    w_source,
    w_out,
    *refs,
):
    peers = sum_coarse.shape[0] // coarse
    received, grad, returned = refs[:peers], refs[peers], refs[peers + 1 : -2]
    hidden, slope = refs[-2:]
    rows = jnp.concatenate([r[...] for r in received], axis=0)
    source = (0.5 * mm(rows, w_source[...])).astype(BF16)
    spare = pick_coarse.shape[1] - source.shape[0]
    if spare:
        source = jnp.concatenate([source, jnp.zeros((spare, source.shape[1]), BF16)], axis=0)
    for c in pieces_of(part.shape[0], 256):
        value, double = half_silu(part[c, :] + mm(pick_coarse[c, :], source))
        hidden[c, :] = value.astype(BF16)
        slope[c, :] = double
    summed = mm(sum_goal2[...], hidden[...]).astype(BF16)
    normed, inverse = normalise(mm(summed, w_out[...]))
    back = normalise_back(centre2[...], normed, inverse).astype(BF16)
    back = (0.5 * mm_t(back, w_out[...])).astype(BF16)
    for c in pieces_of(part.shape[0], 256):
        grad[c, :] = (mm(pick_goal2[c, :], back) * slope[c, :]).astype(BF16)
    sums = mm(sum_coarse[...], grad[...])
    for i, out in enumerate(returned):
        out[...] = sums[i * coarse : (i + 1) * coarse].astype(BF16)


def process_back_kernel(
    grid_rows,
    half,
    grad,
    live_send,
    live_send2,
    sum_goal2,
    cotangent,
    w_source,
    w_dest,
    w_out,
    gain,
    normed,
    inverse,
    grad_local,
    back_ref,
    slope,
    sum_rim,
):
    rows = cotangent.shape[0]
    rim = sum_rim.shape[0] // 2
    near_first, far_first = rim_starts(grid_rows, rim)
    sum_rim[:rim, :] = spread(live_send[...], near_first, rim)
    sum_rim[rim:, :] = spread(live_send[...], far_first, rim)
    table = mm(spread(live_send2[...], 0, rows), grad[...]).astype(BF16)
    dest = mm(sum_goal2[...], grad[...]).astype(BF16)
    local = cotangent[...].astype(F32) + mm_t(table, w_source[...]) + mm_t(dest, w_dest[...])
    grad_local[...] = local
    back = normalise_back(centred(local * as_row(gain)), normed[...], inverse[:, :1])
    back_ref[...] = (0.5 * mm_t(back.astype(BF16), w_out[...])).astype(BF16)
    for c in pieces_of(half.shape[0], 128):
        slope[c, :] = half_silu(half[c, :])[1].astype(BF16)


def encode_back_kernel(
    grad_local, back_local, normed, inverse, slope, pick_goal, sum_rim, gain, w_source2, w_out, *refs
):
    received, (grad, near, far, updated16) = refs[:-4], refs[-4:]
    coarse = updated16.shape[0]
    rim = near.shape[0]
    total = received[0][...].astype(F32)
    for r in received[1:]:
        total = total + r[...].astype(F32)
    updated = grad_local[:coarse, :] + mm_t(total.astype(BF16), w_source2[...])
    updated16[...] = updated
    back = normalise_back(
        centred(updated * as_row(gain)), normed[:coarse, :], inverse[:coarse, :1]
    )
    back = (0.5 * mm_t(back.astype(BF16), w_out[...])).astype(BF16)
    back = jnp.concatenate([back, back_local[coarse:, :]], axis=0)
    for c in pieces_of(slope.shape[0], 256):
        grad[c, :] = (mm(pick_goal[c, :], back) * slope[c, :].astype(F32)).astype(BF16)
    near[...] = mm(sum_rim[:rim, :], grad[...]).astype(BF16)
    far[...] = mm(sum_rim[rim:, :], grad[...]).astype(BF16)


def own_back_kernel(
    grad, live_send, live_goal, grad_local, updated16, w_source, w_dest, mesh_grad, own
):
    coarse = updated16.shape[0]
    rows = grad_local.shape[0]
    dest = mm(spread(live_goal[...], 0, rows), grad[...]).astype(BF16)
    updated = jnp.concatenate([updated16[...], grad_local[coarse:, :]], axis=0)
    mesh_grad[...] = (updated + mm_t(dest, w_dest[...])).astype(BF16)
    source = mm(spread(live_send[...], 0, own.shape[0]), grad[...]).astype(BF16)
    own[...] = mm_t(source, w_source[...])


def finish_kernel(halo, own, near, far, w_source, out_hbm, out, sems):
    rows_near, rows_far = halves(as_row(halo), even_patch())
    peers = jnp.concatenate([near[...], far[...]], axis=0)
    projected = mm_t(peers, w_source[...]).astype(BF16)
    where = jnp.concatenate([rows_near, rows_far], axis=1)
    copies = []
    for i, c in enumerate(pieces_of(own.shape[0], own.shape[0] // 4)):
        chosen = spread(where, c.start, c.stop - c.start)
        out[c, :] = (own[c, :] + mm(chosen, projected)).astype(BF16)
        copies.append(pltpu.make_async_copy(out.at[c], out_hbm.at[c], sems.at[i]))
        copies[-1].start()
    for copy in copies:
        copy.wait()


SMEM = pl.BlockSpec(memory_space=pltpu.SMEM)
HBM = pl.BlockSpec(memory_space=pltpu.HBM)
VMEM = pl.BlockSpec(memory_space=pltpu.VMEM)
MICROSECOND = 1 << 30


def call(kernel, arrays, outs, cost, raw=0, scalars=0, scratch=(), out_space=None):
    return pl.pallas_call(
        kernel,
        out_shape=[jax.ShapeDtypeStruct(s, d) for s, d in outs],
        in_specs=[HBM] * raw + [SMEM] * scalars + [VMEM] * (len(arrays) - raw - scalars),
        out_specs=[out_space or VMEM] * len(outs),
        scratch_shapes=list(scratch),
        compiler_params=pltpu.CompilerParams(vmem_limit_bytes=24 << 20),
        cost_estimate=pl.CostEstimate(
            flops=int(cost * MICROSECOND), bytes_accessed=1 << 20, transcendentals=0
        ),
    )(*(pltpu.with_memory_space_constraint(x, pltpu.HBM) for x in arrays[:raw]), *arrays[raw:])


def swap_halo(near, far, n):
    far_pairs = [(i, (i + 1) % n if i % 2 else (i - 1) % n) for i in range(n)]
    far = lax.ppermute(far, "patch", far_pairs)
    near = lax.ppermute(near, "patch", [(i, i ^ 1) for i in range(n)])
    return near, far


def swap_coarse(pieces, n):
    out = []
    for k, piece in enumerate(pieces, 1):
        out.append(lax.ppermute(piece, "group", [(i, i ^ k) for i in range(n)]))
    return out


def on_device(
    grid_latent,
    mesh_latent,
    cotangent,
    halo_rows,
    encoder_sender,
    encoder_target,
    encoder_count,
    process_sender,
    process_target,
    process_count,
    encoder_source,
    encoder_dest,
    encoder_output,
    encoder_gain,
    process_source,
    process_dest,
    process_output,
    process_gain,
):
    patches, groups = lax.axis_size("patch"), lax.axis_size("group")
    grid_rows, width = grid_latent.shape
    mesh_rows = mesh_latent.shape[0]
    hidden_size = encoder_source.shape[1]
    coarse = mesh_rows // 16
    rim = halo_rows.shape[0] // 2
    slots, slots2 = encoder_sender.shape[0], process_sender.shape[0]

    row_form, row_form2 = ((1, slots), I32), ((1, slots2), I32)
    column_form2 = ((slots2, LANES), I32)
    remote = coarse * (groups - 1)
    near, far, grid = call(
        select_kernel,
        [halo_rows, grid_latent],
        [((rim, width), BF16)] * 2 + [((grid_rows, width), BF16)],
        4,
        raw=2,
        scratch=[pltpu.VMEM(halo_rows.shape, I32), pltpu.SemaphoreType.DMA((2,))],
    )
    near, far = swap_halo(near, far, patches)
    (
        part,
        live_send,
        live_goal,
        live_send2,
        live_goal2,
        send_col2,
        goal_col2,
        pick_rim,
        pick_goal,
    ) = call(
        functools.partial(encode_local_kernel, coarse),
        [
            jnp.concatenate([encoder_count, process_count]),
            encoder_sender,
            encoder_target,
            process_sender,
            process_target,
            grid,
            mesh_latent,
            encoder_source,
            encoder_dest,
        ],
        [((slots, hidden_size), F32), row_form, row_form, row_form2, row_form2]
        + [column_form2, column_form2]
        + [((slots, 2 * rim), BF16), ((slots, mesh_rows), BF16)],
        2,
        scalars=1,
    )
    hidden, half, updated16 = call(
        functools.partial(encode_halo_kernel, coarse),
        [
            near,
            far,
            part,
            pick_rim,
            live_goal,
            mesh_latent,
            encoder_source,
            encoder_output,
            encoder_gain,
        ],
        [((slots, hidden_size), BF16), ((slots, hidden_size), F32), ((coarse, width), BF16)],
        2,
    )
    shifts = swap_coarse([updated16] * (groups - 1), groups)
    normed, inverse, part2, pick_goal2, pick_coarse, sum_goal2, sum_coarse, centre2 = call(
        process_local_kernel,
        [
            hidden,
            live_goal,
            mesh_latent,
            send_col2,
            goal_col2,
            live_send2,
            live_goal2,
            cotangent,
            encoder_output,
            encoder_gain,
            process_gain,
            process_source,
            process_dest,
        ],
        [
            ((mesh_rows, width), F32),
            ((mesh_rows, LANES), F32),
            ((slots2, hidden_size), F32),
            ((slots2, mesh_rows), BF16),
            ((slots2, ceil_to(remote, LANES)), BF16),
            ((mesh_rows, slots2), BF16),
            ((remote, slots2), BF16),
            ((mesh_rows, width), F32),
        ],
        2,
    )
    grad2, *pieces = call(
        functools.partial(process_kernel, coarse),
        [
            part2,
            pick_goal2,
            pick_coarse,
            sum_goal2,
            sum_coarse,
            centre2,
            process_source,
            process_output,
            *shifts,
        ],
        [((slots2, hidden_size), BF16)] + [((coarse, hidden_size), BF16)] * (groups - 1),
        2,
        scratch=[pltpu.VMEM((slots2, hidden_size), BF16), pltpu.VMEM((slots2, hidden_size), F32)],
    )
    pieces = swap_coarse(pieces, groups)
    grad_local, back, slope, sum_rim = call(
        functools.partial(process_back_kernel, grid_rows),
        [
            half,
            grad2,
            live_send,
            live_send2,
            sum_goal2,
            cotangent,
            process_source,
            process_dest,
            encoder_output,
            encoder_gain,
            normed,
            inverse,
        ],
        [
            ((mesh_rows, width), F32),
            ((mesh_rows, hidden_size), BF16),
            ((slots, hidden_size), BF16),
            ((2 * rim, slots), BF16),
        ],
        2,
    )
    grad, near, far, grad16 = call(
        encode_back_kernel,
        [
            grad_local,
            back,
            normed,
            inverse,
            slope,
            pick_goal,
            sum_rim,
            encoder_gain,
            process_source,
            encoder_output,
            *pieces,
        ],
        [((slots, hidden_size), BF16)]
        + [((rim, hidden_size), BF16)] * 2
        + [((coarse, width), F32)],
        2,
    )
    near, far = swap_halo(near, far, patches)
    mesh_grad, own = call(
        own_back_kernel,
        [grad, live_send, live_goal, grad_local, grad16, encoder_source, encoder_dest],
        [((mesh_rows, width), BF16), ((grid_rows, width), F32)],
        2,
    )
    (grid_grad,) = call(
        finish_kernel,
        [halo_rows, own, near, far, encoder_source],
        [((grid_rows, width), BF16)],
        2,
        scratch=[pltpu.VMEM((grid_rows, width), BF16), pltpu.SemaphoreType.DMA((4,))],
        out_space=HBM,
    )
    return grid_grad, mesh_grad


def solution(mesh):
    rows, flat, whole = P(("patch", "group"), None), P(("patch", "group")), P()
    return jax.shard_map(
        on_device,
        mesh=mesh,
        in_specs=(rows,) * 3 + (flat,) * 7 + (whole,) * 8,
        out_specs=(rows, rows),
        check_vma=False,
    )
```

```python
import functools

import jax
import jax.numpy as jnp
from jax import lax
from jax.experimental import pallas as pl
from jax.experimental.pallas import tpu as pltpu
from jax.sharding import PartitionSpec as P


EPSILON = 1e-05
LANES = 128
FIRST = 256
F32 = jnp.float32
BF16 = jnp.bfloat16
I32 = jnp.int32
I16 = jnp.int16


def mm(a, b):
    return jnp.dot(a, b, preferred_element_type=F32)


def mm_t(a, b):
    return lax.dot_general(a, b, (((1,), (1,)), ((), ())), preferred_element_type=F32)


def half_silu(u):
    t = jnp.tanh(u)
    a = 1.0 + t
    value = u * a
    return value, a + value * (1.0 - t)


def ceil_to(n, k):
    return (n + k - 1) // k * k


def to_columns(row):
    n = row.shape[1]
    parts = []
    for i in range(0, n, LANES):
        parts.append(jnp.broadcast_to(row[:, i : i + LANES], (LANES, LANES)).T.astype(I16))
    return jnp.concatenate(parts, axis=0)


def one_hot(equal):
    return jnp.where(equal, jnp.ones((), BF16), jnp.zeros((), BF16))


def pick(columns, first, width):
    lane = lax.broadcasted_iota(I32, columns.shape, 1)
    parts = [one_hot(columns == (lane + (first + i)).astype(I16)) for i in range(0, width, LANES)]
    return parts[0] if len(parts) == 1 else jnp.concatenate(parts, axis=1)


def spread(row, first, height):
    shape = (height, row.shape[1])
    number = lax.broadcasted_iota(I32, shape, 0) + first
    return one_hot(jnp.broadcast_to(row, shape).astype(I16) == number.astype(I16))


def only_live(rows, count):
    slot = lax.broadcasted_iota(I32, rows.shape, 1)
    return jnp.where(slot < count, rows, -1)


def normalise(values):
    center = values - jnp.mean(values, axis=-1, keepdims=True)
    inverse = lax.rsqrt(jnp.mean(center * center, axis=-1, keepdims=True) + EPSILON)
    return center * inverse, inverse


def centred(values):
    return values - jnp.mean(values, axis=-1, keepdims=True)


def normalise_back(centre, normed, inverse):
    return inverse * (centre - normed * jnp.mean(centre * normed, axis=-1, keepdims=True))


def halves(rows, even):
    half = rows.shape[1] // 2
    first, second = rows[:, :half], rows[:, half:]
    return jnp.where(even, second, first), jnp.where(even, first, second)


def coarse_slots(sender, mesh_rows, coarse, me):
    offset = sender - mesh_rows
    owner = offset // coarse
    row = offset - owner * coarse
    mask = owner ^ me
    moved = jnp.where(mask == 0, row, mesh_rows + (mask - 1) * coarse + row)
    return jnp.where(offset < 0, sender, moved)


def even_patch():
    return lax.rem(lax.axis_index("patch"), 2) == 0


def as_row(ref):
    return ref[...].reshape(1, ref.shape[0])


def select_kernel(halo_hbm, grid_hbm, near, far, table, halo, sems):
    copies = [
        pltpu.make_async_copy(halo_hbm, halo, sems.at[0]),
        pltpu.make_async_copy(grid_hbm, table, sems.at[1]),
    ]
    for copy in copies:
        copy.start()
    copies[0].wait()
    rows_near, rows_far = halves(as_row(halo), even_patch())
    pick_near = pick(to_columns(rows_near), 0, table.shape[0])
    pick_far = pick(to_columns(rows_far), 0, table.shape[0])
    copies[1].wait()
    near[...] = mm(pick_near, table[...]).astype(BF16)
    far[...] = mm(pick_far, table[...]).astype(BF16)


def rim_starts(grid_rows, rim):
    even = even_patch()
    return (
        jnp.where(even, grid_rows + rim, grid_rows),
        jnp.where(even, grid_rows, grid_rows + rim),
    )


def arrange(first, rows):
    slots = first.shape[1]
    groups = slots // LANES
    flags = [first[:, i * LANES : (i + 1) * LANES] for i in range(groups)]
    spare = ceil_to(groups, 8) - groups
    stack = jnp.concatenate(flags + [jnp.zeros((spare, LANES), F32)] * bool(spare), axis=0)
    shape = (LANES, LANES)
    before = lax.broadcasted_iota(I32, shape, 0) <= lax.broadcasted_iota(I32, shape, 1)
    sums = mm(stack.astype(BF16), jnp.where(before, 1.0, 0.0).astype(BF16))
    total = jnp.zeros((1, 1), F32)
    counted = []
    for i in range(groups):
        counted.append(sums[i : i + 1, :] + total)
        total = total + sums[i : i + 1, LANES - 1 :]
    counted = jnp.concatenate(counted, axis=1)
    slot = lax.broadcasted_iota(I32, first.shape, 1).astype(F32)
    place = jnp.where(first > 0.0, counted - 1.0, total + slot - counted)
    order = spread(place.astype(I32), 0, slots)
    digits = [d for row in rows for d in (row // LANES, row % LANES)]
    digits = [d.astype(F32) for d in digits]
    spare = ceil_to(len(digits), 8) - len(digits)
    digits = jnp.concatenate(digits + [jnp.zeros((spare, slots), F32)] * bool(spare), axis=0)
    moved = mm_t(digits.astype(BF16), order).astype(I32)
    moved = [moved[2 * i : 2 * i + 1, :] * LANES + moved[2 * i + 1 : 2 * i + 2, :] for i in range(len(rows))]
    return total, moved


def flagged(condition, count):
    slot = lax.broadcasted_iota(I32, condition.shape, 1)
    return jnp.where(condition & (slot < count), 1.0, 0.0)


def encode_local_kernel(
    coarse,
    counts,
    sender,
    target,
    sender2,
    target2,
    grid,
    mesh,
    w_source,
    w_dest,
    early,
    part,
    hidden,
    summed16,
    live_send,
    live_goal,
    live_send2,
    live_goal2,
    send_col2,
    goal_col2,
    pick_rim,
    pick_goal,
):
    rows, grid_rows = mesh.shape[0], grid.shape[0]
    rim = pick_rim.shape[1] // 2
    source = (0.5 * mm(grid[...], w_source[...])).astype(BF16)
    dest = (0.5 * mm(mesh[...], w_dest[...])).astype(BF16)
    send = as_row(sender)
    total, (send, goal) = arrange(flagged(send >= grid_rows, counts[0]), [send, as_row(target)])
    early[:1, :] = jnp.broadcast_to(total, (1, LANES)).astype(I32)
    send_col = to_columns(send)
    near_first, far_first = rim_starts(grid_rows, rim)
    pick_rim[:, :rim] = pick(send_col, near_first, rim)
    pick_rim[:, rim:] = pick(send_col, far_first, rim)
    pick_goal[...] = pick(to_columns(goal), 0, rows)
    live_send[...] = only_live(send, counts[0])
    live_goal[...] = only_live(goal, counts[0])
    for c in pieces_of(part.shape[0], FIRST):
        u = mm(pick(send_col[c, :], 0, grid_rows), source) + mm(pick_goal[c, :], dest)
        part[c, :] = u
        if c.start:
            hidden[c, :] = (u + u * jnp.tanh(u)).astype(BF16)
    summed16[...] = mm(spread(live_goal[:, FIRST:], 0, coarse), hidden[FIRST:, :])
    send2 = coarse_slots(as_row(sender2), rows, coarse, lax.axis_index("group"))
    total, (send2, goal2) = arrange(flagged(send2 >= rows, counts[1]), [send2, as_row(target2)])
    early[1:, :] = jnp.broadcast_to(total, (1, LANES)).astype(I32)
    send_col2[...] = to_columns(send2)
    goal_col2[...] = to_columns(goal2)
    live_send2[...] = only_live(send2, counts[1])
    live_goal2[...] = only_live(goal2, counts[1])


def pieces_of(n, size):
    return [slice(i, min(i + size, n)) for i in range(0, n, size)]


def encode_halo_kernel(
    coarse,
    early,
    near,
    far,
    part,
    hidden_local,
    summed16,
    pick_rim,
    live_goal,
    mesh,
    w_source,
    w_out,
    gain,
    half,
    hidden,
    updated16,
):
    number = jnp.max(early[:1, :])
    halo = jnp.concatenate([near[...], far[...]], axis=0)
    source = (0.5 * mm(halo, w_source[...])).astype(BF16)

    def edges(c):
        u = part[c, :] + mm(pick_rim[c, :], source)
        half[c, :] = u
        hidden[c, :] = (u + u * jnp.tanh(u)).astype(BF16)

    def finish(summed):
        normed, _ = normalise(mm(summed.astype(BF16), w_out[...]))
        updated16[...] = (mesh[:coarse, :].astype(F32) + normed * as_row(gain)).astype(BF16)

    edges(slice(0, FIRST))

    @pl.when(number <= FIRST)
    def _():
        goal = spread(live_goal[:, :FIRST], 0, coarse)
        finish(summed16[...] + mm(goal, hidden[:FIRST, :]))

    @pl.when(number > FIRST)
    def _():
        for c in pieces_of(part.shape[0], FIRST)[1:]:
            edges(c)
        finish(mm(spread(live_goal[...], 0, coarse), hidden[...]))


def process_local_kernel(
    hidden,
    live_goal,
    mesh,
    send_col2,
    goal_col2,
    live_send2,
    live_goal2,
    cotangent,
    w_out,
    gain,
    gain2,
    w_source,
    w_dest,
    normed_ref,
    inverse_ref,
    part,
    pick_goal2,
    pick_coarse,
    sum_goal2,
    sum_coarse,
    centre2,
    summed2,
    hidden2,
):
    rows = mesh.shape[0]
    summed = mm(spread(live_goal[...], 0, rows), hidden[...]).astype(BF16)
    normed, inverse = normalise(mm(summed, w_out[...]))
    normed_ref[...] = normed
    inverse_ref[...] = jnp.broadcast_to(inverse, inverse_ref.shape)
    updated = (mesh[...].astype(F32) + normed * as_row(gain)).astype(BF16)
    source = (0.5 * mm(updated, w_source[...])).astype(BF16)
    dest = (0.5 * mm(updated, w_dest[...])).astype(BF16)
    pick_goal2[...] = pick(goal_col2[...], 0, rows)
    pick_coarse[...] = pick(send_col2[...], rows, pick_coarse.shape[1])
    sum_goal2[...] = spread(live_goal2[...], 0, rows)
    sum_coarse[...] = spread(live_send2[...], rows, sum_coarse.shape[0])
    centre2[...] = centred(cotangent[...].astype(F32) * as_row(gain2))
    for c in pieces_of(part.shape[0], FIRST):
        u = mm(pick(send_col2[c, :], 0, rows), source) + mm(pick_goal2[c, :], dest)
        part[c, :] = u
        if c.start:
            hidden2[c, :] = (u + u * jnp.tanh(u)).astype(BF16)
    summed2[...] = mm(sum_goal2[:, FIRST:], hidden2[FIRST:, :])


def process_kernel(
    coarse,
    early,
    part,
    pick_goal2,
    pick_coarse,
    sum_goal2,
    sum_coarse,
    centre2,
    summed2,
    w_source,
    w_out,
    *refs,
):
    peers = sum_coarse.shape[0] // coarse
    received, (half, grad_first, back_ref) = refs[:peers], refs[peers : peers + 3]
    returned, (hidden, slope, grad) = refs[peers + 3 : -3], refs[-3:]
    number = jnp.max(early[1:, :])
    rows = jnp.concatenate([r[...] for r in received], axis=0)
    source = (0.5 * mm(rows, w_source[...])).astype(BF16)
    spare = pick_coarse.shape[1] - source.shape[0]
    if spare:
        source = jnp.concatenate([source, jnp.zeros((spare, source.shape[1]), BF16)], axis=0)

    def edges(c):
        u = part[c, :] + mm(pick_coarse[c, :], source)
        half[c, :] = u
        value, double = half_silu(u)
        hidden[c, :] = value.astype(BF16)
        slope[c, :] = double

    def turn(summed):
        normed, inverse = normalise(mm(summed.astype(BF16), w_out[...]))
        back = normalise_back(centre2[...], normed, inverse).astype(BF16)
        back = (0.5 * mm_t(back, w_out[...])).astype(BF16)
        back_ref[...] = back
        grad_first[...] = (mm(pick_goal2[:FIRST, :], back) * slope[:FIRST, :]).astype(BF16)
        return back

    def send(sums):
        for i, out in enumerate(returned):
            out[...] = sums[i * coarse : (i + 1) * coarse].astype(BF16)

    edges(slice(0, FIRST))

    @pl.when(number <= FIRST)
    def _():
        turn(summed2[...] + mm(sum_goal2[:, :FIRST], hidden[:FIRST, :]))
        send(mm(sum_coarse[:, :FIRST], grad_first[...]))

    @pl.when(number > FIRST)
    def _():
        later = pieces_of(part.shape[0], FIRST)[1:]
        for c in later:
            edges(c)
        back = turn(mm(sum_goal2[...], hidden[...]))
        grad[:FIRST, :] = grad_first[...]
        for c in later:
            grad[c, :] = (mm(pick_goal2[c, :], back) * slope[c, :]).astype(BF16)
        send(mm(sum_coarse[...], grad[...]))


def process_back_kernel(
    grid_rows,
    half,
    half2,
    grad_first,
    back2,
    pick_goal2,
    live_send,
    live_send2,
    sum_goal2,
    cotangent,
    w_source,
    w_dest,
    w_out,
    gain,
    normed,
    inverse,
    grad_local,
    back_ref,
    slope,
    sum_rim,
    grad,
):
    rows = cotangent.shape[0]
    rim = sum_rim.shape[0] // 2
    grad[:FIRST, :] = grad_first[...]
    for c in pieces_of(half2.shape[0], FIRST)[1:]:
        double = half_silu(half2[c, :])[1]
        grad[c, :] = (mm(pick_goal2[c, :], back2[...]) * double).astype(BF16)
    table = mm(spread(live_send2[...], 0, rows), grad[...]).astype(BF16)
    dest = mm(sum_goal2[...], grad[...]).astype(BF16)
    local = cotangent[...].astype(F32) + mm_t(table, w_source[...]) + mm_t(dest, w_dest[...])
    grad_local[...] = local
    back = normalise_back(centred(local * as_row(gain)), normed[...], inverse[:, :1])
    back_ref[...] = (0.5 * mm_t(back.astype(BF16), w_out[...])).astype(BF16)
    near_first, far_first = rim_starts(grid_rows, rim)
    sum_rim[:rim, :] = spread(live_send[...], near_first, rim)
    sum_rim[rim:, :] = spread(live_send[...], far_first, rim)
    slope[...] = half_silu(half[:FIRST, :])[1].astype(BF16)


def encode_back_kernel(
    early,
    grad_local,
    back_local,
    normed,
    inverse,
    half,
    slope,
    pick_goal,
    sum_rim,
    gain,
    w_source2,
    w_out,
    *refs,
):
    received, (back_ref, grad_first, near, far, updated16, grad) = refs[:-6], refs[-6:]
    coarse = updated16.shape[0]
    rim = near.shape[0]
    number = jnp.max(early[:1, :])
    total = received[0][...].astype(F32)
    for r in received[1:]:
        total = total + r[...].astype(F32)
    updated = grad_local[:coarse, :] + mm_t(total.astype(BF16), w_source2[...])
    updated16[...] = updated
    back = normalise_back(
        centred(updated * as_row(gain)), normed[:coarse, :], inverse[:coarse, :1]
    )
    back = (0.5 * mm_t(back.astype(BF16), w_out[...])).astype(BF16)
    back = jnp.concatenate([back, back_local[coarse:, :]], axis=0)
    back_ref[...] = back
    first = mm(pick_goal[:FIRST, :], back) * slope[...].astype(F32)
    grad_first[...] = first.astype(BF16)

    @pl.when(number <= FIRST)
    def _():
        far[...] = mm(sum_rim[rim:, :FIRST], grad_first[...]).astype(BF16)
        near[...] = mm(sum_rim[:rim, :FIRST], grad_first[...]).astype(BF16)

    @pl.when(number > FIRST)
    def _():
        grad[:FIRST, :] = grad_first[...]
        for c in pieces_of(half.shape[0], FIRST)[1:]:
            grad[c, :] = edge_grad(c, pick_goal, back_ref[...], half)
        far[...] = mm(sum_rim[rim:, :], grad[...]).astype(BF16)
        near[...] = mm(sum_rim[:rim, :], grad[...]).astype(BF16)


def edge_grad(c, pick_goal, back, half):
    return (mm(pick_goal[c, :], back) * half_silu(half[c, :])[1]).astype(BF16)


def own_back_kernel(
    grad_first,
    back,
    half,
    pick_goal,
    live_send,
    live_goal,
    grad_local,
    updated16,
    w_source,
    w_dest,
    mesh_grad,
    own,
    grad,
):
    coarse = updated16.shape[0]
    rows = grad_local.shape[0]
    grad[:FIRST, :] = grad_first[...]
    for c in pieces_of(half.shape[0], FIRST)[1:]:
        grad[c, :] = edge_grad(c, pick_goal, back[...], half)
    dest = mm(spread(live_goal[...], 0, rows), grad[...]).astype(BF16)
    updated = jnp.concatenate([updated16[...], grad_local[coarse:, :]], axis=0)
    mesh_grad[...] = (updated + mm_t(dest, w_dest[...])).astype(BF16)
    source = mm(spread(live_send[...], 0, own.shape[0]), grad[...]).astype(BF16)
    own[...] = mm_t(source, w_source[...])


def finish_kernel(halo, own, near, far, w_source, out_hbm, out, sems):
    rows_near, rows_far = halves(as_row(halo), even_patch())
    peers = jnp.concatenate([near[...], far[...]], axis=0)
    projected = mm_t(peers, w_source[...]).astype(BF16)
    where = jnp.concatenate([rows_near, rows_far], axis=1)
    copies = []
    for i, c in enumerate(pieces_of(own.shape[0], own.shape[0] // 4)):
        chosen = spread(where, c.start, c.stop - c.start)
        out[c, :] = (own[c, :] + mm(chosen, projected)).astype(BF16)
        copies.append(pltpu.make_async_copy(out.at[c], out_hbm.at[c], sems.at[i]))
        copies[-1].start()
    for copy in copies:
        copy.wait()


SMEM = pl.BlockSpec(memory_space=pltpu.SMEM)
HBM = pl.BlockSpec(memory_space=pltpu.HBM)
VMEM = pl.BlockSpec(memory_space=pltpu.VMEM)
MICROSECOND = 1 << 30


def call(kernel, arrays, outs, cost, raw=0, scalars=0, scratch=(), out_specs=None, aliases=None):
    return pl.pallas_call(
        kernel,
        out_shape=[jax.ShapeDtypeStruct(s, d) for s, d in outs],
        in_specs=[HBM] * raw + [SMEM] * scalars + [VMEM] * (len(arrays) - raw - scalars),
        out_specs=out_specs or [VMEM] * len(outs),
        input_output_aliases=aliases or {},
        scratch_shapes=list(scratch),
        compiler_params=pltpu.CompilerParams(vmem_limit_bytes=24 << 20),
        cost_estimate=pl.CostEstimate(
            flops=int(cost * MICROSECOND), bytes_accessed=1 << 20, transcendentals=0
        ),
    )(*(pltpu.with_memory_space_constraint(x, pltpu.HBM) for x in arrays[:raw]), *arrays[raw:])


def swap_halo(near, far, n):
    far_pairs = [(i, (i + 1) % n if i % 2 else (i - 1) % n) for i in range(n)]
    far = lax.ppermute(far, "patch", far_pairs)
    near = lax.ppermute(near, "patch", [(i, i ^ 1) for i in range(n)])
    return near, far


def swap_coarse(pieces, n):
    out = []
    for k, piece in enumerate(pieces, 1):
        out.append(lax.ppermute(piece, "group", [(i, i ^ k) for i in range(n)]))
    return out


def on_device(
    grid_latent,
    mesh_latent,
    cotangent,
    halo_rows,
    encoder_sender,
    encoder_target,
    encoder_count,
    process_sender,
    process_target,
    process_count,
    encoder_source,
    encoder_dest,
    encoder_output,
    encoder_gain,
    process_source,
    process_dest,
    process_output,
    process_gain,
):
    patches, groups = lax.axis_size("patch"), lax.axis_size("group")
    grid_rows, width = grid_latent.shape
    mesh_rows = mesh_latent.shape[0]
    hidden_size = encoder_source.shape[1]
    coarse = mesh_rows // 16
    rim = halo_rows.shape[0] // 2
    slots, slots2 = encoder_sender.shape[0], process_sender.shape[0]

    row_form, row_form2 = ((1, slots), I32), ((1, slots2), I32)
    column_form2 = ((slots2, LANES), I16)
    remote = coarse * (groups - 1)
    near, far, grid = call(
        select_kernel,
        [halo_rows, grid_latent],
        [((rim, width), BF16)] * 2 + [((grid_rows, width), BF16)],
        4,
        raw=2,
        scratch=[pltpu.VMEM(halo_rows.shape, I32), pltpu.SemaphoreType.DMA((2,))],
    )
    near, far = swap_halo(near, far, patches)
    (
        early,
        part,
        hidden,
        summed16,
        live_send,
        live_goal,
        live_send2,
        live_goal2,
        send_col2,
        goal_col2,
        pick_rim,
        pick_goal,
    ) = call(
        functools.partial(encode_local_kernel, coarse),
        [
            jnp.concatenate([encoder_count, process_count]),
            encoder_sender,
            encoder_target,
            process_sender,
            process_target,
            grid,
            mesh_latent,
            encoder_source,
            encoder_dest,
        ],
        [((2, LANES), I32), ((slots, hidden_size), F32), ((slots, hidden_size), BF16)]
        + [((coarse, hidden_size), F32), row_form, row_form, row_form2, row_form2]
        + [column_form2, column_form2]
        + [((slots, 2 * rim), BF16), ((slots, mesh_rows), BF16)],
        2,
        scalars=1,
    )
    half, hidden, updated16 = call(
        functools.partial(encode_halo_kernel, coarse),
        [
            early,
            near,
            far,
            part,
            hidden,
            summed16,
            pick_rim,
            live_goal,
            mesh_latent,
            encoder_source,
            encoder_output,
            encoder_gain,
        ],
        [((slots, hidden_size), F32), ((slots, hidden_size), BF16), ((coarse, width), BF16)],
        2,
        aliases={3: 0, 4: 1},
    )
    shifts = swap_coarse([updated16] * (groups - 1), groups)
    (
        normed,
        inverse,
        part2,
        pick_goal2,
        pick_coarse,
        sum_goal2,
        sum_coarse,
        centre2,
        summed2,
    ) = call(
        process_local_kernel,
        [
            hidden,
            live_goal,
            mesh_latent,
            send_col2,
            goal_col2,
            live_send2,
            live_goal2,
            cotangent,
            encoder_output,
            encoder_gain,
            process_gain,
            process_source,
            process_dest,
        ],
        [
            ((mesh_rows, width), F32),
            ((mesh_rows, LANES), F32),
            ((slots2, hidden_size), F32),
            ((slots2, mesh_rows), BF16),
            ((slots2, ceil_to(remote, LANES)), BF16),
            ((mesh_rows, slots2), BF16),
            ((remote, slots2), BF16),
            ((mesh_rows, width), F32),
            ((mesh_rows, hidden_size), F32),
        ],
        2,
        scratch=[pltpu.VMEM((slots2, hidden_size), BF16)],
    )
    half2, grad_first2, back2, *pieces = call(
        functools.partial(process_kernel, coarse),
        [
            early,
            part2,
            pick_goal2,
            pick_coarse,
            sum_goal2,
            sum_coarse,
            centre2,
            summed2,
            process_source,
            process_output,
            *shifts,
        ],
        [((slots2, hidden_size), F32), ((FIRST, hidden_size), BF16)]
        + [((mesh_rows, hidden_size), BF16)]
        + [((coarse, hidden_size), BF16)] * (groups - 1),
        2,
        scratch=[
            pltpu.VMEM((slots2, hidden_size), BF16),
            pltpu.VMEM((slots2, hidden_size), F32),
            pltpu.VMEM((slots2, hidden_size), BF16),
        ],
        aliases={1: 0},
    )
    pieces = swap_coarse(pieces, groups)
    grad_local, back, slope, sum_rim = call(
        functools.partial(process_back_kernel, grid_rows),
        [
            half,
            half2,
            grad_first2,
            back2,
            pick_goal2,
            live_send,
            live_send2,
            sum_goal2,
            cotangent,
            process_source,
            process_dest,
            encoder_output,
            encoder_gain,
            normed,
            inverse,
        ],
        [
            ((mesh_rows, width), F32),
            ((mesh_rows, hidden_size), BF16),
            ((FIRST, hidden_size), BF16),
            ((2 * rim, slots), BF16),
        ],
        2,
        scratch=[pltpu.VMEM((slots2, hidden_size), BF16)],
    )
    back, grad_first, near, far, grad16 = call(
        encode_back_kernel,
        [
            early,
            grad_local,
            back,
            normed,
            inverse,
            half,
            slope,
            pick_goal,
            sum_rim,
            encoder_gain,
            process_source,
            encoder_output,
            *pieces,
        ],
        [((mesh_rows, hidden_size), BF16), ((FIRST, hidden_size), BF16)]
        + [((rim, hidden_size), BF16)] * 2
        + [((coarse, width), F32)],
        2,
        scratch=[pltpu.VMEM((slots, hidden_size), BF16)],
    )
    near, far = swap_halo(near, far, patches)
    mesh_grad, own = call(
        own_back_kernel,
        [
            grad_first,
            back,
            half,
            pick_goal,
            live_send,
            live_goal,
            grad_local,
            grad16,
            encoder_source,
            encoder_dest,
        ],
        [((mesh_rows, width), BF16), ((grid_rows, width), F32)],
        2,
        scratch=[pltpu.VMEM((slots, hidden_size), BF16)],
    )
    (grid_grad,) = call(
        finish_kernel,
        [halo_rows, own, near, far, encoder_source],
        [((grid_rows, width), BF16)],
        2,
        scratch=[pltpu.VMEM((grid_rows, width), BF16), pltpu.SemaphoreType.DMA((4,))],
        out_specs=[HBM],
    )
    return grid_grad, mesh_grad


def solution(mesh):
    rows, flat, whole = P(("patch", "group"), None), P(("patch", "group")), P()
    return jax.shard_map(
        on_device,
        mesh=mesh,
        in_specs=(rows,) * 3 + (flat,) * 7 + (whole,) * 8,
        out_specs=(rows, rows),
        check_vma=False,
    )
```

```python
import functools

import jax
import jax.numpy as jnp
from jax import lax
from jax.experimental import pallas as pl
from jax.experimental.pallas import tpu as pltpu
from jax.sharding import PartitionSpec as P


EPSILON = 1e-05
LANES = 128
FIRST = 256
F32 = jnp.float32
BF16 = jnp.bfloat16
I32 = jnp.int32
I16 = jnp.int16


def mm(a, b):
    return jnp.dot(a, b, preferred_element_type=F32)


def mm_t(a, b):
    return lax.dot_general(a, b, (((1,), (1,)), ((), ())), preferred_element_type=F32)


def half_silu(u):
    t = jnp.tanh(u)
    a = 1.0 + t
    value = u * a
    return value, a + value * (1.0 - t)


def ceil_to(n, k):
    return (n + k - 1) // k * k


def to_columns(*rows):
    packed = rows[0] if len(rows) == 1 else rows[0] + rows[1] * 4096
    parts = []
    for i in range(0, packed.shape[1], LANES):
        parts.append(jnp.broadcast_to(packed[:, i : i + LANES], (LANES, LANES)).T)
    columns = jnp.concatenate(parts, axis=0)
    if len(rows) == 1:
        return columns.astype(I16)
    low = jnp.bitwise_and(columns, 4095).astype(I16)
    return low, lax.shift_right_logical(columns, 12).astype(I16)


def one_hot(equal):
    return jnp.where(equal, jnp.ones((), BF16), jnp.zeros((), BF16))


def pick(columns, first, width):
    lane = lax.broadcasted_iota(I32, columns.shape, 1)
    parts = [one_hot(columns == (lane + (first + i)).astype(I16)) for i in range(0, width, LANES)]
    return parts[0] if len(parts) == 1 else jnp.concatenate(parts, axis=1)


def spread(row, first, height):
    shape = (height, row.shape[1])
    number = lax.broadcasted_iota(I32, shape, 0) + first
    return one_hot(jnp.broadcast_to(row, shape).astype(I16) == number.astype(I16))


def only_live(rows, count):
    slot = lax.broadcasted_iota(I32, rows.shape, 1)
    return jnp.where(slot < count, rows, -1)


def normalise(values):
    center = values - jnp.mean(values, axis=-1, keepdims=True)
    inverse = lax.rsqrt(jnp.mean(center * center, axis=-1, keepdims=True) + EPSILON)
    return center * inverse, inverse


def centred(values):
    return values - jnp.mean(values, axis=-1, keepdims=True)


def normalise_back(centre, normed, inverse):
    return inverse * (centre - normed * jnp.mean(centre * normed, axis=-1, keepdims=True))


def halves(rows, even):
    half = rows.shape[1] // 2
    first, second = rows[:, :half], rows[:, half:]
    return jnp.where(even, second, first), jnp.where(even, first, second)


def plans(n):
    masks = [tuple(i ^ k for i in range(n)) for k in range(n - 1, 0, -1)]
    if n == 4:
        return [(1, 3, 0, 2), (3, 2, 1, 0), (2, 0, 3, 1)], masks
    return masks, masks


def look_up(table, index):
    value = jnp.int32(table[0])
    for i, entry in enumerate(table[1:], 1):
        value = jnp.where(index == i, jnp.int32(entry), value)
    return value


def coarse_slots(sender, mesh_rows, coarse, owners):
    offset = sender - mesh_rows
    owner = offset // coarse
    moved = offset - owner * coarse
    for k, other in enumerate(owners):
        moved = moved + jnp.where(owner == other, mesh_rows + k * coarse, 0)
    return jnp.where(offset < 0, sender, moved)


def even_patch():
    return lax.rem(lax.axis_index("patch"), 2) == 0


def as_row(ref):
    return ref[...].reshape(1, ref.shape[0])


def select_kernel(halo_hbm, grid_hbm, near, far, table, halo, sems):
    copies = [
        pltpu.make_async_copy(halo_hbm, halo, sems.at[0]),
        pltpu.make_async_copy(grid_hbm, table, sems.at[1]),
    ]
    for copy in copies:
        copy.start()
    copies[0].wait()
    rows_near, rows_far = halves(as_row(halo), even_patch())
    pick_near = pick(to_columns(rows_near), 0, table.shape[0])
    pick_far = pick(to_columns(rows_far), 0, table.shape[0])
    copies[1].wait()
    near[...] = mm(pick_near, table[...]).astype(BF16)
    far[...] = mm(pick_far, table[...]).astype(BF16)


def rim_starts(grid_rows, rim):
    even = even_patch()
    return (
        jnp.where(even, grid_rows + rim, grid_rows),
        jnp.where(even, grid_rows, grid_rows + rim),
    )


def arrange(first, rows):
    slots = first.shape[1]
    groups = slots // LANES
    flags = [first[:, i * LANES : (i + 1) * LANES] for i in range(groups)]
    spare = ceil_to(groups, 8) - groups
    stack = jnp.concatenate(flags + [jnp.zeros((spare, LANES), F32)] * bool(spare), axis=0)
    shape = (LANES, LANES)
    before = lax.broadcasted_iota(I32, shape, 0) <= lax.broadcasted_iota(I32, shape, 1)
    sums = mm(stack.astype(BF16), jnp.where(before, 1.0, 0.0).astype(BF16))
    total = jnp.zeros((1, 1), F32)
    counted = []
    for i in range(groups):
        counted.append(sums[i : i + 1, :] + total)
        total = total + sums[i : i + 1, LANES - 1 :]
    counted = jnp.concatenate(counted, axis=1)
    slot = lax.broadcasted_iota(I32, first.shape, 1).astype(F32)
    place = jnp.where(first > 0.0, counted - 1.0, total + slot - counted)
    order = spread(place.astype(I32), 0, slots)
    digits = []
    for row in rows:
        digits += [lax.shift_right_logical(row, 7), jnp.bitwise_and(row, 127)]
    digits = [d.astype(F32) for d in digits]
    spare = ceil_to(len(digits), 8) - len(digits)
    digits = jnp.concatenate(digits + [jnp.zeros((spare, slots), F32)] * bool(spare), axis=0)
    moved = mm_t(digits.astype(BF16), order).astype(I32)
    moved = [moved[2 * i : 2 * i + 1, :] * 128 + moved[2 * i + 1 : 2 * i + 2, :] for i in range(len(rows))]
    return total, moved


def flagged(condition, count):
    slot = lax.broadcasted_iota(I32, condition.shape, 1)
    return jnp.where(condition & (slot < count), 1.0, 0.0)


def encode_local_kernel(
    groups,
    coarse,
    counts,
    sender,
    target,
    sender2,
    target2,
    grid,
    mesh,
    w_source,
    w_dest,
    early,
    part,
    hidden,
    summed16,
    live_send,
    live_goal,
    live_send2,
    live_goal2,
    send_col2,
    goal_col2,
    pick_rim,
    pick_goal,
):
    count, count2 = counts[0], counts[1]
    rows, grid_rows = mesh.shape[0], grid.shape[0]
    rim = pick_rim.shape[1] // 2
    source = (0.5 * mm(grid[...], w_source[...])).astype(BF16)
    dest = (0.5 * mm(mesh[...], w_dest[...])).astype(BF16)
    me = lax.axis_index("group")
    gather, reduce = plans(groups)
    sources = [look_up([p.index(i) for i in range(groups)], me) for p in gather]
    goals = [look_up(p, me) for p in reduce]
    send, send2 = as_row(sender), as_row(sender2)
    back2 = coarse_slots(send2, rows, coarse, goals)
    send2 = coarse_slots(send2, rows, coarse, sources)
    total, (send, goal) = arrange(flagged(send >= grid_rows, count), [send, as_row(target)])
    moved = [send2, as_row(target2), back2]
    total2, (send2, goal2, back2) = arrange(flagged(send2 >= rows, count2), moved)
    early[:1, :] = jnp.broadcast_to(total, (1, LANES)).astype(I32)
    early[1:, :] = jnp.broadcast_to(total2, (1, LANES)).astype(I32)
    send_col, goal_col = to_columns(send, goal)
    send_col2[...], goal_col2[...] = to_columns(send2, goal2)
    near_first, far_first = rim_starts(grid_rows, rim)
    pick_rim[:, :rim] = pick(send_col, near_first, rim)
    pick_rim[:, rim:] = pick(send_col, far_first, rim)
    pick_goal[...] = pick(goal_col, 0, rows)
    live_send[...] = only_live(send, count)
    live_goal[...] = only_live(goal, count)
    live_send2[...] = only_live(back2, count2)
    live_goal2[...] = only_live(goal2, count2)
    for c in pieces_of(part.shape[0], FIRST):
        u = mm(pick(send_col[c, :], 0, grid_rows), source) + mm(pick_goal[c, :], dest)
        part[c, :] = u
        if c.start:
            hidden[c, :] = (u + u * jnp.tanh(u)).astype(BF16)
    summed16[...] = mm(spread(live_goal[:, FIRST:], 0, coarse), hidden[FIRST:, :])


def pieces_of(n, size):
    return [slice(i, min(i + size, n)) for i in range(0, n, size)]


def encode_halo_kernel(
    coarse,
    early,
    near,
    far,
    part,
    hidden_local,
    summed16,
    pick_rim,
    live_goal,
    mesh,
    w_source,
    w_out,
    gain,
    half,
    hidden,
    updated16,
):
    number = jnp.max(early[:1, :])
    halo = jnp.concatenate([near[...], far[...]], axis=0)
    source = (0.5 * mm(halo, w_source[...])).astype(BF16)

    def edges(c):
        u = part[c, :] + mm(pick_rim[c, :], source)
        half[c, :] = u
        hidden[c, :] = (u + u * jnp.tanh(u)).astype(BF16)

    def finish(summed):
        normed, _ = normalise(mm(summed.astype(BF16), w_out[...]))
        updated16[...] = (mesh[:coarse, :].astype(F32) + normed * as_row(gain)).astype(BF16)

    edges(slice(0, FIRST))

    @pl.when(number <= FIRST)
    def _():
        goal = spread(live_goal[:, :FIRST], 0, coarse)
        finish(summed16[...] + mm(goal, hidden[:FIRST, :]))

    @pl.when(number > FIRST)
    def _():
        for c in pieces_of(part.shape[0], FIRST)[1:]:
            edges(c)
        finish(mm(spread(live_goal[...], 0, coarse), hidden[...]))


def process_local_kernel(
    hidden,
    live_goal,
    mesh,
    send_col2,
    goal_col2,
    live_send2,
    live_goal2,
    cotangent,
    w_out,
    gain,
    gain2,
    w_source,
    w_dest,
    normed_ref,
    inverse_ref,
    part,
    pick_goal2,
    pick_coarse,
    sum_goal2,
    sum_coarse,
    centre2,
    summed2,
    hidden2,
):
    rows = mesh.shape[0]
    summed = mm(spread(live_goal[...], 0, rows), hidden[...]).astype(BF16)
    normed, inverse = normalise(mm(summed, w_out[...]))
    normed_ref[...] = normed
    inverse_ref[...] = jnp.broadcast_to(inverse, inverse_ref.shape)
    updated = (mesh[...].astype(F32) + normed * as_row(gain)).astype(BF16)
    source = (0.5 * mm(updated, w_source[...])).astype(BF16)
    dest = (0.5 * mm(updated, w_dest[...])).astype(BF16)
    pick_goal2[...] = pick(goal_col2[...], 0, rows)
    pick_coarse[...] = pick(send_col2[...], rows, pick_coarse.shape[1])
    sum_goal2[...] = spread(live_goal2[...], 0, rows)
    sum_coarse[...] = spread(live_send2[...], rows, sum_coarse.shape[0])
    centre2[...] = centred(cotangent[...].astype(F32) * as_row(gain2))
    for c in pieces_of(part.shape[0], FIRST):
        u = mm(pick(send_col2[c, :], 0, rows), source) + mm(pick_goal2[c, :], dest)
        part[c, :] = u
        if c.start:
            hidden2[c, :] = (u + u * jnp.tanh(u)).astype(BF16)
    summed2[...] = mm(sum_goal2[:, FIRST:], hidden2[FIRST:, :])


def process_kernel(
    coarse,
    early,
    part,
    pick_goal2,
    pick_coarse,
    sum_goal2,
    sum_coarse,
    centre2,
    summed2,
    w_source,
    w_out,
    *refs,
):
    peers = sum_coarse.shape[0] // coarse
    received, (half, grad_first, back_ref) = refs[:peers], refs[peers : peers + 3]
    returned, (hidden, slope, grad) = refs[peers + 3 : -3], refs[-3:]
    number = jnp.max(early[1:, :])
    rows = jnp.concatenate([r[...] for r in received], axis=0)
    source = (0.5 * mm(rows, w_source[...])).astype(BF16)
    spare = pick_coarse.shape[1] - source.shape[0]
    if spare:
        source = jnp.concatenate([source, jnp.zeros((spare, source.shape[1]), BF16)], axis=0)

    def edges(c):
        u = part[c, :] + mm(pick_coarse[c, :], source)
        half[c, :] = u
        value, double = half_silu(u)
        hidden[c, :] = value.astype(BF16)
        slope[c, :] = double

    def turn(summed):
        center = centred(mm(summed.astype(BF16), w_out[...]))
        inverse = lax.rsqrt(jnp.mean(center * center, axis=-1, keepdims=True) + EPSILON)
        share = jnp.mean(center * centre2[...], axis=-1, keepdims=True)
        share = share * inverse * inverse
        back = (inverse * (centre2[...] - center * share)).astype(BF16)
        back = (0.5 * mm_t(back, w_out[...])).astype(BF16)
        back_ref[...] = back
        grad_first[...] = (mm(pick_goal2[:FIRST, :], back) * slope[:FIRST, :]).astype(BF16)
        return back

    def send(sums):
        for i, out in enumerate(returned):
            out[...] = sums[i * coarse : (i + 1) * coarse].astype(BF16)

    edges(slice(0, FIRST))

    @pl.when(number <= FIRST)
    def _():
        turn(summed2[...] + mm(sum_goal2[:, :FIRST], hidden[:FIRST, :]))
        send(mm(sum_coarse[:, :FIRST], grad_first[...]))

    @pl.when(number > FIRST)
    def _():
        later = pieces_of(part.shape[0], FIRST)[1:]
        for c in later:
            edges(c)
        back = turn(mm(sum_goal2[...], hidden[...]))
        grad[:FIRST, :] = grad_first[...]
        for c in later:
            grad[c, :] = (mm(pick_goal2[c, :], back) * slope[c, :]).astype(BF16)
        send(mm(sum_coarse[...], grad[...]))


def process_back_kernel(
    grid_rows,
    half,
    half2,
    grad_first,
    back2,
    pick_goal2,
    live_send,
    live_send2,
    sum_goal2,
    cotangent,
    w_source,
    w_dest,
    w_out,
    gain,
    normed,
    inverse,
    grad_local,
    back_ref,
    slope,
    sum_rim,
    grad,
):
    rows = cotangent.shape[0]
    rim = sum_rim.shape[0] // 2
    grad[:FIRST, :] = grad_first[...]
    for c in pieces_of(half2.shape[0], FIRST)[1:]:
        double = half_silu(half2[c, :])[1]
        grad[c, :] = (mm(pick_goal2[c, :], back2[...]) * double).astype(BF16)
    table = mm(spread(live_send2[...], 0, rows), grad[...]).astype(BF16)
    dest = mm(sum_goal2[...], grad[...]).astype(BF16)
    local = cotangent[...].astype(F32) + mm_t(table, w_source[...]) + mm_t(dest, w_dest[...])
    grad_local[...] = local
    back = normalise_back(centred(local * as_row(gain)), normed[...], inverse[:, :1])
    back_ref[...] = (0.5 * mm_t(back.astype(BF16), w_out[...])).astype(BF16)
    near_first, far_first = rim_starts(grid_rows, rim)
    sum_rim[:rim, :] = spread(live_send[...], near_first, rim)
    sum_rim[rim:, :] = spread(live_send[...], far_first, rim)
    slope[...] = half_silu(half[:FIRST, :])[1].astype(BF16)


def encode_back_kernel(
    early,
    grad_local,
    back_local,
    normed,
    inverse,
    half,
    slope,
    pick_goal,
    sum_rim,
    gain,
    w_source2,
    w_out,
    *refs,
):
    received, (back_ref, grad_first, near, far, updated16, grad) = refs[:-6], refs[-6:]
    coarse = updated16.shape[0]
    rim = near.shape[0]
    number = jnp.max(early[:1, :])
    total = received[0][...].astype(F32)
    for r in received[1:]:
        total = total + r[...].astype(F32)
    updated = grad_local[:coarse, :] + mm_t(total.astype(BF16), w_source2[...])
    updated16[...] = updated
    back = normalise_back(
        centred(updated * as_row(gain)), normed[:coarse, :], inverse[:coarse, :1]
    )
    back = (0.5 * mm_t(back.astype(BF16), w_out[...])).astype(BF16)
    back = jnp.concatenate([back, back_local[coarse:, :]], axis=0)
    back_ref[...] = back
    first = mm(pick_goal[:FIRST, :], back) * slope[...].astype(F32)
    grad_first[...] = first.astype(BF16)

    @pl.when(number <= FIRST)
    def _():
        far[...] = mm(sum_rim[rim:, :FIRST], grad_first[...]).astype(BF16)
        near[...] = mm(sum_rim[:rim, :FIRST], grad_first[...]).astype(BF16)

    @pl.when(number > FIRST)
    def _():
        grad[:FIRST, :] = grad_first[...]
        for c in pieces_of(half.shape[0], FIRST)[1:]:
            grad[c, :] = edge_grad(c, pick_goal, back_ref[...], half)
        far[...] = mm(sum_rim[rim:, :], grad[...]).astype(BF16)
        near[...] = mm(sum_rim[:rim, :], grad[...]).astype(BF16)


def edge_grad(c, pick_goal, back, half):
    return (mm(pick_goal[c, :], back) * half_silu(half[c, :])[1]).astype(BF16)


def own_back_kernel(
    grad_first,
    back,
    half,
    pick_goal,
    live_send,
    live_goal,
    grad_local,
    updated16,
    w_source,
    w_dest,
    halo,
    near,
    mesh_grad,
    own,
    sum_far,
    grad,
):
    coarse = updated16.shape[0]
    rows = grad_local.shape[0]
    grad[:FIRST, :] = grad_first[...]
    for c in pieces_of(half.shape[0], FIRST)[1:]:
        grad[c, :] = edge_grad(c, pick_goal, back[...], half)
    dest = mm(spread(live_goal[...], 0, rows), grad[...]).astype(BF16)
    updated = jnp.concatenate([updated16[...], grad_local[coarse:, :]], axis=0)
    mesh_grad[...] = (updated + mm_t(dest, w_dest[...])).astype(BF16)
    source = mm(spread(live_send[...], 0, own.shape[0]), grad[...]).astype(BF16)
    rows_near, rows_far = halves(as_row(halo), even_patch())
    sum_far[...] = spread(rows_far, 0, own.shape[0])
    back_near = mm_t(near[...], w_source[...]).astype(BF16)
    own[...] = mm_t(source, w_source[...]) + mm(spread(rows_near, 0, own.shape[0]), back_near)


def finish_kernel(own, sum_far, far, w_source, out_hbm, out, sems):
    projected = mm_t(far[...], w_source[...]).astype(BF16)
    copies = []
    for i, c in enumerate(pieces_of(own.shape[0], own.shape[0] // 8)):
        out[c, :] = (own[c, :] + mm(sum_far[c, :], projected)).astype(BF16)
        copies.append(pltpu.make_async_copy(out.at[c], out_hbm.at[c], sems.at[i]))
        copies[-1].start()
    for copy in copies:
        copy.wait()


SMEM = pl.BlockSpec(memory_space=pltpu.SMEM)
HBM = pl.BlockSpec(memory_space=pltpu.HBM)
VMEM = pl.BlockSpec(memory_space=pltpu.VMEM)
MICROSECOND = 1 << 30


def call(kernel, arrays, outs, cost, raw=0, scalars=0, scratch=(), out_specs=None, aliases=None):
    return pl.pallas_call(
        kernel,
        out_shape=[jax.ShapeDtypeStruct(s, d) for s, d in outs],
        in_specs=[HBM] * raw + [SMEM] * scalars + [VMEM] * (len(arrays) - raw - scalars),
        out_specs=out_specs or [VMEM] * len(outs),
        input_output_aliases=aliases or {},
        scratch_shapes=list(scratch),
        compiler_params=pltpu.CompilerParams(vmem_limit_bytes=24 << 20),
        cost_estimate=pl.CostEstimate(
            flops=int(cost * MICROSECOND), bytes_accessed=1 << 20, transcendentals=0
        ),
    )(*(pltpu.with_memory_space_constraint(x, pltpu.HBM) for x in arrays[:raw]), *arrays[raw:])


def swap_halo(near, far, n):
    far_pairs = [(i, (i + 1) % n if i % 2 else (i - 1) % n) for i in range(n)]
    far = lax.ppermute(far, "patch", far_pairs)
    near = lax.ppermute(near, "patch", [(i, i ^ 1) for i in range(n)])
    return near, far


def exchange(pieces, plan):
    out = []
    for piece, goals in zip(pieces, plan):
        out.append(lax.ppermute(piece, "group", list(enumerate(goals))))
    return out


def on_device(
    grid_latent,
    mesh_latent,
    cotangent,
    halo_rows,
    encoder_sender,
    encoder_target,
    encoder_count,
    process_sender,
    process_target,
    process_count,
    encoder_source,
    encoder_dest,
    encoder_output,
    encoder_gain,
    process_source,
    process_dest,
    process_output,
    process_gain,
):
    patches, groups = lax.axis_size("patch"), lax.axis_size("group")
    grid_rows, width = grid_latent.shape
    mesh_rows = mesh_latent.shape[0]
    hidden_size = encoder_source.shape[1]
    coarse = mesh_rows // 16
    rim = halo_rows.shape[0] // 2
    slots, slots2 = encoder_sender.shape[0], process_sender.shape[0]

    row_form, row_form2 = ((1, slots), I32), ((1, slots2), I32)
    column_form2 = ((slots2, LANES), I16)
    remote = coarse * (groups - 1)
    near, far, grid = call(
        select_kernel,
        [halo_rows, grid_latent],
        [((rim, width), BF16)] * 2 + [((grid_rows, width), BF16)],
        4,
        raw=2,
        scratch=[pltpu.VMEM(halo_rows.shape, I32), pltpu.SemaphoreType.DMA((2,))],
    )
    near, far = swap_halo(near, far, patches)
    (
        early,
        part,
        hidden,
        summed16,
        live_send,
        live_goal,
        live_send2,
        live_goal2,
        send_col2,
        goal_col2,
        pick_rim,
        pick_goal,
    ) = call(
        functools.partial(encode_local_kernel, groups, coarse),
        [
            jnp.concatenate([encoder_count, process_count]),
            encoder_sender,
            encoder_target,
            process_sender,
            process_target,
            grid,
            mesh_latent,
            encoder_source,
            encoder_dest,
        ],
        [((2, LANES), I32), ((slots, hidden_size), F32), ((slots, hidden_size), BF16)]
        + [((coarse, hidden_size), F32), row_form, row_form, row_form2, row_form2]
        + [column_form2, column_form2]
        + [((slots, 2 * rim), BF16), ((slots, mesh_rows), BF16)],
        2,
        scalars=1,
    )
    half, hidden, updated16 = call(
        functools.partial(encode_halo_kernel, coarse),
        [
            early,
            near,
            far,
            part,
            hidden,
            summed16,
            pick_rim,
            live_goal,
            mesh_latent,
            encoder_source,
            encoder_output,
            encoder_gain,
        ],
        [((slots, hidden_size), F32), ((slots, hidden_size), BF16), ((coarse, width), BF16)],
        2,
        aliases={3: 0, 4: 1},
    )
    shifts = exchange([updated16] * (groups - 1), plans(groups)[0])
    (
        normed,
        inverse,
        part2,
        pick_goal2,
        pick_coarse,
        sum_goal2,
        sum_coarse,
        centre2,
        summed2,
    ) = call(
        process_local_kernel,
        [
            hidden,
            live_goal,
            mesh_latent,
            send_col2,
            goal_col2,
            live_send2,
            live_goal2,
            cotangent,
            encoder_output,
            encoder_gain,
            process_gain,
            process_source,
            process_dest,
        ],
        [
            ((mesh_rows, width), F32),
            ((mesh_rows, LANES), F32),
            ((slots2, hidden_size), F32),
            ((slots2, mesh_rows), BF16),
            ((slots2, ceil_to(remote, LANES)), BF16),
            ((mesh_rows, slots2), BF16),
            ((remote, slots2), BF16),
            ((mesh_rows, width), F32),
            ((mesh_rows, hidden_size), F32),
        ],
        2,
        scratch=[pltpu.VMEM((slots2, hidden_size), BF16)],
    )
    half2, grad_first2, back2, *pieces = call(
        functools.partial(process_kernel, coarse),
        [
            early,
            part2,
            pick_goal2,
            pick_coarse,
            sum_goal2,
            sum_coarse,
            centre2,
            summed2,
            process_source,
            process_output,
            *shifts,
        ],
        [((slots2, hidden_size), F32), ((FIRST, hidden_size), BF16)]
        + [((mesh_rows, hidden_size), BF16)]
        + [((coarse, hidden_size), BF16)] * (groups - 1),
        2,
        scratch=[
            pltpu.VMEM((slots2, hidden_size), BF16),
            pltpu.VMEM((slots2, hidden_size), F32),
            pltpu.VMEM((slots2, hidden_size), BF16),
        ],
        aliases={1: 0},
    )
    pieces = exchange(pieces, plans(groups)[1])
    grad_local, back, slope, sum_rim = call(
        functools.partial(process_back_kernel, grid_rows),
        [
            half,
            half2,
            grad_first2,
            back2,
            pick_goal2,
            live_send,
            live_send2,
            sum_goal2,
            cotangent,
            process_source,
            process_dest,
            encoder_output,
            encoder_gain,
            normed,
            inverse,
        ],
        [
            ((mesh_rows, width), F32),
            ((mesh_rows, hidden_size), BF16),
            ((FIRST, hidden_size), BF16),
            ((2 * rim, slots), BF16),
        ],
        2,
        scratch=[pltpu.VMEM((slots2, hidden_size), BF16)],
    )
    back, grad_first, near, far, grad16 = call(
        encode_back_kernel,
        [
            early,
            grad_local,
            back,
            normed,
            inverse,
            half,
            slope,
            pick_goal,
            sum_rim,
            encoder_gain,
            process_source,
            encoder_output,
            *pieces,
        ],
        [((mesh_rows, hidden_size), BF16), ((FIRST, hidden_size), BF16)]
        + [((rim, hidden_size), BF16)] * 2
        + [((coarse, width), F32)],
        2,
        scratch=[pltpu.VMEM((slots, hidden_size), BF16)],
    )
    near, far = swap_halo(near, far, patches)
    mesh_grad, own, sum_far = call(
        own_back_kernel,
        [
            grad_first,
            back,
            half,
            pick_goal,
            live_send,
            live_goal,
            grad_local,
            grad16,
            encoder_source,
            encoder_dest,
            halo_rows,
            near,
        ],
        [((mesh_rows, width), BF16), ((grid_rows, width), F32), ((grid_rows, rim), BF16)],
        2,
        scratch=[pltpu.VMEM((slots, hidden_size), BF16)],
    )
    (grid_grad,) = call(
        finish_kernel,
        [own, sum_far, far, encoder_source],
        [((grid_rows, width), BF16)],
        2,
        scratch=[pltpu.VMEM((grid_rows, width), BF16), pltpu.SemaphoreType.DMA((8,))],
        out_specs=[HBM],
    )
    return grid_grad, mesh_grad


def solution(mesh):
    rows, flat, whole = P(("patch", "group"), None), P(("patch", "group")), P()
    return jax.shard_map(
        on_device,
        mesh=mesh,
        in_specs=(rows,) * 3 + (flat,) * 7 + (whole,) * 8,
        out_specs=(rows, rows),
        check_vma=False,
    )
```

```python
import functools

import jax
import jax.numpy as jnp
from jax import lax
from jax.experimental import pallas as pl
from jax.experimental.pallas import tpu as pltpu
from jax.sharding import PartitionSpec as P


EPSILON = 1e-05
LANES = 128
FIRST = 256
F32 = jnp.float32
BF16 = jnp.bfloat16
I32 = jnp.int32
I16 = jnp.int16


def mm(a, b):
    return jnp.dot(a, b, preferred_element_type=F32)


def mm_t(a, b):
    return lax.dot_general(a, b, (((1,), (1,)), ((), ())), preferred_element_type=F32)


def half_silu(u):
    t = jnp.tanh(u)
    a = 1.0 + t
    value = u * a
    return value, a + value * (1.0 - t)


def ceil_to(n, k):
    return (n + k - 1) // k * k


def to_columns(*rows):
    packed = rows[0] if len(rows) == 1 else rows[0] + rows[1] * 4096
    parts = []
    for i in range(0, packed.shape[1], LANES):
        parts.append(jnp.broadcast_to(packed[:, i : i + LANES], (LANES, LANES)).T)
    columns = jnp.concatenate(parts, axis=0)
    if len(rows) == 1:
        return columns.astype(I16)
    low = jnp.bitwise_and(columns, 4095).astype(I16)
    return low, lax.shift_right_logical(columns, 12).astype(I16)


def one_hot(equal):
    return jnp.where(equal, jnp.ones((), BF16), jnp.zeros((), BF16))


def pick(columns, first, width):
    lane = lax.broadcasted_iota(I32, columns.shape, 1)
    parts = [one_hot(columns == (lane + (first + i)).astype(I16)) for i in range(0, width, LANES)]
    return parts[0] if len(parts) == 1 else jnp.concatenate(parts, axis=1)


def spread(row, first, height):
    shape = (height, row.shape[1])
    number = lax.broadcasted_iota(I32, shape, 0) + first
    return one_hot(jnp.broadcast_to(row, shape).astype(I16) == number.astype(I16))


def only_live(rows, count):
    slot = lax.broadcasted_iota(I32, rows.shape, 1)
    return jnp.where(slot < count, rows, -1)


def normalise(values):
    center = values - jnp.mean(values, axis=-1, keepdims=True)
    inverse = lax.rsqrt(jnp.mean(center * center, axis=-1, keepdims=True) + EPSILON)
    return center * inverse, inverse


def centred(values):
    return values - jnp.mean(values, axis=-1, keepdims=True)


def normalise_back(centre, normed, inverse):
    return inverse * (centre - normed * jnp.mean(centre * normed, axis=-1, keepdims=True))


def halves(rows, even):
    half = rows.shape[1] // 2
    first, second = rows[:, :half], rows[:, half:]
    return jnp.where(even, second, first), jnp.where(even, first, second)


def plans(n):
    masks = [tuple(i ^ k for i in range(n)) for k in range(n - 1, 0, -1)]
    if n == 4:
        return [(1, 3, 0, 2), (3, 2, 1, 0), (2, 0, 3, 1)], masks
    return masks, masks


def look_up(table, index):
    value = jnp.int32(table[0])
    for i, entry in enumerate(table[1:], 1):
        value = jnp.where(index == i, jnp.int32(entry), value)
    return value


def coarse_slots(sender, mesh_rows, coarse, owners):
    offset = sender - mesh_rows
    owner = offset // coarse
    moved = offset - owner * coarse
    for k, other in enumerate(owners):
        moved = moved + jnp.where(owner == other, mesh_rows + k * coarse, 0)
    return jnp.where(offset < 0, sender, moved)


def even_patch():
    return lax.rem(lax.axis_index("patch"), 2) == 0


def as_row(ref):
    return ref[...].reshape(1, ref.shape[0])


def select_kernel(halo_hbm, grid_hbm, near, far, table, halo, sems):
    copies = [
        pltpu.make_async_copy(halo_hbm, halo, sems.at[0]),
        pltpu.make_async_copy(grid_hbm, table, sems.at[1]),
    ]
    for copy in copies:
        copy.start()
    copies[0].wait()
    rows_near, rows_far = halves(as_row(halo), even_patch())
    pick_near = pick(to_columns(rows_near), 0, table.shape[0])
    pick_far = pick(to_columns(rows_far), 0, table.shape[0])
    copies[1].wait()
    near[...] = mm(pick_near, table[...]).astype(BF16)
    far[...] = mm(pick_far, table[...]).astype(BF16)


def rim_starts(grid_rows, rim):
    even = even_patch()
    return (
        jnp.where(even, grid_rows + rim, grid_rows),
        jnp.where(even, grid_rows, grid_rows + rim),
    )


def arrange(first, rows):
    slots = first.shape[1]
    groups = slots // LANES
    flags = [first[:, i * LANES : (i + 1) * LANES] for i in range(groups)]
    spare = ceil_to(groups, 8) - groups
    stack = jnp.concatenate(flags + [jnp.zeros((spare, LANES), F32)] * bool(spare), axis=0)
    shape = (LANES, LANES)
    before = lax.broadcasted_iota(I32, shape, 0) <= lax.broadcasted_iota(I32, shape, 1)
    sums = mm(stack.astype(BF16), jnp.where(before, 1.0, 0.0).astype(BF16))
    total = jnp.zeros((1, 1), F32)
    counted = []
    for i in range(groups):
        counted.append(sums[i : i + 1, :] + total)
        total = total + sums[i : i + 1, LANES - 1 :]
    counted = jnp.concatenate(counted, axis=1)
    slot = lax.broadcasted_iota(I32, first.shape, 1).astype(F32)
    place = jnp.where(first > 0.0, counted - 1.0, total + slot - counted)
    order = spread(place.astype(I32), 0, slots)
    digits = []
    for row in rows:
        digits += [lax.shift_right_logical(row, 7), jnp.bitwise_and(row, 127)]
    digits = [d.astype(F32) for d in digits]
    spare = ceil_to(len(digits), 8) - len(digits)
    digits = jnp.concatenate(digits + [jnp.zeros((spare, slots), F32)] * bool(spare), axis=0)
    moved = mm_t(digits.astype(BF16), order).astype(I32)
    moved = [moved[2 * i : 2 * i + 1, :] * 128 + moved[2 * i + 1 : 2 * i + 2, :] for i in range(len(rows))]
    return total, moved


def flagged(condition, count):
    slot = lax.broadcasted_iota(I32, condition.shape, 1)
    return jnp.where(condition & (slot < count), 1.0, 0.0)


def encode_local_kernel(
    groups,
    coarse,
    counts,
    sender,
    target,
    sender2,
    target2,
    grid,
    mesh,
    w_source,
    w_dest,
    early,
    part,
    hidden,
    summed16,
    live_send,
    live_goal,
    live_send2,
    live_goal2,
    send_col2,
    goal_col2,
    pick_rim,
    pick_goal,
):
    count, count2 = counts[0], counts[1]
    rows, grid_rows = mesh.shape[0], grid.shape[0]
    rim = pick_rim.shape[1] // 2
    source = (0.5 * mm(grid[...], w_source[...])).astype(BF16)
    dest = (0.5 * mm(mesh[...], w_dest[...])).astype(BF16)
    me = lax.axis_index("group")
    gather, reduce = plans(groups)
    sources = [look_up([p.index(i) for i in range(groups)], me) for p in gather]
    goals = [look_up(p, me) for p in reduce]
    send, send2 = as_row(sender), as_row(sender2)
    back2 = coarse_slots(send2, rows, coarse, goals)
    send2 = coarse_slots(send2, rows, coarse, sources)
    total, (send, goal) = arrange(flagged(send >= grid_rows, count), [send, as_row(target)])
    moved = [send2, as_row(target2), back2]
    total2, (send2, goal2, back2) = arrange(flagged(send2 >= rows, count2), moved)
    early[:1, :] = jnp.broadcast_to(total, (1, LANES)).astype(I32)
    early[1:, :] = jnp.broadcast_to(total2, (1, LANES)).astype(I32)
    send_col, goal_col = to_columns(send, goal)
    send_col2[...], goal_col2[...] = to_columns(send2, goal2)
    near_first, far_first = rim_starts(grid_rows, rim)
    pick_rim[:, :rim] = pick(send_col, near_first, rim)
    pick_rim[:, rim:] = pick(send_col, far_first, rim)
    pick_goal[...] = pick(goal_col, 0, rows)
    live_send[...] = only_live(send, count)
    live_goal[...] = only_live(goal, count)
    live_send2[...] = only_live(back2, count2)
    live_goal2[...] = only_live(goal2, count2)
    for c in pieces_of(part.shape[0], FIRST):
        u = mm(pick(send_col[c, :], 0, grid_rows), source) + mm(pick_goal[c, :], dest)
        part[c, :] = u
        if c.start:
            hidden[c, :] = (u + u * jnp.tanh(u)).astype(BF16)
    summed16[...] = mm(spread(live_goal[:, FIRST:], 0, coarse), hidden[FIRST:, :])


def pieces_of(n, size):
    return [slice(i, min(i + size, n)) for i in range(0, n, size)]


def encode_halo_kernel(
    coarse,
    early,
    near,
    far,
    part,
    hidden_local,
    summed16,
    pick_rim,
    live_goal,
    mesh,
    w_source,
    w_out,
    gain,
    half,
    hidden,
    updated16,
):
    number = jnp.max(early[:1, :])
    halo = jnp.concatenate([near[...], far[...]], axis=0)
    source = (0.5 * mm(halo, w_source[...])).astype(BF16)

    def edges(c):
        u = part[c, :] + mm(pick_rim[c, :], source)
        half[c, :] = u
        hidden[c, :] = (u + u * jnp.tanh(u)).astype(BF16)

    def finish(summed):
        normed, _ = normalise(mm(summed.astype(BF16), w_out[...]))
        updated16[...] = (mesh[:coarse, :].astype(F32) + normed * as_row(gain)).astype(BF16)

    def first_edges():
        for c in pieces_of(FIRST, 128):
            edges(c)

    @pl.when(number <= FIRST)
    def _():
        first_edges()
        goal = spread(live_goal[:, :FIRST], 0, coarse)
        finish(summed16[...] + mm(goal, hidden[:FIRST, :]))

    @pl.when(number > FIRST)
    def _():
        first_edges()
        for c in pieces_of(part.shape[0], FIRST)[1:]:
            edges(c)
        finish(mm(spread(live_goal[...], 0, coarse), hidden[...]))


def process_local_kernel(
    hidden,
    live_goal,
    mesh,
    send_col2,
    goal_col2,
    live_send2,
    live_goal2,
    cotangent,
    w_out,
    gain,
    gain2,
    w_source,
    w_dest,
    normed_ref,
    inverse_ref,
    part,
    pick_goal2,
    pick_coarse,
    sum_goal2,
    sum_coarse,
    centre2,
    summed2,
    hidden2,
):
    rows = mesh.shape[0]
    summed = mm(spread(live_goal[...], 0, rows), hidden[...]).astype(BF16)
    normed, inverse = normalise(mm(summed, w_out[...]))
    normed_ref[...] = normed
    inverse_ref[...] = jnp.broadcast_to(inverse, inverse_ref.shape)
    updated = (mesh[...].astype(F32) + normed * as_row(gain)).astype(BF16)
    source = (0.5 * mm(updated, w_source[...])).astype(BF16)
    dest = (0.5 * mm(updated, w_dest[...])).astype(BF16)
    pick_goal2[...] = pick(goal_col2[...], 0, rows)
    pick_coarse[...] = pick(send_col2[...], rows, pick_coarse.shape[1])
    sum_goal2[...] = spread(live_goal2[...], 0, rows)
    sum_coarse[...] = spread(live_send2[...], rows, sum_coarse.shape[0])
    centre2[...] = centred(cotangent[...].astype(F32) * as_row(gain2))
    for c in pieces_of(part.shape[0], FIRST):
        u = mm(pick(send_col2[c, :], 0, rows), source) + mm(pick_goal2[c, :], dest)
        part[c, :] = u
        if c.start:
            hidden2[c, :] = (u + u * jnp.tanh(u)).astype(BF16)
    summed2[...] = mm(sum_goal2[:, FIRST:], hidden2[FIRST:, :])


def process_kernel(
    coarse,
    early,
    part,
    pick_goal2,
    pick_coarse,
    sum_goal2,
    sum_coarse,
    centre2,
    summed2,
    w_source,
    w_out,
    *refs,
):
    peers = sum_coarse.shape[0] // coarse
    received, (half, grad_first, back_ref) = refs[:peers], refs[peers : peers + 3]
    returned, (hidden, slope, grad) = refs[peers + 3 : -3], refs[-3:]
    number = jnp.max(early[1:, :])
    rows = jnp.concatenate([r[...] for r in received], axis=0)
    source = (0.5 * mm(rows, w_source[...])).astype(BF16)
    spare = pick_coarse.shape[1] - source.shape[0]
    if spare:
        source = jnp.concatenate([source, jnp.zeros((spare, source.shape[1]), BF16)], axis=0)

    def edges(c):
        u = part[c, :] + mm(pick_coarse[c, :], source)
        if c.start >= FIRST:
            half[c, :] = u
        value, double = half_silu(u)
        hidden[c, :] = value.astype(BF16)
        slope[c, :] = double.astype(BF16)

    def turn(summed):
        center = centred(mm(summed.astype(BF16), w_out[...]))
        inverse = lax.rsqrt(jnp.mean(center * center, axis=-1, keepdims=True) + EPSILON)
        share = jnp.mean(center * centre2[...], axis=-1, keepdims=True)
        share = share * inverse * inverse
        back = (inverse * (centre2[...] - center * share)).astype(BF16)
        back = (0.5 * mm_t(back, w_out[...])).astype(BF16)
        back_ref[...] = back
        grad_first[...] = (mm(pick_goal2[:FIRST, :], back) * slope[:FIRST, :].astype(F32)).astype(BF16)
        return back

    def send(sums):
        for i, out in enumerate(returned):
            out[...] = sums[i * coarse : (i + 1) * coarse].astype(BF16)

    def first_edges():
        for c in pieces_of(FIRST, 128):
            edges(c)

    @pl.when(number <= FIRST)
    def _():
        first_edges()
        turn(summed2[...] + mm(sum_goal2[:, :FIRST], hidden[:FIRST, :]))
        send(mm(sum_coarse[:, :FIRST], grad_first[...]))

    @pl.when(number > FIRST)
    def _():
        first_edges()
        later = pieces_of(part.shape[0], FIRST)[1:]
        for c in later:
            edges(c)
        back = turn(mm(sum_goal2[...], hidden[...]))
        grad[:FIRST, :] = grad_first[...]
        for c in later:
            grad[c, :] = (mm(pick_goal2[c, :], back) * slope[c, :].astype(F32)).astype(BF16)
        send(mm(sum_coarse[...], grad[...]))


def process_back_kernel(
    grid_rows,
    half,
    half2,
    grad_first,
    back2,
    pick_goal2,
    live_send,
    live_send2,
    sum_goal2,
    cotangent,
    w_source,
    w_dest,
    w_out,
    gain,
    normed,
    inverse,
    grad_local,
    back_ref,
    slope,
    sum_rim,
    grad,
):
    rows = cotangent.shape[0]
    rim = sum_rim.shape[0] // 2
    grad[:FIRST, :] = grad_first[...]
    for c in pieces_of(half2.shape[0], FIRST)[1:]:
        double = half_silu(half2[c, :])[1]
        grad[c, :] = (mm(pick_goal2[c, :], back2[...]) * double).astype(BF16)
    table = mm(spread(live_send2[...], 0, rows), grad[...]).astype(BF16)
    dest = mm(sum_goal2[...], grad[...]).astype(BF16)
    local = cotangent[...].astype(F32) + mm_t(table, w_source[...]) + mm_t(dest, w_dest[...])
    grad_local[...] = local
    back = normalise_back(centred(local * as_row(gain)), normed[...], inverse[:, :1])
    back_ref[...] = (0.5 * mm_t(back.astype(BF16), w_out[...])).astype(BF16)
    near_first, far_first = rim_starts(grid_rows, rim)
    sum_rim[:rim, :] = spread(live_send[...], near_first, rim)
    sum_rim[rim:, :] = spread(live_send[...], far_first, rim)
    slope[...] = half_silu(half[:FIRST, :])[1].astype(BF16)


def encode_back_kernel(
    early,
    grad_local,
    back_local,
    normed,
    inverse,
    half,
    slope,
    pick_goal,
    sum_rim,
    gain,
    w_source2,
    w_out,
    *refs,
):
    received, (back_ref, grad_first, near, far, updated16, grad) = refs[:-6], refs[-6:]
    coarse = updated16.shape[0]
    rim = near.shape[0]
    number = jnp.max(early[:1, :])
    total = received[0][...].astype(F32)
    for r in received[1:]:
        total = total + r[...].astype(F32)
    updated = grad_local[:coarse, :] + mm_t(total.astype(BF16), w_source2[...])
    updated16[...] = updated

    def turn():
        back = normalise_back(
            centred(updated * as_row(gain)), normed[:coarse, :], inverse[:coarse, :1]
        )
        back = (0.5 * mm_t(back.astype(BF16), w_out[...])).astype(BF16)
        back = jnp.concatenate([back, back_local[coarse:, :]], axis=0)
        back_ref[...] = back
        first = mm(pick_goal[:FIRST, :], back) * slope[...].astype(F32)
        grad_first[...] = first.astype(BF16)

    @pl.when(number <= FIRST)
    def _():
        turn()
        far[...] = mm(sum_rim[rim:, :FIRST], grad_first[...]).astype(BF16)
        near[...] = mm(sum_rim[:rim, :FIRST], grad_first[...]).astype(BF16)

    @pl.when(number > FIRST)
    def _():
        turn()
        grad[:FIRST, :] = grad_first[...]
        for c in pieces_of(half.shape[0], FIRST)[1:]:
            grad[c, :] = edge_grad(c, pick_goal, back_ref[...], half)
        far[...] = mm(sum_rim[rim:, :], grad[...]).astype(BF16)
        near[...] = mm(sum_rim[:rim, :], grad[...]).astype(BF16)


def edge_grad(c, pick_goal, back, half):
    return (mm(pick_goal[c, :], back) * half_silu(half[c, :])[1]).astype(BF16)


def own_back_kernel(
    grad_first,
    back,
    half,
    pick_goal,
    live_send,
    live_goal,
    grad_local,
    updated16,
    w_source,
    w_dest,
    halo,
    near,
    mesh_grad,
    own,
    sum_far,
    grad,
):
    coarse = updated16.shape[0]
    rows = grad_local.shape[0]
    grad[:FIRST, :] = grad_first[...]
    for c in pieces_of(half.shape[0], FIRST)[1:]:
        grad[c, :] = edge_grad(c, pick_goal, back[...], half)
    dest = mm(spread(live_goal[...], 0, rows), grad[...]).astype(BF16)
    updated = jnp.concatenate([updated16[...], grad_local[coarse:, :]], axis=0)
    mesh_grad[...] = (updated + mm_t(dest, w_dest[...])).astype(BF16)
    source = mm(spread(live_send[...], 0, own.shape[0]), grad[...]).astype(BF16)
    rows_near, rows_far = halves(as_row(halo), even_patch())
    sum_far[...] = spread(rows_far, 0, own.shape[0])
    back_near = mm_t(near[...], w_source[...]).astype(BF16)
    own[...] = mm_t(source, w_source[...]) + mm(spread(rows_near, 0, own.shape[0]), back_near)


def finish_kernel(own, sum_far, far, w_source, out_hbm, out, sems):
    projected = mm_t(far[...], w_source[...]).astype(BF16)
    copies = []
    for i, c in enumerate(pieces_of(own.shape[0], own.shape[0] // 8)):
        out[c, :] = (own[c, :] + mm(sum_far[c, :], projected)).astype(BF16)
        copies.append(pltpu.make_async_copy(out.at[c], out_hbm.at[c], sems.at[i]))
        copies[-1].start()
    for copy in copies:
        copy.wait()


SMEM = pl.BlockSpec(memory_space=pltpu.SMEM)
HBM = pl.BlockSpec(memory_space=pltpu.HBM)
VMEM = pl.BlockSpec(memory_space=pltpu.VMEM)
MICROSECOND = 1 << 30


def call(kernel, arrays, outs, cost, raw=0, scalars=0, scratch=(), out_specs=None, aliases=None):
    return pl.pallas_call(
        kernel,
        out_shape=[jax.ShapeDtypeStruct(s, d) for s, d in outs],
        in_specs=[HBM] * raw + [SMEM] * scalars + [VMEM] * (len(arrays) - raw - scalars),
        out_specs=out_specs or [VMEM] * len(outs),
        input_output_aliases=aliases or {},
        scratch_shapes=list(scratch),
        compiler_params=pltpu.CompilerParams(vmem_limit_bytes=24 << 20),
        cost_estimate=pl.CostEstimate(
            flops=int(cost * MICROSECOND), bytes_accessed=1 << 20, transcendentals=0
        ),
    )(*(pltpu.with_memory_space_constraint(x, pltpu.HBM) for x in arrays[:raw]), *arrays[raw:])


def swap_halo(near, far, n):
    far_pairs = [(i, (i + 1) % n if i % 2 else (i - 1) % n) for i in range(n)]
    far = lax.ppermute(far, "patch", far_pairs)
    near = lax.ppermute(near, "patch", [(i, i ^ 1) for i in range(n)])
    return near, far


def exchange(pieces, plan):
    out = []
    for piece, goals in zip(pieces, plan):
        out.append(lax.ppermute(piece, "group", list(enumerate(goals))))
    return out


def on_device(
    grid_latent,
    mesh_latent,
    cotangent,
    halo_rows,
    encoder_sender,
    encoder_target,
    encoder_count,
    process_sender,
    process_target,
    process_count,
    encoder_source,
    encoder_dest,
    encoder_output,
    encoder_gain,
    process_source,
    process_dest,
    process_output,
    process_gain,
):
    patches, groups = lax.axis_size("patch"), lax.axis_size("group")
    grid_rows, width = grid_latent.shape
    mesh_rows = mesh_latent.shape[0]
    hidden_size = encoder_source.shape[1]
    coarse = mesh_rows // 16
    rim = halo_rows.shape[0] // 2
    slots, slots2 = encoder_sender.shape[0], process_sender.shape[0]

    row_form, row_form2 = ((1, slots), I32), ((1, slots2), I32)
    column_form2 = ((slots2, LANES), I16)
    remote = coarse * (groups - 1)
    near, far, grid = call(
        select_kernel,
        [halo_rows, grid_latent],
        [((rim, width), BF16)] * 2 + [((grid_rows, width), BF16)],
        4,
        raw=2,
        scratch=[pltpu.VMEM(halo_rows.shape, I32), pltpu.SemaphoreType.DMA((2,))],
    )
    near, far = swap_halo(near, far, patches)
    (
        early,
        part,
        hidden,
        summed16,
        live_send,
        live_goal,
        live_send2,
        live_goal2,
        send_col2,
        goal_col2,
        pick_rim,
        pick_goal,
    ) = call(
        functools.partial(encode_local_kernel, groups, coarse),
        [
            jnp.concatenate([encoder_count, process_count]),
            encoder_sender,
            encoder_target,
            process_sender,
            process_target,
            grid,
            mesh_latent,
            encoder_source,
            encoder_dest,
        ],
        [((2, LANES), I32), ((slots, hidden_size), F32), ((slots, hidden_size), BF16)]
        + [((coarse, hidden_size), F32), row_form, row_form, row_form2, row_form2]
        + [column_form2, column_form2]
        + [((slots, 2 * rim), BF16), ((slots, mesh_rows), BF16)],
        2,
        scalars=1,
    )
    half, hidden, updated16 = call(
        functools.partial(encode_halo_kernel, coarse),
        [
            early,
            near,
            far,
            part,
            hidden,
            summed16,
            pick_rim,
            live_goal,
            mesh_latent,
            encoder_source,
            encoder_output,
            encoder_gain,
        ],
        [((slots, hidden_size), F32), ((slots, hidden_size), BF16), ((coarse, width), BF16)],
        2,
        aliases={3: 0, 4: 1},
    )
    shifts = exchange([updated16] * (groups - 1), plans(groups)[0])
    (
        normed,
        inverse,
        part2,
        pick_goal2,
        pick_coarse,
        sum_goal2,
        sum_coarse,
        centre2,
        summed2,
    ) = call(
        process_local_kernel,
        [
            hidden,
            live_goal,
            mesh_latent,
            send_col2,
            goal_col2,
            live_send2,
            live_goal2,
            cotangent,
            encoder_output,
            encoder_gain,
            process_gain,
            process_source,
            process_dest,
        ],
        [
            ((mesh_rows, width), F32),
            ((mesh_rows, LANES), F32),
            ((slots2, hidden_size), F32),
            ((slots2, mesh_rows), BF16),
            ((slots2, ceil_to(remote, LANES)), BF16),
            ((mesh_rows, slots2), BF16),
            ((remote, slots2), BF16),
            ((mesh_rows, width), F32),
            ((mesh_rows, hidden_size), F32),
        ],
        2,
        scratch=[pltpu.VMEM((slots2, hidden_size), BF16)],
    )
    half2, grad_first2, back2, *pieces = call(
        functools.partial(process_kernel, coarse),
        [
            early,
            part2,
            pick_goal2,
            pick_coarse,
            sum_goal2,
            sum_coarse,
            centre2,
            summed2,
            process_source,
            process_output,
            *shifts,
        ],
        [((slots2, hidden_size), F32), ((FIRST, hidden_size), BF16)]
        + [((mesh_rows, hidden_size), BF16)]
        + [((coarse, hidden_size), BF16)] * (groups - 1),
        2,
        scratch=[
            pltpu.VMEM((slots2, hidden_size), BF16),
            pltpu.VMEM((slots2, hidden_size), BF16),
            pltpu.VMEM((slots2, hidden_size), BF16),
        ],
        aliases={1: 0},
    )
    pieces = exchange(pieces, plans(groups)[1])
    grad_local, back, slope, sum_rim = call(
        functools.partial(process_back_kernel, grid_rows),
        [
            half,
            half2,
            grad_first2,
            back2,
            pick_goal2,
            live_send,
            live_send2,
            sum_goal2,
            cotangent,
            process_source,
            process_dest,
            encoder_output,
            encoder_gain,
            normed,
            inverse,
        ],
        [
            ((mesh_rows, width), F32),
            ((mesh_rows, hidden_size), BF16),
            ((FIRST, hidden_size), BF16),
            ((2 * rim, slots), BF16),
        ],
        2,
        scratch=[pltpu.VMEM((slots2, hidden_size), BF16)],
    )
    back, grad_first, near, far, grad16 = call(
        encode_back_kernel,
        [
            early,
            grad_local,
            back,
            normed,
            inverse,
            half,
            slope,
            pick_goal,
            sum_rim,
            encoder_gain,
            process_source,
            encoder_output,
            *pieces,
        ],
        [((mesh_rows, hidden_size), BF16), ((FIRST, hidden_size), BF16)]
        + [((rim, hidden_size), BF16)] * 2
        + [((coarse, width), F32)],
        2,
        scratch=[pltpu.VMEM((slots, hidden_size), BF16)],
    )
    near, far = swap_halo(near, far, patches)
    mesh_grad, own, sum_far = call(
        own_back_kernel,
        [
            grad_first,
            back,
            half,
            pick_goal,
            live_send,
            live_goal,
            grad_local,
            grad16,
            encoder_source,
            encoder_dest,
            halo_rows,
            near,
        ],
        [((mesh_rows, width), BF16), ((grid_rows, width), F32), ((grid_rows, rim), BF16)],
        2,
        scratch=[pltpu.VMEM((slots, hidden_size), BF16)],
    )
    (grid_grad,) = call(
        finish_kernel,
        [own, sum_far, far, encoder_source],
        [((grid_rows, width), BF16)],
        2,
        scratch=[pltpu.VMEM((grid_rows, width), BF16), pltpu.SemaphoreType.DMA((8,))],
        out_specs=[HBM],
    )
    return grid_grad, mesh_grad


def solution(mesh):
    rows, flat, whole = P(("patch", "group"), None), P(("patch", "group")), P()
    return jax.shard_map(
        on_device,
        mesh=mesh,
        in_specs=(rows,) * 3 + (flat,) * 7 + (whole,) * 8,
        out_specs=(rows, rows),
        check_vma=False,
    )
```

```python
import functools

import jax
import jax.numpy as jnp
from jax import lax
from jax.experimental import pallas as pl
from jax.experimental.pallas import tpu as pltpu
from jax.sharding import PartitionSpec as P


EPSILON = 1e-05
LANES = 128
FIRST = 256
F32 = jnp.float32
BF16 = jnp.bfloat16
I32 = jnp.int32
I16 = jnp.int16


def mm(a, b):
    return jnp.dot(a, b, preferred_element_type=F32)


def mm_t(a, b):
    return lax.dot_general(a, b, (((1,), (1,)), ((), ())), preferred_element_type=F32)


def half_silu(u):
    t = jnp.tanh(u)
    a = 1.0 + t
    value = u * a
    return value, a + value * (1.0 - t)


def ceil_to(n, k):
    return (n + k - 1) // k * k


def to_columns(*rows):
    packed = rows[0] if len(rows) == 1 else rows[0] + rows[1] * 4096
    parts = []
    for i in range(0, packed.shape[1], LANES):
        parts.append(jnp.broadcast_to(packed[:, i : i + LANES], (LANES, LANES)).T)
    columns = jnp.concatenate(parts, axis=0)
    if len(rows) == 1:
        return columns.astype(I16)
    low = jnp.bitwise_and(columns, 4095).astype(I16)
    return low, lax.shift_right_logical(columns, 12).astype(I16)


def one_hot(equal):
    return jnp.where(equal, jnp.ones((), BF16), jnp.zeros((), BF16))


def pick(columns, first, width):
    lane = lax.broadcasted_iota(I32, columns.shape, 1)
    parts = [one_hot(columns == (lane + (first + i)).astype(I16)) for i in range(0, width, LANES)]
    return parts[0] if len(parts) == 1 else jnp.concatenate(parts, axis=1)


def spread(row, first, height):
    shape = (height, row.shape[1])
    number = lax.broadcasted_iota(I32, shape, 0) + first
    return one_hot(jnp.broadcast_to(row, shape).astype(I16) == number.astype(I16))


def only_live(rows, count):
    slot = lax.broadcasted_iota(I32, rows.shape, 1)
    return jnp.where(slot < count, rows, -1)


def normalise(values):
    center = values - jnp.mean(values, axis=-1, keepdims=True)
    inverse = lax.rsqrt(jnp.mean(center * center, axis=-1, keepdims=True) + EPSILON)
    return center * inverse, inverse


def centred(values):
    return values - jnp.mean(values, axis=-1, keepdims=True)


def normalise_back(centre, normed, inverse):
    return inverse * (centre - normed * jnp.mean(centre * normed, axis=-1, keepdims=True))


def halves(rows, even):
    half = rows.shape[1] // 2
    first, second = rows[:, :half], rows[:, half:]
    return jnp.where(even, second, first), jnp.where(even, first, second)


def plans(n):
    masks = [tuple(i ^ k for i in range(n)) for k in range(n - 1, 0, -1)]
    if n == 4:
        return [(1, 3, 0, 2), (3, 2, 1, 0), (2, 0, 3, 1)], masks
    return masks, masks


def look_up(table, index):
    value = jnp.int32(table[0])
    for i, entry in enumerate(table[1:], 1):
        value = jnp.where(index == i, jnp.int32(entry), value)
    return value


def coarse_slots(sender, mesh_rows, coarse, owners):
    offset = sender - mesh_rows
    owner = offset // coarse
    moved = offset - owner * coarse
    for k, other in enumerate(owners):
        moved = moved + jnp.where(owner == other, mesh_rows + k * coarse, 0)
    return jnp.where(offset < 0, sender, moved)


def even_patch():
    return lax.rem(lax.axis_index("patch"), 2) == 0


def as_row(ref):
    return ref[...].reshape(1, ref.shape[0])


def select_kernel(halo_hbm, grid_hbm, near, far, table, halo, sems):
    copies = [
        pltpu.make_async_copy(halo_hbm, halo, sems.at[0]),
        pltpu.make_async_copy(grid_hbm, table, sems.at[1]),
    ]
    for copy in copies:
        copy.start()
    copies[0].wait()
    rows_near, rows_far = halves(as_row(halo), even_patch())
    pick_near = pick(to_columns(rows_near), 0, table.shape[0])
    pick_far = pick(to_columns(rows_far), 0, table.shape[0])
    copies[1].wait()
    near[...] = mm(pick_near, table[...]).astype(BF16)
    far[...] = mm(pick_far, table[...]).astype(BF16)


def rim_starts(grid_rows, rim):
    even = even_patch()
    return (
        jnp.where(even, grid_rows + rim, grid_rows),
        jnp.where(even, grid_rows, grid_rows + rim),
    )


def arrange(first, rows):
    slots = first.shape[1]
    groups = slots // LANES
    flags = [first[:, i * LANES : (i + 1) * LANES] for i in range(groups)]
    spare = ceil_to(groups, 8) - groups
    stack = jnp.concatenate(flags + [jnp.zeros((spare, LANES), F32)] * bool(spare), axis=0)
    shape = (LANES, LANES)
    before = lax.broadcasted_iota(I32, shape, 0) <= lax.broadcasted_iota(I32, shape, 1)
    sums = mm(stack.astype(BF16), jnp.where(before, 1.0, 0.0).astype(BF16))
    total = jnp.zeros((1, 1), F32)
    counted = []
    for i in range(groups):
        counted.append(sums[i : i + 1, :] + total)
        total = total + sums[i : i + 1, LANES - 1 :]
    counted = jnp.concatenate(counted, axis=1)
    slot = lax.broadcasted_iota(I32, first.shape, 1).astype(F32)
    place = jnp.where(first > 0.0, counted - 1.0, total + slot - counted)
    order = spread(place.astype(I32), 0, slots)
    digits = []
    for row in rows:
        digits += [lax.shift_right_logical(row, 7), jnp.bitwise_and(row, 127)]
    digits = [d.astype(F32) for d in digits]
    spare = ceil_to(len(digits), 8) - len(digits)
    digits = jnp.concatenate(digits + [jnp.zeros((spare, slots), F32)] * bool(spare), axis=0)
    moved = mm_t(digits.astype(BF16), order).astype(I32)
    moved = [moved[2 * i : 2 * i + 1, :] * 128 + moved[2 * i + 1 : 2 * i + 2, :] for i in range(len(rows))]
    return total, moved


def flagged(condition, count):
    slot = lax.broadcasted_iota(I32, condition.shape, 1)
    return jnp.where(condition & (slot < count), 1.0, 0.0)


def encode_local_kernel(
    groups,
    coarse,
    counts,
    sender,
    target,
    sender2,
    target2,
    grid,
    mesh,
    w_source,
    w_dest,
    near,
    early,
    near_source,
    part,
    hidden,
    summed16,
    live_send,
    live_goal,
    live_send2,
    live_goal2,
    send_col2,
    goal_col2,
    pick_rim,
    pick_goal,
):
    count, count2 = counts[0], counts[1]
    rows, grid_rows = mesh.shape[0], grid.shape[0]
    rim = pick_rim.shape[1] // 2
    source = (0.5 * mm(grid[...], w_source[...])).astype(BF16)
    dest = (0.5 * mm(mesh[...], w_dest[...])).astype(BF16)
    near_source[...] = (0.5 * mm(near[...], w_source[...])).astype(BF16)
    me = lax.axis_index("group")
    gather, reduce = plans(groups)
    sources = [look_up([p.index(i) for i in range(groups)], me) for p in gather]
    goals = [look_up(p, me) for p in reduce]
    send, send2 = as_row(sender), as_row(sender2)
    back2 = coarse_slots(send2, rows, coarse, goals)
    send2 = coarse_slots(send2, rows, coarse, sources)
    total, (send, goal) = arrange(flagged(send >= grid_rows, count), [send, as_row(target)])
    moved = [send2, as_row(target2), back2]
    total2, (send2, goal2, back2) = arrange(flagged(send2 >= rows, count2), moved)
    early[:1, :] = jnp.broadcast_to(total, (1, LANES)).astype(I32)
    early[1:, :] = jnp.broadcast_to(total2, (1, LANES)).astype(I32)
    send_col, goal_col = to_columns(send, goal)
    send_col2[...], goal_col2[...] = to_columns(send2, goal2)
    near_first, far_first = rim_starts(grid_rows, rim)
    pick_rim[:, :rim] = pick(send_col, near_first, rim)
    pick_rim[:, rim:] = pick(send_col, far_first, rim)
    pick_goal[...] = pick(goal_col, 0, rows)
    live_send[...] = only_live(send, count)
    live_goal[...] = only_live(goal, count)
    live_send2[...] = only_live(back2, count2)
    live_goal2[...] = only_live(goal2, count2)
    for c in pieces_of(part.shape[0], FIRST):
        u = mm(pick(send_col[c, :], 0, grid_rows), source) + mm(pick_goal[c, :], dest)
        part[c, :] = u
        if c.start:
            hidden[c, :] = (u + u * jnp.tanh(u)).astype(BF16)
    summed16[...] = mm(spread(live_goal[:, FIRST:], 0, coarse), hidden[FIRST:, :])


def pieces_of(n, size):
    return [slice(i, min(i + size, n)) for i in range(0, n, size)]


def encode_halo_kernel(
    coarse,
    early,
    near_source,
    far,
    part,
    hidden_local,
    summed16,
    pick_rim,
    live_goal,
    mesh,
    w_source,
    w_out,
    gain,
    half,
    hidden,
    updated16,
):
    number = jnp.max(early[:1, :])
    far_source = (0.5 * mm(far[...], w_source[...])).astype(BF16)
    source = jnp.concatenate([near_source[...], far_source], axis=0)

    def edges(c):
        u = part[c, :] + mm(pick_rim[c, :], source)
        half[c, :] = u
        hidden[c, :] = (u + u * jnp.tanh(u)).astype(BF16)

    def finish(summed):
        normed, _ = normalise(mm(summed.astype(BF16), w_out[...]))
        updated16[...] = (mesh[:coarse, :].astype(F32) + normed * as_row(gain)).astype(BF16)

    def first_edges():
        for c in pieces_of(FIRST, 128):
            edges(c)

    @pl.when(number <= FIRST)
    def _():
        first_edges()
        goal = spread(live_goal[:, :FIRST], 0, coarse)
        finish(summed16[...] + mm(goal, hidden[:FIRST, :]))

    @pl.when(number > FIRST)
    def _():
        first_edges()
        for c in pieces_of(part.shape[0], FIRST)[1:]:
            edges(c)
        finish(mm(spread(live_goal[...], 0, coarse), hidden[...]))


def process_local_kernel(
    hidden,
    live_goal,
    mesh,
    send_col2,
    goal_col2,
    live_send2,
    live_goal2,
    cotangent,
    w_out,
    gain,
    gain2,
    w_source,
    w_dest,
    normed_ref,
    inverse_ref,
    part,
    pick_goal2,
    pick_coarse,
    sum_goal2,
    sum_coarse,
    centre2,
    summed2,
    hidden2,
):
    rows = mesh.shape[0]
    summed = mm(spread(live_goal[...], 0, rows), hidden[...]).astype(BF16)
    normed, inverse = normalise(mm(summed, w_out[...]))
    normed_ref[...] = normed
    inverse_ref[...] = jnp.broadcast_to(inverse, inverse_ref.shape)
    updated = (mesh[...].astype(F32) + normed * as_row(gain)).astype(BF16)
    source = (0.5 * mm(updated, w_source[...])).astype(BF16)
    dest = (0.5 * mm(updated, w_dest[...])).astype(BF16)
    pick_goal2[...] = pick(goal_col2[...], 0, rows)
    pick_coarse[...] = pick(send_col2[...], rows, pick_coarse.shape[1])
    sum_goal2[...] = spread(live_goal2[...], 0, rows)
    sum_coarse[...] = spread(live_send2[...], rows, sum_coarse.shape[0])
    centre2[...] = centred(cotangent[...].astype(F32) * as_row(gain2))
    for c in pieces_of(part.shape[0], FIRST):
        u = mm(pick(send_col2[c, :], 0, rows), source) + mm(pick_goal2[c, :], dest)
        part[c, :] = u
        if c.start:
            hidden2[c, :] = (u + u * jnp.tanh(u)).astype(BF16)
    summed2[...] = mm(sum_goal2[:, FIRST:], hidden2[FIRST:, :])


def process_kernel(
    coarse,
    early,
    part,
    pick_goal2,
    pick_coarse,
    sum_goal2,
    sum_coarse,
    centre2,
    summed2,
    w_source,
    w_out,
    *refs,
):
    peers = sum_coarse.shape[0] // coarse
    received, (half, grad_first, back_ref) = refs[:peers], refs[peers : peers + 3]
    returned, (hidden, slope, grad, gathered, turned) = refs[peers + 3 : -5], refs[-5:]
    number = jnp.max(early[1:, :])
    rows = jnp.concatenate([r[...] for r in received], axis=0)
    source = (0.5 * mm(rows, w_source[...])).astype(BF16)
    spare = pick_coarse.shape[1] - source.shape[0]
    if spare:
        source = jnp.concatenate([source, jnp.zeros((spare, source.shape[1]), BF16)], axis=0)

    def edges(c):
        u = part[c, :] + mm(pick_coarse[c, :], source)
        if c.start >= FIRST:
            half[c, :] = u
        value, double = half_silu(u)
        hidden[c, :] = value.astype(BF16)
        slope[c, :] = double.astype(BF16)

    def turn(summed):
        gathered[...] = mm(summed.astype(BF16), w_out[...])
        for r in pieces_of(gathered.shape[0], 32):
            center = centred(gathered[r, :])
            inverse = lax.rsqrt(jnp.mean(center * center, axis=-1, keepdims=True) + EPSILON)
            share = jnp.mean(center * centre2[r, :], axis=-1, keepdims=True)
            share = share * inverse * inverse
            turned[r, :] = (inverse * (centre2[r, :] - center * share)).astype(BF16)
        back = (0.5 * mm_t(turned[...], w_out[...])).astype(BF16)
        back_ref[...] = back
        grad_first[...] = (mm(pick_goal2[:FIRST, :], back) * slope[:FIRST, :].astype(F32)).astype(BF16)
        return back

    def send(sums):
        for i, out in enumerate(returned):
            out[...] = sums[i * coarse : (i + 1) * coarse].astype(BF16)

    def first_edges():
        for c in pieces_of(FIRST, 128):
            edges(c)

    @pl.when(number <= FIRST)
    def _():
        first_edges()
        turn(summed2[...] + mm(sum_goal2[:, :FIRST], hidden[:FIRST, :]))
        send(mm(sum_coarse[:, :FIRST], grad_first[...]))

    @pl.when(number > FIRST)
    def _():
        first_edges()
        later = pieces_of(part.shape[0], FIRST)[1:]
        for c in later:
            edges(c)
        back = turn(mm(sum_goal2[...], hidden[...]))
        grad[:FIRST, :] = grad_first[...]
        for c in later:
            grad[c, :] = (mm(pick_goal2[c, :], back) * slope[c, :].astype(F32)).astype(BF16)
        send(mm(sum_coarse[...], grad[...]))


def process_back_kernel(
    grid_rows,
    half,
    half2,
    grad_first,
    back2,
    pick_goal2,
    live_send,
    live_send2,
    sum_goal2,
    cotangent,
    w_source,
    w_dest,
    w_out,
    gain,
    normed,
    inverse,
    grad_local,
    back_ref,
    slope,
    sum_rim,
    grad,
):
    rows = cotangent.shape[0]
    rim = sum_rim.shape[0] // 2
    grad[:FIRST, :] = grad_first[...]
    for c in pieces_of(half2.shape[0], FIRST)[1:]:
        double = half_silu(half2[c, :])[1]
        grad[c, :] = (mm(pick_goal2[c, :], back2[...]) * double).astype(BF16)
    table = mm(spread(live_send2[...], 0, rows), grad[...]).astype(BF16)
    dest = mm(sum_goal2[...], grad[...]).astype(BF16)
    local = cotangent[...].astype(F32) + mm_t(table, w_source[...]) + mm_t(dest, w_dest[...])
    grad_local[...] = local
    back = normalise_back(centred(local * as_row(gain)), normed[...], inverse[:, :1])
    back_ref[...] = (0.5 * mm_t(back.astype(BF16), w_out[...])).astype(BF16)
    near_first, far_first = rim_starts(grid_rows, rim)
    sum_rim[:rim, :] = spread(live_send[...], near_first, rim)
    sum_rim[rim:, :] = spread(live_send[...], far_first, rim)
    slope[...] = half_silu(half[:FIRST, :])[1].astype(BF16)


def encode_back_kernel(
    early,
    grad_local,
    back_local,
    normed,
    inverse,
    half,
    slope,
    pick_goal,
    sum_rim,
    gain,
    w_source2,
    w_out,
    *refs,
):
    received, (back_ref, grad_first, near, far, updated16, grad) = refs[:-6], refs[-6:]
    coarse = updated16.shape[0]
    rim = near.shape[0]
    number = jnp.max(early[:1, :])
    total = received[0][...].astype(F32)
    for r in received[1:]:
        total = total + r[...].astype(F32)
    updated = grad_local[:coarse, :] + mm_t(total.astype(BF16), w_source2[...])
    updated16[...] = updated

    def turn():
        back = normalise_back(
            centred(updated * as_row(gain)), normed[:coarse, :], inverse[:coarse, :1]
        )
        back = (0.5 * mm_t(back.astype(BF16), w_out[...])).astype(BF16)
        back = jnp.concatenate([back, back_local[coarse:, :]], axis=0)
        back_ref[...] = back
        first = mm(pick_goal[:FIRST, :], back) * slope[...].astype(F32)
        grad_first[...] = first.astype(BF16)

    @pl.when(number <= FIRST)
    def _():
        turn()
        far[...] = mm(sum_rim[rim:, :FIRST], grad_first[...]).astype(BF16)
        near[...] = mm(sum_rim[:rim, :FIRST], grad_first[...]).astype(BF16)

    @pl.when(number > FIRST)
    def _():
        turn()
        grad[:FIRST, :] = grad_first[...]
        for c in pieces_of(half.shape[0], FIRST)[1:]:
            grad[c, :] = edge_grad(c, pick_goal, back_ref[...], half)
        far[...] = mm(sum_rim[rim:, :], grad[...]).astype(BF16)
        near[...] = mm(sum_rim[:rim, :], grad[...]).astype(BF16)


def edge_grad(c, pick_goal, back, half):
    return (mm(pick_goal[c, :], back) * half_silu(half[c, :])[1]).astype(BF16)


def own_back_kernel(
    grad_first,
    back,
    half,
    pick_goal,
    live_send,
    live_goal,
    grad_local,
    updated16,
    w_source,
    w_dest,
    halo,
    near,
    mesh_grad,
    own,
    sum_far,
    grad,
):
    coarse = updated16.shape[0]
    rows = grad_local.shape[0]
    grad[:FIRST, :] = grad_first[...]
    for c in pieces_of(half.shape[0], FIRST)[1:]:
        grad[c, :] = edge_grad(c, pick_goal, back[...], half)
    dest = mm(spread(live_goal[...], 0, rows), grad[...]).astype(BF16)
    updated = jnp.concatenate([updated16[...], grad_local[coarse:, :]], axis=0)
    mesh_grad[...] = (updated + mm_t(dest, w_dest[...])).astype(BF16)
    source = mm(spread(live_send[...], 0, own.shape[0]), grad[...]).astype(BF16)
    rows_near, rows_far = halves(as_row(halo), even_patch())
    sum_far[...] = spread(rows_far, 0, own.shape[0])
    back_near = mm_t(near[...], w_source[...]).astype(BF16)
    own[...] = mm_t(source, w_source[...]) + mm(spread(rows_near, 0, own.shape[0]), back_near)


def finish_kernel(own, sum_far, far, w_source, out_hbm, out, sems):
    projected = mm_t(far[...], w_source[...]).astype(BF16)
    copies = []
    for i, c in enumerate(pieces_of(own.shape[0], own.shape[0] // 8)):
        out[c, :] = (own[c, :] + mm(sum_far[c, :], projected)).astype(BF16)
        copies.append(pltpu.make_async_copy(out.at[c], out_hbm.at[c], sems.at[i]))
        copies[-1].start()
    for copy in copies:
        copy.wait()


SMEM = pl.BlockSpec(memory_space=pltpu.SMEM)
HBM = pl.BlockSpec(memory_space=pltpu.HBM)
VMEM = pl.BlockSpec(memory_space=pltpu.VMEM)
MICROSECOND = 1 << 30


def call(kernel, arrays, outs, cost, raw=0, scalars=0, scratch=(), out_specs=None, aliases=None):
    return pl.pallas_call(
        kernel,
        out_shape=[jax.ShapeDtypeStruct(s, d) for s, d in outs],
        in_specs=[HBM] * raw + [SMEM] * scalars + [VMEM] * (len(arrays) - raw - scalars),
        out_specs=out_specs or [VMEM] * len(outs),
        input_output_aliases=aliases or {},
        scratch_shapes=list(scratch),
        compiler_params=pltpu.CompilerParams(vmem_limit_bytes=24 << 20),
        cost_estimate=pl.CostEstimate(
            flops=int(cost * MICROSECOND), bytes_accessed=1 << 20, transcendentals=0
        ),
    )(*(pltpu.with_memory_space_constraint(x, pltpu.HBM) for x in arrays[:raw]), *arrays[raw:])


def swap_halo(near, far, n):
    far_pairs = [(i, (i + 1) % n if i % 2 else (i - 1) % n) for i in range(n)]
    far = lax.ppermute(far, "patch", far_pairs)
    near = lax.ppermute(near, "patch", [(i, i ^ 1) for i in range(n)])
    return near, far


def exchange(pieces, plan):
    out = []
    for piece, goals in zip(pieces, plan):
        out.append(lax.ppermute(piece, "group", list(enumerate(goals))))
    return out


def on_device(
    grid_latent,
    mesh_latent,
    cotangent,
    halo_rows,
    encoder_sender,
    encoder_target,
    encoder_count,
    process_sender,
    process_target,
    process_count,
    encoder_source,
    encoder_dest,
    encoder_output,
    encoder_gain,
    process_source,
    process_dest,
    process_output,
    process_gain,
):
    patches, groups = lax.axis_size("patch"), lax.axis_size("group")
    grid_rows, width = grid_latent.shape
    mesh_rows = mesh_latent.shape[0]
    hidden_size = encoder_source.shape[1]
    coarse = mesh_rows // 16
    rim = halo_rows.shape[0] // 2
    slots, slots2 = encoder_sender.shape[0], process_sender.shape[0]

    row_form, row_form2 = ((1, slots), I32), ((1, slots2), I32)
    column_form2 = ((slots2, LANES), I16)
    remote = coarse * (groups - 1)
    near, far, grid = call(
        select_kernel,
        [halo_rows, grid_latent],
        [((rim, width), BF16)] * 2 + [((grid_rows, width), BF16)],
        4,
        raw=2,
        scratch=[pltpu.VMEM(halo_rows.shape, I32), pltpu.SemaphoreType.DMA((2,))],
    )
    near, far = swap_halo(near, far, patches)
    (
        early,
        near_source,
        part,
        hidden,
        summed16,
        live_send,
        live_goal,
        live_send2,
        live_goal2,
        send_col2,
        goal_col2,
        pick_rim,
        pick_goal,
    ) = call(
        functools.partial(encode_local_kernel, groups, coarse),
        [
            jnp.concatenate([encoder_count, process_count]),
            encoder_sender,
            encoder_target,
            process_sender,
            process_target,
            grid,
            mesh_latent,
            encoder_source,
            encoder_dest,
            near,
        ],
        [((2, LANES), I32), ((rim, hidden_size), BF16), ((slots, hidden_size), F32), ((slots, hidden_size), BF16)]
        + [((coarse, hidden_size), F32), row_form, row_form, row_form2, row_form2]
        + [column_form2, column_form2]
        + [((slots, 2 * rim), BF16), ((slots, mesh_rows), BF16)],
        2,
        scalars=1,
    )
    half, hidden, updated16 = call(
        functools.partial(encode_halo_kernel, coarse),
        [
            early,
            near_source,
            far,
            part,
            hidden,
            summed16,
            pick_rim,
            live_goal,
            mesh_latent,
            encoder_source,
            encoder_output,
            encoder_gain,
        ],
        [((slots, hidden_size), F32), ((slots, hidden_size), BF16), ((coarse, width), BF16)],
        2,
        aliases={3: 0, 4: 1},
    )
    shifts = exchange([updated16] * (groups - 1), plans(groups)[0])
    (
        normed,
        inverse,
        part2,
        pick_goal2,
        pick_coarse,
        sum_goal2,
        sum_coarse,
        centre2,
        summed2,
    ) = call(
        process_local_kernel,
        [
            hidden,
            live_goal,
            mesh_latent,
            send_col2,
            goal_col2,
            live_send2,
            live_goal2,
            cotangent,
            encoder_output,
            encoder_gain,
            process_gain,
            process_source,
            process_dest,
        ],
        [
            ((mesh_rows, width), F32),
            ((mesh_rows, LANES), F32),
            ((slots2, hidden_size), F32),
            ((slots2, mesh_rows), BF16),
            ((slots2, ceil_to(remote, LANES)), BF16),
            ((mesh_rows, slots2), BF16),
            ((remote, slots2), BF16),
            ((mesh_rows, width), F32),
            ((mesh_rows, hidden_size), F32),
        ],
        2,
        scratch=[pltpu.VMEM((slots2, hidden_size), BF16)],
    )
    half2, grad_first2, back2, *pieces = call(
        functools.partial(process_kernel, coarse),
        [
            early,
            part2,
            pick_goal2,
            pick_coarse,
            sum_goal2,
            sum_coarse,
            centre2,
            summed2,
            process_source,
            process_output,
            *shifts,
        ],
        [((slots2, hidden_size), F32), ((FIRST, hidden_size), BF16)]
        + [((mesh_rows, hidden_size), BF16)]
        + [((coarse, hidden_size), BF16)] * (groups - 1),
        2,
        scratch=[
            pltpu.VMEM((slots2, hidden_size), BF16),
            pltpu.VMEM((slots2, hidden_size), BF16),
            pltpu.VMEM((slots2, hidden_size), BF16),
            pltpu.VMEM((mesh_rows, width), F32),
            pltpu.VMEM((mesh_rows, width), BF16),
        ],
        aliases={1: 0},
    )
    pieces = exchange(pieces, plans(groups)[1])
    grad_local, back, slope, sum_rim = call(
        functools.partial(process_back_kernel, grid_rows),
        [
            half,
            half2,
            grad_first2,
            back2,
            pick_goal2,
            live_send,
            live_send2,
            sum_goal2,
            cotangent,
            process_source,
            process_dest,
            encoder_output,
            encoder_gain,
            normed,
            inverse,
        ],
        [
            ((mesh_rows, width), F32),
            ((mesh_rows, hidden_size), BF16),
            ((FIRST, hidden_size), BF16),
            ((2 * rim, slots), BF16),
        ],
        2,
        scratch=[pltpu.VMEM((slots2, hidden_size), BF16)],
    )
    back, grad_first, near, far, grad16 = call(
        encode_back_kernel,
        [
            early,
            grad_local,
            back,
            normed,
            inverse,
            half,
            slope,
            pick_goal,
            sum_rim,
            encoder_gain,
            process_source,
            encoder_output,
            *pieces,
        ],
        [((mesh_rows, hidden_size), BF16), ((FIRST, hidden_size), BF16)]
        + [((rim, hidden_size), BF16)] * 2
        + [((coarse, width), F32)],
        2,
        scratch=[pltpu.VMEM((slots, hidden_size), BF16)],
    )
    near, far = swap_halo(near, far, patches)
    mesh_grad, own, sum_far = call(
        own_back_kernel,
        [
            grad_first,
            back,
            half,
            pick_goal,
            live_send,
            live_goal,
            grad_local,
            grad16,
            encoder_source,
            encoder_dest,
            halo_rows,
            near,
        ],
        [((mesh_rows, width), BF16), ((grid_rows, width), F32), ((grid_rows, rim), BF16)],
        2,
        scratch=[pltpu.VMEM((slots, hidden_size), BF16)],
    )
    (grid_grad,) = call(
        finish_kernel,
        [own, sum_far, far, encoder_source],
        [((grid_rows, width), BF16)],
        2,
        scratch=[pltpu.VMEM((grid_rows, width), BF16), pltpu.SemaphoreType.DMA((8,))],
        out_specs=[HBM],
    )
    return grid_grad, mesh_grad


def solution(mesh):
    rows, flat, whole = P(("patch", "group"), None), P(("patch", "group")), P()
    return jax.shard_map(
        on_device,
        mesh=mesh,
        in_specs=(rows,) * 3 + (flat,) * 7 + (whole,) * 8,
        out_specs=(rows, rows),
        check_vma=False,
    )
```

```python
import functools

import jax
import jax.numpy as jnp
from jax import lax
from jax.experimental import pallas as pl
from jax.experimental.pallas import tpu as pltpu
from jax.sharding import PartitionSpec as P


EPSILON = 1e-05
LANES = 128
FIRST = 256
FIRST2 = 128
F32 = jnp.float32
BF16 = jnp.bfloat16
I32 = jnp.int32
I16 = jnp.int16


def mm(a, b):
    return jnp.dot(a, b, preferred_element_type=F32)


def mm_t(a, b):
    return lax.dot_general(a, b, (((1,), (1,)), ((), ())), preferred_element_type=F32)


def half_silu(u):
    t = jnp.tanh(u)
    a = 1.0 + t
    value = u * a
    return value, a + value * (1.0 - t)


def ceil_to(n, k):
    return (n + k - 1) // k * k


def to_columns(*rows):
    packed = rows[0] if len(rows) == 1 else rows[0] + rows[1] * 4096
    parts = []
    for i in range(0, packed.shape[1], LANES):
        parts.append(jnp.broadcast_to(packed[:, i : i + LANES], (LANES, LANES)).T)
    columns = jnp.concatenate(parts, axis=0)
    if len(rows) == 1:
        return columns.astype(I16)
    low = jnp.bitwise_and(columns, 4095).astype(I16)
    return low, lax.shift_right_logical(columns, 12).astype(I16)


def one_hot(equal):
    return jnp.where(equal, jnp.ones((), BF16), jnp.zeros((), BF16))


def pick(columns, first, width):
    lane = lax.broadcasted_iota(I32, columns.shape, 1)
    parts = [one_hot(columns == (lane + (first + i)).astype(I16)) for i in range(0, width, LANES)]
    return parts[0] if len(parts) == 1 else jnp.concatenate(parts, axis=1)


def spread(row, first, height):
    shape = (height, row.shape[1])
    number = lax.broadcasted_iota(I32, shape, 0) + first
    return one_hot(jnp.broadcast_to(row, shape).astype(I16) == number.astype(I16))


def only_live(rows, count):
    slot = lax.broadcasted_iota(I32, rows.shape, 1)
    return jnp.where(slot < count, rows, -1)


def normalise(values):
    center = values - jnp.mean(values, axis=-1, keepdims=True)
    inverse = lax.rsqrt(jnp.mean(center * center, axis=-1, keepdims=True) + EPSILON)
    return center * inverse, inverse


def centred(values):
    return values - jnp.mean(values, axis=-1, keepdims=True)


def normalise_back(centre, normed, inverse):
    return inverse * (centre - normed * jnp.mean(centre * normed, axis=-1, keepdims=True))


def halves(rows, even):
    half = rows.shape[1] // 2
    first, second = rows[:, :half], rows[:, half:]
    return jnp.where(even, second, first), jnp.where(even, first, second)


def plans(n):
    masks = [tuple(i ^ k for i in range(n)) for k in range(n - 1, 0, -1)]
    if n == 4:
        return [(1, 3, 0, 2), (3, 2, 1, 0), (2, 0, 3, 1)], masks
    return masks, masks


def look_up(table, index):
    value = jnp.int32(table[0])
    for i, entry in enumerate(table[1:], 1):
        value = jnp.where(index == i, jnp.int32(entry), value)
    return value


def coarse_slots(sender, mesh_rows, coarse, owners):
    offset = sender - mesh_rows
    owner = offset // coarse
    moved = offset - owner * coarse
    for k, other in enumerate(owners):
        moved = moved + jnp.where(owner == other, mesh_rows + k * coarse, 0)
    return jnp.where(offset < 0, sender, moved)


def even_patch():
    return lax.rem(lax.axis_index("patch"), 2) == 0


def as_row(ref):
    return ref[...].reshape(1, ref.shape[0])


def select_kernel(halo_hbm, grid_hbm, near, far, table, halo, sems):
    copies = [
        pltpu.make_async_copy(halo_hbm, halo, sems.at[0]),
        pltpu.make_async_copy(grid_hbm, table, sems.at[1]),
    ]
    for copy in copies:
        copy.start()
    copies[0].wait()
    rows_near, rows_far = halves(as_row(halo), even_patch())
    pick_near = pick(to_columns(rows_near), 0, table.shape[0])
    pick_far = pick(to_columns(rows_far), 0, table.shape[0])
    copies[1].wait()
    near[...] = mm(pick_near, table[...]).astype(BF16)
    far[...] = mm(pick_far, table[...]).astype(BF16)


def rim_starts(grid_rows, rim):
    even = even_patch()
    return (
        jnp.where(even, grid_rows + rim, grid_rows),
        jnp.where(even, grid_rows, grid_rows + rim),
    )


def arrange(first, rows):
    slots = first.shape[1]
    groups = slots // LANES
    flags = [first[:, i * LANES : (i + 1) * LANES] for i in range(groups)]
    spare = ceil_to(groups, 8) - groups
    stack = jnp.concatenate(flags + [jnp.zeros((spare, LANES), F32)] * bool(spare), axis=0)
    shape = (LANES, LANES)
    before = lax.broadcasted_iota(I32, shape, 0) <= lax.broadcasted_iota(I32, shape, 1)
    sums = mm(stack.astype(BF16), jnp.where(before, 1.0, 0.0).astype(BF16))
    total = jnp.zeros((1, 1), F32)
    counted = []
    for i in range(groups):
        counted.append(sums[i : i + 1, :] + total)
        total = total + sums[i : i + 1, LANES - 1 :]
    counted = jnp.concatenate(counted, axis=1)
    slot = lax.broadcasted_iota(I32, first.shape, 1).astype(F32)
    place = jnp.where(first > 0.0, counted - 1.0, total + slot - counted)
    order = spread(place.astype(I32), 0, slots)
    digits = []
    for row in rows:
        digits += [lax.shift_right_logical(row, 7), jnp.bitwise_and(row, 127)]
    digits = [d.astype(F32) for d in digits]
    spare = ceil_to(len(digits), 8) - len(digits)
    digits = jnp.concatenate(digits + [jnp.zeros((spare, slots), F32)] * bool(spare), axis=0)
    moved = mm_t(digits.astype(BF16), order).astype(I32)
    moved = [moved[2 * i : 2 * i + 1, :] * 128 + moved[2 * i + 1 : 2 * i + 2, :] for i in range(len(rows))]
    return total, moved


def flagged(condition, count):
    slot = lax.broadcasted_iota(I32, condition.shape, 1)
    return jnp.where(condition & (slot < count), 1.0, 0.0)


def encode_local_kernel(
    groups,
    coarse,
    counts,
    sender,
    target,
    sender2,
    target2,
    grid,
    mesh,
    w_source,
    w_dest,
    near,
    early,
    near_source,
    part,
    hidden,
    summed16,
    live_send,
    live_goal,
    live_send2,
    live_goal2,
    send_col2,
    goal_col2,
    pick_rim,
    pick_goal,
):
    count, count2 = counts[0], counts[1]
    rows, grid_rows = mesh.shape[0], grid.shape[0]
    rim = pick_rim.shape[1] // 2
    source = (0.5 * mm(grid[...], w_source[...])).astype(BF16)
    dest = (0.5 * mm(mesh[...], w_dest[...])).astype(BF16)
    near_source[...] = (0.5 * mm(near[...], w_source[...])).astype(BF16)
    me = lax.axis_index("group")
    gather, reduce = plans(groups)
    sources = [look_up([p.index(i) for i in range(groups)], me) for p in gather]
    goals = [look_up(p, me) for p in reduce]
    send, send2 = as_row(sender), as_row(sender2)
    back2 = coarse_slots(send2, rows, coarse, goals)
    send2 = coarse_slots(send2, rows, coarse, sources)
    total, (send, goal) = arrange(flagged(send >= grid_rows, count), [send, as_row(target)])
    moved = [send2, as_row(target2), back2]
    total2, (send2, goal2, back2) = arrange(flagged(send2 >= rows, count2), moved)
    early[:1, :] = jnp.broadcast_to(total, (1, LANES)).astype(I32)
    early[1:, :] = jnp.broadcast_to(total2, (1, LANES)).astype(I32)
    send_col, goal_col = to_columns(send, goal)
    send_col2[...], goal_col2[...] = to_columns(send2, goal2)
    near_first, far_first = rim_starts(grid_rows, rim)
    pick_rim[:, :rim] = pick(send_col, near_first, rim)
    pick_rim[:, rim:] = pick(send_col, far_first, rim)
    pick_goal[...] = pick(goal_col, 0, rows)
    live_send[...] = only_live(send, count)
    live_goal[...] = only_live(goal, count)
    live_send2[...] = only_live(back2, count2)
    live_goal2[...] = only_live(goal2, count2)
    for c in pieces_of(part.shape[0], FIRST):
        u = mm(pick(send_col[c, :], 0, grid_rows), source) + mm(pick_goal[c, :], dest)
        part[c, :] = u
        if c.start:
            hidden[c, :] = (u + u * jnp.tanh(u)).astype(BF16)
    summed16[...] = mm(spread(live_goal[:, FIRST:], 0, coarse), hidden[FIRST:, :])


def pieces_of(n, size):
    return [slice(i, min(i + size, n)) for i in range(0, n, size)]


def encode_halo_kernel(
    coarse,
    early,
    near_source,
    far,
    part,
    hidden_local,
    summed16,
    pick_rim,
    live_goal,
    mesh,
    w_source,
    w_out,
    gain,
    half,
    hidden,
    updated16,
):
    number = jnp.max(early[:1, :])
    far_source = (0.5 * mm(far[...], w_source[...])).astype(BF16)
    source = jnp.concatenate([near_source[...], far_source], axis=0)

    def edges(c):
        u = part[c, :] + mm(pick_rim[c, :], source)
        half[c, :] = u
        hidden[c, :] = (u + u * jnp.tanh(u)).astype(BF16)

    def finish(summed):
        normed, _ = normalise(mm(summed.astype(BF16), w_out[...]))
        updated16[...] = (mesh[:coarse, :].astype(F32) + normed * as_row(gain)).astype(BF16)

    def first_edges():
        for c in pieces_of(FIRST, 128):
            edges(c)

    @pl.when(number <= FIRST)
    def _():
        first_edges()
        goal = spread(live_goal[:, :FIRST], 0, coarse)
        finish(summed16[...] + mm(goal, hidden[:FIRST, :]))

    @pl.when(number > FIRST)
    def _():
        first_edges()
        for c in pieces_of(part.shape[0], FIRST)[1:]:
            edges(c)
        finish(mm(spread(live_goal[...], 0, coarse), hidden[...]))


def process_local_kernel(
    hidden,
    live_goal,
    mesh,
    send_col2,
    goal_col2,
    live_send2,
    live_goal2,
    cotangent,
    w_out,
    gain,
    gain2,
    w_source,
    w_dest,
    normed_ref,
    inverse_ref,
    part,
    pick_goal2,
    pick_coarse,
    sum_goal2,
    sum_coarse,
    centre2,
    summed2,
    hidden2,
):
    rows = mesh.shape[0]
    summed = mm(spread(live_goal[...], 0, rows), hidden[...]).astype(BF16)
    normed, inverse = normalise(mm(summed, w_out[...]))
    normed_ref[...] = normed
    inverse_ref[...] = jnp.broadcast_to(inverse, inverse_ref.shape)
    updated = (mesh[...].astype(F32) + normed * as_row(gain)).astype(BF16)
    source = (0.5 * mm(updated, w_source[...])).astype(BF16)
    dest = (0.5 * mm(updated, w_dest[...])).astype(BF16)
    pick_goal2[...] = pick(goal_col2[...], 0, rows)
    pick_coarse[...] = pick(send_col2[...], rows, pick_coarse.shape[1])
    sum_goal2[...] = spread(live_goal2[...], 0, rows)
    sum_coarse[...] = spread(live_send2[...], rows, sum_coarse.shape[0])
    centre2[...] = centred(cotangent[...].astype(F32) * as_row(gain2))
    for c in pieces_of(part.shape[0], FIRST2):
        u = mm(pick(send_col2[c, :], 0, rows), source) + mm(pick_goal2[c, :], dest)
        part[c, :] = u
        if c.start:
            hidden2[c, :] = (u + u * jnp.tanh(u)).astype(BF16)
    summed2[...] = mm(sum_goal2[:, FIRST2:], hidden2[FIRST2:, :])


def process_kernel(
    coarse,
    early,
    part,
    pick_goal2,
    pick_coarse,
    sum_goal2,
    sum_coarse,
    centre2,
    summed2,
    w_source,
    w_out,
    *refs,
):
    peers = sum_coarse.shape[0] // coarse
    received, (half, grad_first, back_ref) = refs[:peers], refs[peers : peers + 3]
    returned, (hidden, slope, grad, gathered, turned) = refs[peers + 3 : -5], refs[-5:]
    number = jnp.max(early[1:, :])
    rows = jnp.concatenate([r[...] for r in received], axis=0)
    source = (0.5 * mm(rows, w_source[...])).astype(BF16)
    spare = pick_coarse.shape[1] - source.shape[0]
    if spare:
        source = jnp.concatenate([source, jnp.zeros((spare, source.shape[1]), BF16)], axis=0)

    def edges(c):
        u = part[c, :] + mm(pick_coarse[c, :], source)
        if c.start >= FIRST2:
            half[c, :] = u
        value, double = half_silu(u)
        hidden[c, :] = value.astype(BF16)
        slope[c, :] = double.astype(BF16)

    def turn(summed):
        gathered[...] = mm(summed.astype(BF16), w_out[...])
        for r in pieces_of(gathered.shape[0], 32):
            center = centred(gathered[r, :])
            inverse = lax.rsqrt(jnp.mean(center * center, axis=-1, keepdims=True) + EPSILON)
            share = jnp.mean(center * centre2[r, :], axis=-1, keepdims=True)
            share = share * inverse * inverse
            turned[r, :] = (inverse * (centre2[r, :] - center * share)).astype(BF16)
        back = (0.5 * mm_t(turned[...], w_out[...])).astype(BF16)
        back_ref[...] = back
        grad_first[...] = (mm(pick_goal2[:FIRST2, :], back) * slope[:FIRST2, :].astype(F32)).astype(BF16)
        return back

    def send(sums):
        for i, out in enumerate(returned):
            out[...] = sums[i * coarse : (i + 1) * coarse].astype(BF16)

    def first_edges():
        for c in pieces_of(FIRST2, 128):
            edges(c)

    @pl.when(number <= FIRST2)
    def _():
        first_edges()
        turn(summed2[...] + mm(sum_goal2[:, :FIRST2], hidden[:FIRST2, :]))
        send(mm(sum_coarse[:, :FIRST2], grad_first[...]))

    @pl.when(number > FIRST2)
    def _():
        first_edges()
        later = pieces_of(part.shape[0], FIRST2)[1:]
        for c in later:
            edges(c)
        back = turn(mm(sum_goal2[...], hidden[...]))
        grad[:FIRST2, :] = grad_first[...]
        for c in later:
            grad[c, :] = (mm(pick_goal2[c, :], back) * slope[c, :].astype(F32)).astype(BF16)
        send(mm(sum_coarse[...], grad[...]))


def process_back_kernel(
    grid_rows,
    half,
    half2,
    grad_first,
    back2,
    pick_goal2,
    live_send,
    live_send2,
    sum_goal2,
    cotangent,
    w_source,
    w_dest,
    w_out,
    gain,
    normed,
    inverse,
    grad_local,
    back_ref,
    slope,
    sum_rim,
    grad,
):
    rows = cotangent.shape[0]
    rim = sum_rim.shape[0] // 2
    grad[:FIRST2, :] = grad_first[...]
    for c in pieces_of(half2.shape[0], FIRST2)[1:]:
        double = half_silu(half2[c, :])[1]
        grad[c, :] = (mm(pick_goal2[c, :], back2[...]) * double).astype(BF16)
    table = mm(spread(live_send2[...], 0, rows), grad[...]).astype(BF16)
    dest = mm(sum_goal2[...], grad[...]).astype(BF16)
    local = cotangent[...].astype(F32) + mm_t(table, w_source[...]) + mm_t(dest, w_dest[...])
    grad_local[...] = local
    back = normalise_back(centred(local * as_row(gain)), normed[...], inverse[:, :1])
    back_ref[...] = (0.5 * mm_t(back.astype(BF16), w_out[...])).astype(BF16)
    near_first, far_first = rim_starts(grid_rows, rim)
    sum_rim[:rim, :] = spread(live_send[...], near_first, rim)
    sum_rim[rim:, :] = spread(live_send[...], far_first, rim)
    slope[...] = half_silu(half[:FIRST, :])[1].astype(BF16)


def encode_back_kernel(
    early,
    grad_local,
    back_local,
    normed,
    inverse,
    half,
    slope,
    pick_goal,
    sum_rim,
    gain,
    w_source2,
    w_out,
    *refs,
):
    received, (back_ref, grad_first, near, far, updated16, grad) = refs[:-6], refs[-6:]
    coarse = updated16.shape[0]
    rim = near.shape[0]
    number = jnp.max(early[:1, :])
    total = received[0][...].astype(F32)
    for r in received[1:]:
        total = total + r[...].astype(F32)
    updated = grad_local[:coarse, :] + mm_t(total.astype(BF16), w_source2[...])
    updated16[...] = updated

    def turn():
        back = normalise_back(
            centred(updated * as_row(gain)), normed[:coarse, :], inverse[:coarse, :1]
        )
        back = (0.5 * mm_t(back.astype(BF16), w_out[...])).astype(BF16)
        back = jnp.concatenate([back, back_local[coarse:, :]], axis=0)
        back_ref[...] = back
        first = mm(pick_goal[:FIRST, :], back) * slope[...].astype(F32)
        grad_first[...] = first.astype(BF16)

    @pl.when(number <= FIRST)
    def _():
        turn()
        far[...] = mm(sum_rim[rim:, :FIRST], grad_first[...]).astype(BF16)
        near[...] = mm(sum_rim[:rim, :FIRST], grad_first[...]).astype(BF16)

    @pl.when(number > FIRST)
    def _():
        turn()
        grad[:FIRST, :] = grad_first[...]
        for c in pieces_of(half.shape[0], FIRST)[1:]:
            grad[c, :] = edge_grad(c, pick_goal, back_ref[...], half)
        far[...] = mm(sum_rim[rim:, :], grad[...]).astype(BF16)
        near[...] = mm(sum_rim[:rim, :], grad[...]).astype(BF16)


def edge_grad(c, pick_goal, back, half):
    return (mm(pick_goal[c, :], back) * half_silu(half[c, :])[1]).astype(BF16)


def own_back_kernel(
    grad_first,
    back,
    half,
    pick_goal,
    live_send,
    live_goal,
    grad_local,
    updated16,
    w_source,
    w_dest,
    halo,
    near,
    mesh_grad,
    own,
    sum_far,
    grad,
):
    coarse = updated16.shape[0]
    rows = grad_local.shape[0]
    grad[:FIRST, :] = grad_first[...]
    for c in pieces_of(half.shape[0], FIRST)[1:]:
        grad[c, :] = edge_grad(c, pick_goal, back[...], half)
    dest = mm(spread(live_goal[...], 0, rows), grad[...]).astype(BF16)
    updated = jnp.concatenate([updated16[...], grad_local[coarse:, :]], axis=0)
    mesh_grad[...] = (updated + mm_t(dest, w_dest[...])).astype(BF16)
    source = mm(spread(live_send[...], 0, own.shape[0]), grad[...]).astype(BF16)
    rows_near, rows_far = halves(as_row(halo), even_patch())
    sum_far[...] = spread(rows_far, 0, own.shape[0])
    back_near = mm_t(near[...], w_source[...]).astype(BF16)
    own[...] = mm_t(source, w_source[...]) + mm(spread(rows_near, 0, own.shape[0]), back_near)


def finish_kernel(own, sum_far, far, w_source, out_hbm, out, sems):
    projected = mm_t(far[...], w_source[...]).astype(BF16)
    copies = []
    for i, c in enumerate(pieces_of(own.shape[0], own.shape[0] // 8)):
        out[c, :] = (own[c, :] + mm(sum_far[c, :], projected)).astype(BF16)
        copies.append(pltpu.make_async_copy(out.at[c], out_hbm.at[c], sems.at[i]))
        copies[-1].start()
    for copy in copies:
        copy.wait()


SMEM = pl.BlockSpec(memory_space=pltpu.SMEM)
HBM = pl.BlockSpec(memory_space=pltpu.HBM)
VMEM = pl.BlockSpec(memory_space=pltpu.VMEM)
MICROSECOND = 1 << 30


def call(kernel, arrays, outs, cost, raw=0, scalars=0, scratch=(), out_specs=None, aliases=None):
    return pl.pallas_call(
        kernel,
        out_shape=[jax.ShapeDtypeStruct(s, d) for s, d in outs],
        in_specs=[HBM] * raw + [SMEM] * scalars + [VMEM] * (len(arrays) - raw - scalars),
        out_specs=out_specs or [VMEM] * len(outs),
        input_output_aliases=aliases or {},
        scratch_shapes=list(scratch),
        compiler_params=pltpu.CompilerParams(vmem_limit_bytes=24 << 20),
        cost_estimate=pl.CostEstimate(
            flops=int(cost * MICROSECOND), bytes_accessed=1 << 20, transcendentals=0
        ),
    )(*(pltpu.with_memory_space_constraint(x, pltpu.HBM) for x in arrays[:raw]), *arrays[raw:])


def swap_halo(near, far, n):
    far_pairs = [(i, (i + 1) % n if i % 2 else (i - 1) % n) for i in range(n)]
    far = lax.ppermute(far, "patch", far_pairs)
    near = lax.ppermute(near, "patch", [(i, i ^ 1) for i in range(n)])
    return near, far


def exchange(pieces, plan):
    out = []
    for piece, goals in zip(pieces, plan):
        out.append(lax.ppermute(piece, "group", list(enumerate(goals))))
    return out


def on_device(
    grid_latent,
    mesh_latent,
    cotangent,
    halo_rows,
    encoder_sender,
    encoder_target,
    encoder_count,
    process_sender,
    process_target,
    process_count,
    encoder_source,
    encoder_dest,
    encoder_output,
    encoder_gain,
    process_source,
    process_dest,
    process_output,
    process_gain,
):
    patches, groups = lax.axis_size("patch"), lax.axis_size("group")
    grid_rows, width = grid_latent.shape
    mesh_rows = mesh_latent.shape[0]
    hidden_size = encoder_source.shape[1]
    coarse = mesh_rows // 16
    rim = halo_rows.shape[0] // 2
    slots, slots2 = encoder_sender.shape[0], process_sender.shape[0]

    row_form, row_form2 = ((1, slots), I32), ((1, slots2), I32)
    column_form2 = ((slots2, LANES), I16)
    remote = coarse * (groups - 1)
    near, far, grid = call(
        select_kernel,
        [halo_rows, grid_latent],
        [((rim, width), BF16)] * 2 + [((grid_rows, width), BF16)],
        4,
        raw=2,
        scratch=[pltpu.VMEM(halo_rows.shape, I32), pltpu.SemaphoreType.DMA((2,))],
    )
    near, far = swap_halo(near, far, patches)
    (
        early,
        near_source,
        part,
        hidden,
        summed16,
        live_send,
        live_goal,
        live_send2,
        live_goal2,
        send_col2,
        goal_col2,
        pick_rim,
        pick_goal,
    ) = call(
        functools.partial(encode_local_kernel, groups, coarse),
        [
            jnp.concatenate([encoder_count, process_count]),
            encoder_sender,
            encoder_target,
            process_sender,
            process_target,
            grid,
            mesh_latent,
            encoder_source,
            encoder_dest,
            near,
        ],
        [((2, LANES), I32), ((rim, hidden_size), BF16), ((slots, hidden_size), F32), ((slots, hidden_size), BF16)]
        + [((coarse, hidden_size), F32), row_form, row_form, row_form2, row_form2]
        + [column_form2, column_form2]
        + [((slots, 2 * rim), BF16), ((slots, mesh_rows), BF16)],
        2,
        scalars=1,
    )
    half, hidden, updated16 = call(
        functools.partial(encode_halo_kernel, coarse),
        [
            early,
            near_source,
            far,
            part,
            hidden,
            summed16,
            pick_rim,
            live_goal,
            mesh_latent,
            encoder_source,
            encoder_output,
            encoder_gain,
        ],
        [((slots, hidden_size), F32), ((slots, hidden_size), BF16), ((coarse, width), BF16)],
        2,
        aliases={3: 0, 4: 1},
    )
    shifts = exchange([updated16] * (groups - 1), plans(groups)[0])
    (
        normed,
        inverse,
        part2,
        pick_goal2,
        pick_coarse,
        sum_goal2,
        sum_coarse,
        centre2,
        summed2,
    ) = call(
        process_local_kernel,
        [
            hidden,
            live_goal,
            mesh_latent,
            send_col2,
            goal_col2,
            live_send2,
            live_goal2,
            cotangent,
            encoder_output,
            encoder_gain,
            process_gain,
            process_source,
            process_dest,
        ],
        [
            ((mesh_rows, width), F32),
            ((mesh_rows, LANES), F32),
            ((slots2, hidden_size), F32),
            ((slots2, mesh_rows), BF16),
            ((slots2, ceil_to(remote, LANES)), BF16),
            ((mesh_rows, slots2), BF16),
            ((remote, slots2), BF16),
            ((mesh_rows, width), F32),
            ((mesh_rows, hidden_size), F32),
        ],
        2,
        scratch=[pltpu.VMEM((slots2, hidden_size), BF16)],
    )
    half2, grad_first2, back2, *pieces = call(
        functools.partial(process_kernel, coarse),
        [
            early,
            part2,
            pick_goal2,
            pick_coarse,
            sum_goal2,
            sum_coarse,
            centre2,
            summed2,
            process_source,
            process_output,
            *shifts,
        ],
        [((slots2, hidden_size), F32), ((FIRST2, hidden_size), BF16)]
        + [((mesh_rows, hidden_size), BF16)]
        + [((coarse, hidden_size), BF16)] * (groups - 1),
        2,
        scratch=[
            pltpu.VMEM((slots2, hidden_size), BF16),
            pltpu.VMEM((slots2, hidden_size), BF16),
            pltpu.VMEM((slots2, hidden_size), BF16),
            pltpu.VMEM((mesh_rows, width), F32),
            pltpu.VMEM((mesh_rows, width), BF16),
        ],
        aliases={1: 0},
    )
    pieces = exchange(pieces, plans(groups)[1])
    grad_local, back, slope, sum_rim = call(
        functools.partial(process_back_kernel, grid_rows),
        [
            half,
            half2,
            grad_first2,
            back2,
            pick_goal2,
            live_send,
            live_send2,
            sum_goal2,
            cotangent,
            process_source,
            process_dest,
            encoder_output,
            encoder_gain,
            normed,
            inverse,
        ],
        [
            ((mesh_rows, width), F32),
            ((mesh_rows, hidden_size), BF16),
            ((FIRST, hidden_size), BF16),
            ((2 * rim, slots), BF16),
        ],
        2,
        scratch=[pltpu.VMEM((slots2, hidden_size), BF16)],
    )
    back, grad_first, near, far, grad16 = call(
        encode_back_kernel,
        [
            early,
            grad_local,
            back,
            normed,
            inverse,
            half,
            slope,
            pick_goal,
            sum_rim,
            encoder_gain,
            process_source,
            encoder_output,
            *pieces,
        ],
        [((mesh_rows, hidden_size), BF16), ((FIRST, hidden_size), BF16)]
        + [((rim, hidden_size), BF16)] * 2
        + [((coarse, width), F32)],
        2,
        scratch=[pltpu.VMEM((slots, hidden_size), BF16)],
    )
    near, far = swap_halo(near, far, patches)
    mesh_grad, own, sum_far = call(
        own_back_kernel,
        [
            grad_first,
            back,
            half,
            pick_goal,
            live_send,
            live_goal,
            grad_local,
            grad16,
            encoder_source,
            encoder_dest,
            halo_rows,
            near,
        ],
        [((mesh_rows, width), BF16), ((grid_rows, width), F32), ((grid_rows, rim), BF16)],
        2,
        scratch=[pltpu.VMEM((slots, hidden_size), BF16)],
    )
    (grid_grad,) = call(
        finish_kernel,
        [own, sum_far, far, encoder_source],
        [((grid_rows, width), BF16)],
        2,
        scratch=[pltpu.VMEM((grid_rows, width), BF16), pltpu.SemaphoreType.DMA((8,))],
        out_specs=[HBM],
    )
    return grid_grad, mesh_grad


def solution(mesh):
    rows, flat, whole = P(("patch", "group"), None), P(("patch", "group")), P()
    return jax.shard_map(
        on_device,
        mesh=mesh,
        in_specs=(rows,) * 3 + (flat,) * 7 + (whole,) * 8,
        out_specs=(rows, rows),
        check_vma=False,
    )
```

```python
import functools

import jax
import jax.numpy as jnp
from jax import lax
from jax.experimental import pallas as pl
from jax.experimental.pallas import tpu as pltpu
from jax.sharding import PartitionSpec as P


EPSILON = 1e-05
LANES = 128
FIRST = 256
FIRST2 = 128
F32 = jnp.float32
BF16 = jnp.bfloat16
I32 = jnp.int32
I16 = jnp.int16


def mm(a, b):
    return jnp.dot(a, b, preferred_element_type=F32)


def mm_t(a, b):
    return lax.dot_general(a, b, (((1,), (1,)), ((), ())), preferred_element_type=F32)


def half_silu(u):
    t = jnp.tanh(u)
    a = 1.0 + t
    value = u * a
    return value, a + value * (1.0 - t)


def ceil_to(n, k):
    return (n + k - 1) // k * k


def to_columns(*rows):
    packed = rows[0] if len(rows) == 1 else rows[0] + rows[1] * 4096
    parts = []
    for i in range(0, packed.shape[1], LANES):
        parts.append(jnp.broadcast_to(packed[:, i : i + LANES], (LANES, LANES)).T)
    columns = jnp.concatenate(parts, axis=0)
    if len(rows) == 1:
        return columns.astype(I16)
    low = jnp.bitwise_and(columns, 4095).astype(I16)
    return low, lax.shift_right_logical(columns, 12).astype(I16)


def one_hot(equal):
    return jnp.where(equal, jnp.ones((), BF16), jnp.zeros((), BF16))


def pick(columns, first, width):
    lane = lax.broadcasted_iota(I32, columns.shape, 1)
    parts = [one_hot(columns == (lane + (first + i)).astype(I16)) for i in range(0, width, LANES)]
    return parts[0] if len(parts) == 1 else jnp.concatenate(parts, axis=1)


def spread(row, first, height):
    shape = (height, row.shape[1])
    number = lax.broadcasted_iota(I32, shape, 0) + first
    return one_hot(jnp.broadcast_to(row, shape).astype(I16) == number.astype(I16))


def only_live(rows, count):
    slot = lax.broadcasted_iota(I32, rows.shape, 1)
    return jnp.where(slot < count, rows, -1)


def normalise(values):
    center = values - jnp.mean(values, axis=-1, keepdims=True)
    inverse = lax.rsqrt(jnp.mean(center * center, axis=-1, keepdims=True) + EPSILON)
    return center * inverse, inverse


def centred(values):
    return values - jnp.mean(values, axis=-1, keepdims=True)


def normalise_back(centre, normed, inverse):
    return inverse * (centre - normed * jnp.mean(centre * normed, axis=-1, keepdims=True))


def halves(rows, even):
    half = rows.shape[1] // 2
    first, second = rows[:, :half], rows[:, half:]
    return jnp.where(even, second, first), jnp.where(even, first, second)


def plans(n):
    masks = [tuple(i ^ k for i in range(n)) for k in range(n - 1, 0, -1)]
    if n == 4:
        return [(1, 3, 0, 2), (3, 2, 1, 0), (2, 0, 3, 1)], masks
    return masks, masks


def look_up(table, index):
    value = jnp.int32(table[0])
    for i, entry in enumerate(table[1:], 1):
        value = jnp.where(index == i, jnp.int32(entry), value)
    return value


def coarse_slots(sender, mesh_rows, coarse, owners):
    offset = sender - mesh_rows
    owner = offset // coarse
    moved = offset - owner * coarse
    for k, other in enumerate(owners):
        moved = moved + jnp.where(owner == other, mesh_rows + k * coarse, 0)
    return jnp.where(offset < 0, sender, moved)


def even_patch():
    return lax.rem(lax.axis_index("patch"), 2) == 0


def as_row(ref):
    return ref[...].reshape(1, ref.shape[0])


def select_kernel(halo_hbm, grid_hbm, near, far, table, halo, sems):
    copies = [
        pltpu.make_async_copy(halo_hbm, halo, sems.at[0]),
        pltpu.make_async_copy(grid_hbm, table, sems.at[1]),
    ]
    for copy in copies:
        copy.start()
    copies[0].wait()
    rows_near, rows_far = halves(as_row(halo), even_patch())
    pick_near = pick(to_columns(rows_near), 0, table.shape[0])
    pick_far = pick(to_columns(rows_far), 0, table.shape[0])
    copies[1].wait()
    near[...] = mm(pick_near, table[...]).astype(BF16)
    far[...] = mm(pick_far, table[...]).astype(BF16)


def rim_starts(grid_rows, rim):
    even = even_patch()
    return (
        jnp.where(even, grid_rows + rim, grid_rows),
        jnp.where(even, grid_rows, grid_rows + rim),
    )


def arrange(first, rows):
    slots = first.shape[1]
    groups = slots // LANES
    flags = [first[:, i * LANES : (i + 1) * LANES] for i in range(groups)]
    spare = ceil_to(groups, 8) - groups
    stack = jnp.concatenate(flags + [jnp.zeros((spare, LANES), F32)] * bool(spare), axis=0)
    shape = (LANES, LANES)
    before = lax.broadcasted_iota(I32, shape, 0) <= lax.broadcasted_iota(I32, shape, 1)
    sums = mm(stack.astype(BF16), jnp.where(before, 1.0, 0.0).astype(BF16))
    total = jnp.zeros((1, 1), F32)
    counted = []
    for i in range(groups):
        counted.append(sums[i : i + 1, :] + total)
        total = total + sums[i : i + 1, LANES - 1 :]
    counted = jnp.concatenate(counted, axis=1)
    slot = lax.broadcasted_iota(I32, first.shape, 1).astype(F32)
    place = jnp.where(first > 0.0, counted - 1.0, total + slot - counted)
    order = spread(place.astype(I32), 0, slots)
    digits = []
    for row in rows:
        digits += [lax.shift_right_logical(row, 7), jnp.bitwise_and(row, 127)]
    digits = [d.astype(F32) for d in digits]
    spare = ceil_to(len(digits), 8) - len(digits)
    digits = jnp.concatenate(digits + [jnp.zeros((spare, slots), F32)] * bool(spare), axis=0)
    moved = mm_t(digits.astype(BF16), order).astype(I32)
    moved = [moved[2 * i : 2 * i + 1, :] * 128 + moved[2 * i + 1 : 2 * i + 2, :] for i in range(len(rows))]
    return total, moved


def flagged(condition, count):
    slot = lax.broadcasted_iota(I32, condition.shape, 1)
    return jnp.where(condition & (slot < count), 1.0, 0.0)


def encode_local_kernel(
    groups,
    coarse,
    counts,
    sender,
    target,
    sender2,
    target2,
    grid,
    mesh,
    w_source,
    w_dest,
    near,
    early,
    near_source,
    part,
    hidden,
    summed16,
    live_send,
    live_goal,
    live_send2,
    live_goal2,
    send_col2,
    goal_col2,
    pick_rim,
    pick_goal,
):
    count, count2 = counts[0], counts[1]
    rows, grid_rows = mesh.shape[0], grid.shape[0]
    rim = pick_rim.shape[1] // 2
    source = (0.5 * mm(grid[...], w_source[...])).astype(BF16)
    dest = (0.5 * mm(mesh[...], w_dest[...])).astype(BF16)
    near_source[...] = (0.5 * mm(near[...], w_source[...])).astype(BF16)
    me = lax.axis_index("group")
    gather, reduce = plans(groups)
    sources = [look_up([p.index(i) for i in range(groups)], me) for p in gather]
    goals = [look_up(p, me) for p in reduce]
    send, send2 = as_row(sender), as_row(sender2)
    back2 = coarse_slots(send2, rows, coarse, goals)
    send2 = coarse_slots(send2, rows, coarse, sources)
    total, (send, goal) = arrange(flagged(send >= grid_rows, count), [send, as_row(target)])
    moved = [send2, as_row(target2), back2]
    total2, (send2, goal2, back2) = arrange(flagged(send2 >= rows, count2), moved)
    early[:1, :] = jnp.broadcast_to(total, (1, LANES)).astype(I32)
    early[1:, :] = jnp.broadcast_to(total2, (1, LANES)).astype(I32)
    send_col, goal_col = to_columns(send, goal)
    send_col2[...], goal_col2[...] = to_columns(send2, goal2)
    near_first, far_first = rim_starts(grid_rows, rim)
    pick_rim[:, :rim] = pick(send_col, near_first, rim)
    pick_rim[:, rim:] = pick(send_col, far_first, rim)
    pick_goal[...] = pick(goal_col, 0, rows)
    live_send[...] = only_live(send, count)
    live_goal[...] = only_live(goal, count)
    live_send2[...] = only_live(back2, count2)
    live_goal2[...] = only_live(goal2, count2)
    for c in pieces_of(part.shape[0], FIRST):
        u = mm(pick(send_col[c, :], 0, grid_rows), source) + mm(pick_goal[c, :], dest)
        part[c, :] = u
        if c.start:
            hidden[c, :] = (u + u * jnp.tanh(u)).astype(BF16)
    summed16[...] = mm(spread(live_goal[:, FIRST:], 0, coarse), hidden[FIRST:, :])


def pieces_of(n, size):
    return [slice(i, min(i + size, n)) for i in range(0, n, size)]


def encode_halo_kernel(
    coarse,
    early,
    near_source,
    far,
    part,
    hidden_local,
    summed16,
    pick_rim,
    live_goal,
    mesh,
    w_source,
    w_out,
    gain,
    half,
    hidden,
    updated16,
):
    number = jnp.max(early[:1, :])
    far_source = (0.5 * mm(far[...], w_source[...])).astype(BF16)
    source = jnp.concatenate([near_source[...], far_source], axis=0)

    def edges(c):
        u = part[c, :] + mm(pick_rim[c, :], source)
        half[c, :] = u
        hidden[c, :] = (u + u * jnp.tanh(u)).astype(BF16)

    def finish(summed):
        normed, _ = normalise(mm(summed.astype(BF16), w_out[...]))
        updated16[...] = (mesh[:coarse, :].astype(F32) + normed * as_row(gain)).astype(BF16)

    def first_edges():
        for c in pieces_of(FIRST, 128):
            edges(c)

    @pl.when(number <= FIRST)
    def _():
        first_edges()
        goal = spread(live_goal[:, :FIRST], 0, coarse)
        finish(summed16[...] + mm(goal, hidden[:FIRST, :]))

    @pl.when(number > FIRST)
    def _():
        first_edges()
        for c in pieces_of(part.shape[0], FIRST)[1:]:
            edges(c)
        finish(mm(spread(live_goal[...], 0, coarse), hidden[...]))


def process_local_kernel(
    hidden,
    live_goal,
    mesh,
    send_col2,
    goal_col2,
    live_send2,
    live_goal2,
    cotangent,
    w_out,
    gain,
    gain2,
    w_source,
    w_dest,
    normed_ref,
    inverse_ref,
    part,
    pick_goal2,
    pick_coarse,
    sum_goal2,
    sum_coarse,
    centre2,
    summed2,
    hidden2,
):
    rows = mesh.shape[0]
    summed = mm(spread(live_goal[...], 0, rows), hidden[...]).astype(BF16)
    normed, inverse = normalise(mm(summed, w_out[...]))
    normed_ref[...] = normed
    inverse_ref[...] = jnp.broadcast_to(inverse, inverse_ref.shape)
    updated = (mesh[...].astype(F32) + normed * as_row(gain)).astype(BF16)
    source = (0.5 * mm(updated, w_source[...])).astype(BF16)
    dest = (0.5 * mm(updated, w_dest[...])).astype(BF16)
    pick_goal2[...] = pick(goal_col2[...], 0, rows)
    pick_coarse[...] = pick(send_col2[...], rows, pick_coarse.shape[1])
    sum_goal2[...] = spread(live_goal2[...], 0, rows)
    sum_coarse[...] = spread(live_send2[...], rows, sum_coarse.shape[0])
    centre2[...] = centred(cotangent[...].astype(F32) * as_row(gain2))
    for c in pieces_of(part.shape[0], FIRST2):
        u = mm(pick(send_col2[c, :], 0, rows), source) + mm(pick_goal2[c, :], dest)
        part[c, :] = u
        if c.start:
            hidden2[c, :] = (u + u * jnp.tanh(u)).astype(BF16)
    summed2[...] = mm(sum_goal2[:, FIRST2:], hidden2[FIRST2:, :])


def process_kernel(
    coarse,
    early,
    part,
    pick_goal2,
    pick_coarse,
    sum_goal2,
    sum_coarse,
    centre2,
    summed2,
    w_source,
    w_out,
    *refs,
):
    peers = sum_coarse.shape[0] // coarse
    received, (half, grad_first, back_ref) = refs[:peers], refs[peers : peers + 3]
    returned, (hidden, slope, grad, gathered, turned) = refs[peers + 3 : -5], refs[-5:]
    number = jnp.max(early[1:, :])
    rows = jnp.concatenate([r[...] for r in received], axis=0)
    source = (0.5 * mm(rows, w_source[...])).astype(BF16)
    spare = pick_coarse.shape[1] - source.shape[0]
    if spare:
        source = jnp.concatenate([source, jnp.zeros((spare, source.shape[1]), BF16)], axis=0)

    def edges(c):
        u = part[c, :] + mm(pick_coarse[c, :], source)
        if c.start >= FIRST2:
            half[c, :] = u
        value, double = half_silu(u)
        hidden[c, :] = value.astype(BF16)
        slope[c, :] = double.astype(BF16)

    def turn(summed):
        gathered[...] = mm(summed.astype(BF16), w_out[...])
        for r in pieces_of(gathered.shape[0], 32):
            center = centred(gathered[r, :])
            inverse = lax.rsqrt(jnp.mean(center * center, axis=-1, keepdims=True) + EPSILON)
            share = jnp.mean(center * centre2[r, :], axis=-1, keepdims=True)
            share = share * inverse * inverse
            turned[r, :] = (inverse * (centre2[r, :] - center * share)).astype(BF16)
        back = (0.5 * mm_t(turned[...], w_out[...])).astype(BF16)
        back_ref[...] = back
        grad_first[...] = (mm(pick_goal2[:FIRST2, :], back) * slope[:FIRST2, :].astype(F32)).astype(BF16)
        return back

    def send(sums):
        for i, out in enumerate(returned):
            out[...] = sums[i * coarse : (i + 1) * coarse].astype(BF16)

    def first_edges():
        for c in pieces_of(FIRST2, 128):
            edges(c)

    @pl.when(number <= FIRST2)
    def _():
        first_edges()
        turn(summed2[...] + mm(sum_goal2[:, :FIRST2], hidden[:FIRST2, :]))
        send(mm(sum_coarse[:, :FIRST2], grad_first[...]))

    @pl.when(number > FIRST2)
    def _():
        first_edges()
        later = pieces_of(part.shape[0], FIRST2)[1:]
        for c in later:
            edges(c)
        back = turn(mm(sum_goal2[...], hidden[...]))
        grad[:FIRST2, :] = grad_first[...]
        for c in later:
            grad[c, :] = (mm(pick_goal2[c, :], back) * slope[c, :].astype(F32)).astype(BF16)
        send(mm(sum_coarse[...], grad[...]))


def process_back_kernel(
    grid_rows,
    half,
    half2,
    grad_first,
    back2,
    pick_goal2,
    live_send,
    live_send2,
    sum_goal2,
    cotangent,
    w_source,
    w_dest,
    w_out,
    gain,
    normed,
    inverse,
    grad_local,
    back_ref,
    slope,
    sum_rim,
    grad,
):
    rows = cotangent.shape[0]
    rim = sum_rim.shape[0] // 2
    grad[:FIRST2, :] = grad_first[...]
    for c in pieces_of(half2.shape[0], FIRST2)[1:]:
        double = half_silu(half2[c, :])[1]
        grad[c, :] = (mm(pick_goal2[c, :], back2[...]) * double).astype(BF16)
    table = mm(spread(live_send2[...], 0, rows), grad[...]).astype(BF16)
    dest = mm(sum_goal2[...], grad[...]).astype(BF16)
    local = cotangent[...].astype(F32) + mm_t(table, w_source[...]) + mm_t(dest, w_dest[...])
    grad_local[...] = local
    back = normalise_back(centred(local * as_row(gain)), normed[...], inverse[:, :1])
    back_ref[...] = (0.5 * mm_t(back.astype(BF16), w_out[...])).astype(BF16)
    near_first, far_first = rim_starts(grid_rows, rim)
    sum_rim[:rim, :] = spread(live_send[...], near_first, rim)
    sum_rim[rim:, :] = spread(live_send[...], far_first, rim)
    slope[...] = half_silu(half[:FIRST, :])[1].astype(BF16)


def encode_back_kernel(
    early,
    grad_local,
    back_local,
    normed,
    inverse,
    half,
    slope,
    pick_goal,
    sum_rim,
    gain,
    w_source2,
    w_out,
    *refs,
):
    received, (back_ref, grad_first, near, far, updated16, grad) = refs[:-6], refs[-6:]
    coarse = updated16.shape[0]
    rim = near.shape[0]
    number = jnp.max(early[:1, :])
    total = received[0][...].astype(F32)
    for r in received[1:]:
        total = total + r[...].astype(F32)
    updated = grad_local[:coarse, :] + mm_t(total.astype(BF16), w_source2[...])
    updated16[...] = updated

    def turn():
        back = normalise_back(
            centred(updated * as_row(gain)), normed[:coarse, :], inverse[:coarse, :1]
        )
        back = (0.5 * mm_t(back.astype(BF16), w_out[...])).astype(BF16)
        back = jnp.concatenate([back, back_local[coarse:, :]], axis=0)
        back_ref[...] = back
        for c in pieces_of(FIRST, 128):
            first = mm(pick_goal[c, :], back) * slope[c, :].astype(F32)
            grad_first[c, :] = first.astype(BF16)

    @pl.when(number <= FIRST)
    def _():
        turn()
        rows = mm(sum_rim[:, :FIRST], grad_first[...]).astype(BF16)
        near[...] = rows[:rim]
        far[...] = rows[rim:]

    @pl.when(number > FIRST)
    def _():
        turn()
        grad[:FIRST, :] = grad_first[...]
        for c in pieces_of(half.shape[0], FIRST)[1:]:
            grad[c, :] = edge_grad(c, pick_goal, back_ref[...], half)
        far[...] = mm(sum_rim[rim:, :], grad[...]).astype(BF16)
        near[...] = mm(sum_rim[:rim, :], grad[...]).astype(BF16)


def edge_grad(c, pick_goal, back, half):
    return (mm(pick_goal[c, :], back) * half_silu(half[c, :])[1]).astype(BF16)


def own_back_kernel(
    grad_first,
    back,
    half,
    pick_goal,
    live_send,
    live_goal,
    grad_local,
    updated16,
    w_source,
    w_dest,
    halo,
    near,
    mesh_grad,
    own,
    sum_far,
    grad,
):
    coarse = updated16.shape[0]
    rows = grad_local.shape[0]
    grad[:FIRST, :] = grad_first[...]
    for c in pieces_of(half.shape[0], FIRST)[1:]:
        grad[c, :] = edge_grad(c, pick_goal, back[...], half)
    dest = mm(spread(live_goal[...], 0, rows), grad[...]).astype(BF16)
    updated = jnp.concatenate([updated16[...], grad_local[coarse:, :]], axis=0)
    mesh_grad[...] = (updated + mm_t(dest, w_dest[...])).astype(BF16)
    source = mm(spread(live_send[...], 0, own.shape[0]), grad[...]).astype(BF16)
    rows_near, rows_far = halves(as_row(halo), even_patch())
    sum_far[...] = spread(rows_far, 0, own.shape[0])
    back_near = mm_t(near[...], w_source[...]).astype(BF16)
    own[...] = mm_t(source, w_source[...]) + mm(spread(rows_near, 0, own.shape[0]), back_near)


def finish_kernel(own, sum_far, far, w_source, out_hbm, out, sems):
    projected = mm_t(far[...], w_source[...]).astype(BF16)
    copies = []
    for i, c in enumerate(pieces_of(own.shape[0], own.shape[0] // 8)):
        out[c, :] = (own[c, :] + mm(sum_far[c, :], projected)).astype(BF16)
        copies.append(pltpu.make_async_copy(out.at[c], out_hbm.at[c], sems.at[i]))
        copies[-1].start()
    for copy in copies:
        copy.wait()


SMEM = pl.BlockSpec(memory_space=pltpu.SMEM)
HBM = pl.BlockSpec(memory_space=pltpu.HBM)
VMEM = pl.BlockSpec(memory_space=pltpu.VMEM)
MICROSECOND = 1 << 30


def call(kernel, arrays, outs, cost, raw=0, scalars=0, scratch=(), out_specs=None, aliases=None):
    return pl.pallas_call(
        kernel,
        out_shape=[jax.ShapeDtypeStruct(s, d) for s, d in outs],
        in_specs=[HBM] * raw + [SMEM] * scalars + [VMEM] * (len(arrays) - raw - scalars),
        out_specs=out_specs or [VMEM] * len(outs),
        input_output_aliases=aliases or {},
        scratch_shapes=list(scratch),
        compiler_params=pltpu.CompilerParams(vmem_limit_bytes=24 << 20),
        cost_estimate=pl.CostEstimate(
            flops=int(cost * MICROSECOND), bytes_accessed=1 << 20, transcendentals=0
        ),
    )(*(pltpu.with_memory_space_constraint(x, pltpu.HBM) for x in arrays[:raw]), *arrays[raw:])


def swap_halo(near, far, n):
    far_pairs = [(i, (i + 1) % n if i % 2 else (i - 1) % n) for i in range(n)]
    far = lax.ppermute(far, "patch", far_pairs)
    near = lax.ppermute(near, "patch", [(i, i ^ 1) for i in range(n)])
    return near, far


def exchange(pieces, plan):
    out = []
    for piece, goals in zip(pieces, plan):
        out.append(lax.ppermute(piece, "group", list(enumerate(goals))))
    return out


def on_device(
    grid_latent,
    mesh_latent,
    cotangent,
    halo_rows,
    encoder_sender,
    encoder_target,
    encoder_count,
    process_sender,
    process_target,
    process_count,
    encoder_source,
    encoder_dest,
    encoder_output,
    encoder_gain,
    process_source,
    process_dest,
    process_output,
    process_gain,
):
    patches, groups = lax.axis_size("patch"), lax.axis_size("group")
    grid_rows, width = grid_latent.shape
    mesh_rows = mesh_latent.shape[0]
    hidden_size = encoder_source.shape[1]
    coarse = mesh_rows // 16
    rim = halo_rows.shape[0] // 2
    slots, slots2 = encoder_sender.shape[0], process_sender.shape[0]

    row_form, row_form2 = ((1, slots), I32), ((1, slots2), I32)
    column_form2 = ((slots2, LANES), I16)
    remote = coarse * (groups - 1)
    near, far, grid = call(
        select_kernel,
        [halo_rows, grid_latent],
        [((rim, width), BF16)] * 2 + [((grid_rows, width), BF16)],
        4,
        raw=2,
        scratch=[pltpu.VMEM(halo_rows.shape, I32), pltpu.SemaphoreType.DMA((2,))],
    )
    near, far = swap_halo(near, far, patches)
    (
        early,
        near_source,
        part,
        hidden,
        summed16,
        live_send,
        live_goal,
        live_send2,
        live_goal2,
        send_col2,
        goal_col2,
        pick_rim,
        pick_goal,
    ) = call(
        functools.partial(encode_local_kernel, groups, coarse),
        [
            jnp.concatenate([encoder_count, process_count]),
            encoder_sender,
            encoder_target,
            process_sender,
            process_target,
            grid,
            mesh_latent,
            encoder_source,
            encoder_dest,
            near,
        ],
        [((2, LANES), I32), ((rim, hidden_size), BF16), ((slots, hidden_size), F32), ((slots, hidden_size), BF16)]
        + [((coarse, hidden_size), F32), row_form, row_form, row_form2, row_form2]
        + [column_form2, column_form2]
        + [((slots, 2 * rim), BF16), ((slots, mesh_rows), BF16)],
        2,
        scalars=1,
    )
    half, hidden, updated16 = call(
        functools.partial(encode_halo_kernel, coarse),
        [
            early,
            near_source,
            far,
            part,
            hidden,
            summed16,
            pick_rim,
            live_goal,
            mesh_latent,
            encoder_source,
            encoder_output,
            encoder_gain,
        ],
        [((slots, hidden_size), F32), ((slots, hidden_size), BF16), ((coarse, width), BF16)],
        2,
        aliases={3: 0, 4: 1},
    )
    shifts = exchange([updated16] * (groups - 1), plans(groups)[0])
    (
        normed,
        inverse,
        part2,
        pick_goal2,
        pick_coarse,
        sum_goal2,
        sum_coarse,
        centre2,
        summed2,
    ) = call(
        process_local_kernel,
        [
            hidden,
            live_goal,
            mesh_latent,
            send_col2,
            goal_col2,
            live_send2,
            live_goal2,
            cotangent,
            encoder_output,
            encoder_gain,
            process_gain,
            process_source,
            process_dest,
        ],
        [
            ((mesh_rows, width), F32),
            ((mesh_rows, LANES), F32),
            ((slots2, hidden_size), F32),
            ((slots2, mesh_rows), BF16),
            ((slots2, ceil_to(remote, LANES)), BF16),
            ((mesh_rows, slots2), BF16),
            ((remote, slots2), BF16),
            ((mesh_rows, width), F32),
            ((mesh_rows, hidden_size), F32),
        ],
        2,
        scratch=[pltpu.VMEM((slots2, hidden_size), BF16)],
    )
    half2, grad_first2, back2, *pieces = call(
        functools.partial(process_kernel, coarse),
        [
            early,
            part2,
            pick_goal2,
            pick_coarse,
            sum_goal2,
            sum_coarse,
            centre2,
            summed2,
            process_source,
            process_output,
            *shifts,
        ],
        [((slots2, hidden_size), F32), ((FIRST2, hidden_size), BF16)]
        + [((mesh_rows, hidden_size), BF16)]
        + [((coarse, hidden_size), BF16)] * (groups - 1),
        2,
        scratch=[
            pltpu.VMEM((slots2, hidden_size), BF16),
            pltpu.VMEM((slots2, hidden_size), BF16),
            pltpu.VMEM((slots2, hidden_size), BF16),
            pltpu.VMEM((mesh_rows, width), F32),
            pltpu.VMEM((mesh_rows, width), BF16),
        ],
        aliases={1: 0},
    )
    pieces = exchange(pieces, plans(groups)[1])
    grad_local, back, slope, sum_rim = call(
        functools.partial(process_back_kernel, grid_rows),
        [
            half,
            half2,
            grad_first2,
            back2,
            pick_goal2,
            live_send,
            live_send2,
            sum_goal2,
            cotangent,
            process_source,
            process_dest,
            encoder_output,
            encoder_gain,
            normed,
            inverse,
        ],
        [
            ((mesh_rows, width), F32),
            ((mesh_rows, hidden_size), BF16),
            ((FIRST, hidden_size), BF16),
            ((2 * rim, slots), BF16),
        ],
        2,
        scratch=[pltpu.VMEM((slots2, hidden_size), BF16)],
    )
    back, grad_first, near, far, grad16 = call(
        encode_back_kernel,
        [
            early,
            grad_local,
            back,
            normed,
            inverse,
            half,
            slope,
            pick_goal,
            sum_rim,
            encoder_gain,
            process_source,
            encoder_output,
            *pieces,
        ],
        [((mesh_rows, hidden_size), BF16), ((FIRST, hidden_size), BF16)]
        + [((rim, hidden_size), BF16)] * 2
        + [((coarse, width), F32)],
        2,
        scratch=[pltpu.VMEM((slots, hidden_size), BF16)],
    )
    near, far = swap_halo(near, far, patches)
    mesh_grad, own, sum_far = call(
        own_back_kernel,
        [
            grad_first,
            back,
            half,
            pick_goal,
            live_send,
            live_goal,
            grad_local,
            grad16,
            encoder_source,
            encoder_dest,
            halo_rows,
            near,
        ],
        [((mesh_rows, width), BF16), ((grid_rows, width), F32), ((grid_rows, rim), BF16)],
        2,
        scratch=[pltpu.VMEM((slots, hidden_size), BF16)],
    )
    (grid_grad,) = call(
        finish_kernel,
        [own, sum_far, far, encoder_source],
        [((grid_rows, width), BF16)],
        2,
        scratch=[pltpu.VMEM((grid_rows, width), BF16), pltpu.SemaphoreType.DMA((8,))],
        out_specs=[HBM],
    )
    return grid_grad, mesh_grad


def solution(mesh):
    rows, flat, whole = P(("patch", "group"), None), P(("patch", "group")), P()
    return jax.shard_map(
        on_device,
        mesh=mesh,
        in_specs=(rows,) * 3 + (flat,) * 7 + (whole,) * 8,
        out_specs=(rows, rows),
        check_vma=False,
    )
```
